32 devices in a mesh: coil: 16 (over z, x, core), sect: 2 (over y).
Axes of the slice: x: 2, y: 2, z: 4, core: 2. Of those that a mesh axis runs over, the one named last changes fastest.
Arguments:
- measured: float32 [256, 32, 4, 2, 192], P(None, 'coil', 'sect'), may hold values from -6 to 6
- coil_maps: float32 [256, 32, 4, 2, 192], P(None, 'coil', 'sect'), may hold values from -0.75 to 0.75
- sampling: int32 [4, 192], P('sect'), may hold values 0 or 1
- conv_first: bfloat16 [64, 54], replicated, may hold values from -0.875 to 0.875
- bias_first: float32 [64], replicated, may hold values from -3 to 3
- conv_second: bfloat16 [54, 64], replicated, may hold values from -0.15625 to 0.15625
- bias_second: float32 [2], replicated, may hold values from -1.5 to 1.5
Outputs:
- recon: float32 [256, 4, 2, 192], P('coil', 'sect')
The draws below stay inside these ranges and needn't reach their ends.
Inputs may be any that keep to these rules, and one draw needn't show every extreme that they name: sampling[s, l] is 1 where phase-encoding column l of slice s was measured, else 0.
All inputs are finite; a program needn't handle non-finite values. No bound on the sum of `sampling` on one device may be relied on, other than what follows from the above.
Results may differ from the reference program's by a relative error of at most 0.0029.
Values may be sent and summed in bfloat16 or wider, within the bound.
No kernel may reach another device: no remote copies, remote signals or barrier semaphores. Data moves between devices by JAX's collectives and lax.ppermute only.
A program may use at most 64 MiB of HBM per device.

```python
import jax
import jax.numpy as jnp
from jax import lax

H = 256
W = 192
C = 32
CH = 64
ITERS = 2
S = 4


def plant(entries, stream_key, smallest, top_value):
    place = [jax.random.randint(jax.random.fold_in(stream_key, axis), (), 0, length) for axis, length in enumerate(entries.shape)]
    longest = entries.shape.index(max(entries.shape))
    next_to = place[:longest] + [(place[longest] + 1) % entries.shape[longest]] + place[longest + 1:]
    return entries.at[tuple(place)].set(smallest).at[tuple(next_to)].set(top_value)


def level_of(key, shape, split, smallest, largest):
    level = 1.0
    for dim, blocks in split:
        heights = jax.random.uniform(jax.random.fold_in(jax.random.fold_in(key, 6), dim), (blocks,), jnp.float32, smallest / len(split), largest / len(split))
        level = level * jnp.repeat(jnp.exp(heights), shape[dim] // blocks).reshape((-1,) + (1,) * (len(shape) - 1 - dim))
    return level


def scatter_about(own_key, dims, width, reach, split=(), held_as=jnp.bfloat16):
    loudness = level_of(own_key, dims, split, -0.22, 0.18) if split else 1.0
    values = jax.random.normal(own_key, dims, jnp.float32) * width * loudness
    return jnp.minimum(jnp.maximum(values, -reach), reach).astype(held_as)


def setup_inputs(seed: int = 0) -> dict:
    key_list = jax.random.split(jax.random.key(seed), 8)
    measured = scatter_about(key_list[0], (H, C, S, 2, W), 1.0, 6.0, ((1, 16), (2, 2)), jnp.float32)
    coil_maps = scatter_about(key_list[1], (H, C, S, 2, W), 0.125, 0.75, ((1, 16), (2, 2)), jnp.float32)
    sampling = plant((jax.random.randint(key_list[2], (S, W), 0, 3) < 1).astype(jnp.int32), jax.random.fold_in(key_list[2], 1), 0, 1)
    conv_first = scatter_about(key_list[3], (CH, 54), 54 ** -0.5, 0.875)
    bias_first = scatter_about(key_list[4], (CH,), 0.5, 3.0, (), jnp.float32)
    conv_second = scatter_about(key_list[5], (54, CH), (27 * CH) ** -0.5, 0.15625)
    bias_second = scatter_about(key_list[6], (2,), 0.3, 1.5, (), jnp.float32)
    return dict(measured=measured, coil_maps=coil_maps, sampling=sampling, conv_first=conv_first, bias_first=bias_first, conv_second=conv_second, bias_second=bias_second)


step_size = 0.5


def stack_taps(padded, out_rows, out_slices, breadth):
    windows = []
    for first in range(3):
        for second in range(3):
            for third in range(3):
                windows.append(padded[first:first + out_rows, second:second + out_slices, :, third:third + breadth])
    return jnp.concatenate(windows, axis=2)


def tap_sum(taps, out_rows, out_slices, breadth):
    result = jnp.zeros((out_rows, out_slices, 2, breadth), jnp.float32)
    position = 0
    for first in range(3):
        for second in range(3):
            for third in range(3):
                result = result + taps[first:first + out_rows, second:second + out_slices, 2 * position:2 * position + 2, third:third + breadth]
                position = position + 1
    return result


def to_complex(array):
    return lax.complex(array[:, :, 0, :], array[:, :, 1, :]).transpose(1, 0, 2)


def pack_parts(real_part, imag_part):
    return jnp.stack([real_part, imag_part], axis=1).transpose(2, 0, 1, 3)


def reference(measured, coil_maps, sampling, conv_first, bias_first, conv_second, bias_second):
    weights = sampling.astype(jnp.float32)[:, None, :]

    def back_project(image_cplx, use_image):
        def one_coil(running, coil):
            maps = to_complex(lax.dynamic_index_in_dim(coil_maps, coil, 1, keepdims=False))
            data = to_complex(lax.dynamic_index_in_dim(measured, coil, 1, keepdims=False))
            if use_image:
                resid = weights * (jnp.fft.fft2(maps * image_cplx, norm="ortho") - data)
            else:
                resid = weights * data
            term = jnp.conj(maps) * jnp.fft.ifft2(resid, norm="ortho")
            return (running[0] + jnp.real(term), running[1] + jnp.imag(term)), None

        start = (jnp.zeros((S, H, W), jnp.float32), jnp.zeros((S, H, W), jnp.float32))
        final, unused = lax.scan(one_coil, start, jnp.arange(C, dtype=jnp.int32))
        return pack_parts(final[0], final[1])

    def regularize(damped):
        damped_half = damped.astype(jnp.bfloat16)
        padded = jnp.pad(damped_half, ((1, 1), (1, 1), (0, 0), (1, 1)))
        columns = stack_taps(padded, H, S, W).astype(jnp.float32)
        hidden = jnp.einsum("oc,rscw->rsow", conv_first.astype(jnp.float32), columns, precision=lax.Precision.HIGHEST)
        hidden = jax.nn.relu(hidden + bias_first[None, None, :, None]).astype(jnp.bfloat16)
        padded_hidden = jnp.pad(hidden, ((1, 1), (1, 1), (0, 0), (1, 1))).astype(jnp.float32)
        taps = jnp.einsum("tc,rscw->rstw", conv_second.astype(jnp.float32), padded_hidden, precision=lax.Precision.HIGHEST)
        update = tap_sum(taps, H, S, W) + bias_second[None, None, :, None]
        return damped + update

    image = back_project(None, False)
    for turn in range(ITERS):
        damped = image - step_size * back_project(to_complex(image), True)
        image = regularize(damped)
    return image
```

```python
import math

import jax
import jax.numpy as jnp
import numpy as np
from jax import lax
from jax.sharding import PartitionSpec as P

ITERS = 2
STEP = 0.5
F32 = jnp.float32
BF16 = jnp.bfloat16
HIGH = lax.Precision.HIGH


def dft_tables(length):
    index = np.arange(length)
    angle = (index[:, None] * index[None, :] % length) * (2.0 * math.pi / length)
    return np.cos(angle), np.sin(angle)


def with_halo(x, sides, width):
    for axis, dim in sides:
        count, length = lax.axis_size(axis), x.shape[dim]
        up = [(i, i + 1) for i in range(count - 1)]
        down = [(j, i) for i, j in up]
        before = lax.ppermute(lax.slice_in_dim(x, length - width, length, axis=dim), axis, up)
        after = lax.ppermute(lax.slice_in_dim(x, 0, width, axis=dim), axis, down)
        x = jnp.concatenate([before, x, after], axis=dim)
    return x


def stack_taps(padded, rows, slices, breadth):
    return jnp.concatenate(
        [
            padded[a : a + rows, b : b + slices, :, e : e + breadth]
            for a in range(3)
            for b in range(3)
            for e in range(3)
        ],
        axis=2,
    )


def tap_sum(taps, rows, slices, breadth):
    result = jnp.zeros((rows, slices, 2, breadth), F32)
    for place in range(27):
        a, b, e = place // 9, place // 3 % 3, place % 3
        result += taps[a : a + rows, b : b + slices, 2 * place : 2 * place + 2, e : e + breadth]
    return result


def regularize(damped, height, conv_first, bias_first, conv_second, bias_second):
    rows, slices, _, breadth = damped.shape
    extended = with_halo(damped.astype(BF16), (("coil", 0), ("sect", 1)), 2)
    padded = jnp.pad(extended, ((0, 0), (0, 0), (0, 0), (1, 1)))
    columns = stack_taps(padded, rows + 2, slices + 2, breadth)
    hidden = jnp.einsum("oc,rscw->rsow", conv_first, columns, preferred_element_type=F32)
    hidden = jax.nn.relu(hidden + bias_first[None, None, :, None]).astype(BF16)
    row_index = lax.axis_index("coil") * rows - 1 + jnp.arange(rows + 2)
    slice_index = lax.axis_index("sect") * slices - 1 + jnp.arange(slices + 2)
    row_valid = (row_index >= 0) & (row_index < height)
    slice_valid = (slice_index >= 0) & (slice_index < lax.axis_size("sect") * slices)
    inside = row_valid[:, None] & slice_valid[None, :]
    hidden = jnp.where(inside[:, :, None, None], hidden, jnp.zeros_like(hidden))
    hidden = jnp.pad(hidden, ((0, 0), (0, 0), (0, 0), (1, 1)))
    taps = jnp.einsum("tc,rscw->rstw", conv_second, hidden, preferred_element_type=F32)
    return tap_sum(taps, rows, slices, breadth) + bias_second[None, None, :, None]


def per_device(measured, coil_maps, sampling, conv_first, bias_first, conv_second, bias_second):
    height, coils_here, slices_here, _, breadth = coil_maps.shape
    count = lax.axis_size("coil")
    rows = height // count
    mask = sampling.astype(F32)

    def exchange(x):
        split = x.astype(BF16).reshape((count, rows) + x.shape[1:])
        return lax.all_to_all(split, "coil", 0, 0, tiled=True)

    row_cos, row_sin = dft_tables(height)
    col_cos, col_sin = dft_tables(breadth)
    row_table = jnp.asarray(np.stack([row_cos, row_sin]) / math.sqrt(height), F32)
    col_table = jnp.asarray(
        np.block([[col_cos, col_sin], [-col_sin, col_cos]]) / math.sqrt(breadth), F32
    ).reshape(2, breadth, 2, breadth)

    spread = jnp.einsum("tkh,kcsqw->tcsqwh", row_table, measured, precision=HIGH)
    spread = jnp.stack(
        [spread[0, :, :, 0] - spread[1, :, :, 1], spread[0, :, :, 1] + spread[1, :, :, 0]], axis=2
    )
    spread = spread * mask[None, :, None, :, None]
    inverse = jnp.einsum("qwpv,csqwh->csphv", col_table, spread, precision=HIGH)
    maps = jnp.transpose(coil_maps, (1, 2, 3, 0, 4))
    part_re = jnp.sum(maps[:, :, 0] * inverse[:, :, 0] + maps[:, :, 1] * inverse[:, :, 1], axis=0)
    part_im = jnp.sum(maps[:, :, 0] * inverse[:, :, 1] - maps[:, :, 1] * inverse[:, :, 0], axis=0)
    partial = jnp.transpose(jnp.stack([part_re, part_im], axis=1), (2, 0, 1, 3))
    first = jnp.sum(exchange(partial).astype(F32), axis=0)
    near = exchange(coil_maps).astype(F32)
    near_re, near_im = near[..., 0, :], near[..., 1, :]

    angle = jnp.asarray(np.stack([col_cos, col_sin]), F32)
    both = jnp.einsum("sl,alj,blv->absjv", mask, angle, angle, precision=HIGH) / breadth
    project_re = both[0, 0] + both[1, 1]
    project_im = both[0, 1] - both[1, 0]
    project = jnp.stack(
        [jnp.stack([project_re, project_im], 2), jnp.stack([-project_im, project_re], 2)]
    )

    image = first
    for _ in range(ITERS):
        image_re, image_im = image[:, :, 0], image[:, :, 1]
        product = jnp.stack(
            [near_re * image_re[:, None] - near_im * image_im[:, None],
             near_re * image_im[:, None] + near_im * image_re[:, None]]
        )
        spun = jnp.einsum("qnrcsj,qsjpv->pnrcsv", product, project, precision=HIGH)
        normal_re = jnp.sum(near_re * spun[0] + near_im * spun[1], axis=(0, 2))
        normal_im = jnp.sum(near_re * spun[1] - near_im * spun[0], axis=(0, 2))
        normal = jnp.stack([normal_re, normal_im], axis=2)
        damped = image - STEP * (normal - first)
        image = damped + regularize(
            damped, height, conv_first, bias_first, conv_second, bias_second
        )
    return image


def solution(mesh):
    coil_spec = P(None, "coil", "sect", None, None)
    in_specs = (coil_spec, coil_spec, P("sect", None), P(), P(), P(), P())
    return jax.shard_map(
        per_device,
        mesh=mesh,
        in_specs=in_specs,
        out_specs=P("coil", "sect", None, None),
        check_vma=False,
    )
```

```python
import functools
import math

import jax
import jax.numpy as jnp
import numpy as np
from jax import lax
from jax.experimental import pallas as pl
from jax.experimental.pallas import tpu as pltpu
from jax.sharding import PartitionSpec as P

ITERS = 2
STEP = 0.5
F32 = jnp.float32
BF16 = jnp.bfloat16
HIGH = lax.Precision.HIGH
LANES = 256


def dft_tables(length):
    index = np.arange(length)
    angle = (index[:, None] * index[None, :] % length) * (2.0 * math.pi / length)
    return np.cos(angle), np.sin(angle)


def with_halo(x, sides, width):
    for axis, dim in sides:
        count, length = lax.axis_size(axis), x.shape[dim]
        up = [(i, i + 1) for i in range(count - 1)]
        down = [(j, i) for i, j in up]
        before = lax.ppermute(lax.slice_in_dim(x, length - width, length, axis=dim), axis, up)
        after = lax.ppermute(lax.slice_in_dim(x, 0, width, axis=dim), axis, down)
        x = jnp.concatenate([before, x, after], axis=dim)
    return x


def stack_taps(padded, rows, slices, breadth):
    return jnp.concatenate(
        [
            padded[a : a + rows, b : b + slices, :, e : e + breadth]
            for a in range(3)
            for b in range(3)
            for e in range(3)
        ],
        axis=2,
    )


def tap_sum(taps, rows, slices, breadth):
    result = jnp.zeros((rows, slices, 2, breadth), F32)
    for place in range(27):
        a, b, e = place // 9, place // 3 % 3, place % 3
        result += taps[a : a + rows, b : b + slices, 2 * place : 2 * place + 2, e : e + breadth]
    return result


def regularize(damped, height, conv_first, bias_first, conv_second, bias_second):
    rows, slices, _, breadth = damped.shape
    extended = with_halo(damped.astype(BF16), (("coil", 0), ("sect", 1)), 2)
    padded = jnp.pad(extended, ((0, 0), (0, 0), (0, 0), (1, 1)))
    columns = stack_taps(padded, rows + 2, slices + 2, breadth)
    hidden = jnp.einsum("oc,rscw->rsow", conv_first, columns, preferred_element_type=F32)
    hidden = jax.nn.relu(hidden + bias_first[None, None, :, None]).astype(BF16)
    row_index = lax.axis_index("coil") * rows - 1 + jnp.arange(rows + 2)
    slice_index = lax.axis_index("sect") * slices - 1 + jnp.arange(slices + 2)
    row_valid = (row_index >= 0) & (row_index < height)
    slice_valid = (slice_index >= 0) & (slice_index < lax.axis_size("sect") * slices)
    inside = row_valid[:, None] & slice_valid[None, :]
    hidden = jnp.where(inside[:, :, None, None], hidden, jnp.zeros_like(hidden))
    hidden = jnp.pad(hidden, ((0, 0), (0, 0), (0, 0), (1, 1)))
    taps = jnp.einsum("tc,rscw->rstw", conv_second, hidden, preferred_element_type=F32)
    return tap_sum(taps, rows, slices, breadth) + bias_second[None, None, :, None]


def per_device(measured, coil_maps, sampling, conv_first, bias_first, conv_second, bias_second):
    height, coils_here, slices_here, _, breadth = coil_maps.shape
    count = lax.axis_size("coil")
    rows = height // count
    mask = sampling.astype(F32)

    def exchange(x):
        split = x.astype(BF16).reshape((count, rows) + x.shape[1:])
        return lax.all_to_all(split, "coil", 0, 0, tiled=True)

    row_cos, row_sin = dft_tables(height)
    col_cos, col_sin = dft_tables(breadth)
    row_table = jnp.asarray(np.stack([row_cos, row_sin]) / math.sqrt(height), F32)
    col_table = jnp.asarray(
        np.block([[col_cos, col_sin], [-col_sin, col_cos]]) / math.sqrt(breadth), F32
    ).reshape(2, breadth, 2, breadth)

    spread = jnp.einsum("tkh,kcsqw->tcsqwh", row_table, measured, precision=HIGH)
    spread = jnp.stack(
        [spread[0, :, :, 0] - spread[1, :, :, 1], spread[0, :, :, 1] + spread[1, :, :, 0]], axis=2
    )
    spread = spread * mask[None, :, None, :, None]
    inverse = jnp.einsum("qwpv,csqwh->csphv", col_table, spread, precision=HIGH)
    maps = jnp.transpose(coil_maps, (1, 2, 3, 0, 4))
    part_re = jnp.sum(maps[:, :, 0] * inverse[:, :, 0] + maps[:, :, 1] * inverse[:, :, 1], axis=0)
    part_im = jnp.sum(maps[:, :, 0] * inverse[:, :, 1] - maps[:, :, 1] * inverse[:, :, 0], axis=0)
    partial = jnp.transpose(jnp.stack([part_re, part_im], axis=1), (2, 0, 1, 3))
    first = jnp.sum(exchange(partial).astype(F32), axis=0)
    near = exchange(coil_maps).astype(F32)
    near_re, near_im = near[..., 0, :], near[..., 1, :]

    angle = jnp.asarray(np.stack([col_cos, col_sin]), F32)
    both = jnp.einsum("sl,alj,blv->absjv", mask, angle, angle, precision=HIGH) / breadth
    project_re = both[0, 0] + both[1, 1]
    project_im = both[0, 1] - both[1, 0]
    project = jnp.stack(
        [jnp.stack([project_re, project_im], 2), jnp.stack([-project_im, project_re], 2)]
    )

    image = first
    for _ in range(ITERS):
        image_re, image_im = image[:, :, 0], image[:, :, 1]
        product = jnp.stack(
            [near_re * image_re[:, None] - near_im * image_im[:, None],
             near_re * image_im[:, None] + near_im * image_re[:, None]]
        )
        spun = jnp.einsum("qnrcsj,qsjpv->pnrcsv", product, project, precision=HIGH)
        normal_re = jnp.sum(near_re * spun[0] + near_im * spun[1], axis=(0, 2))
        normal_im = jnp.sum(near_re * spun[1] - near_im * spun[0], axis=(0, 2))
        normal = jnp.stack([normal_re, normal_im], axis=2)
        damped = image - STEP * (normal - first)
        image = damped + regularize(
            damped, height, conv_first, bias_first, conv_second, bias_second
        )
    return image


def bf16_pair(table):
    high = table.astype(BF16)
    return high, (table - high.astype(np.float64)).astype(BF16)


def split3(x):
    high = x.astype(BF16)
    return high, (x - high.astype(F32)).astype(BF16)


def dot(x, y):
    return jnp.dot(x, y, preferred_element_type=F32)


def dot3(x, y):
    return dot(x[0], y[0]) + dot(x[1], y[0]) + dot(x[0], y[1])


def vmem(count):
    return [pl.BlockSpec(memory_space=pltpu.VMEM)] * count


def first_kernel(data_ref, maps_ref, mask_ref, row_hi, row_lo, col_hi, col_lo, send_ref, turn_ref):
    coils, _, double, height = data_ref.shape
    breadth = double // 2
    here = pl.program_id(0)
    data = data_ref[:, 0].reshape(coils * double, height)
    spread = dot3(split3(data), (row_hi[...], row_lo[...]))
    pieces = []
    for c in range(coils):
        real = spread[c * double : c * double + breadth]
        imag = spread[c * double + breadth : (c + 1) * double]
        pieces.append(real[:, :height] - imag[:, height:])
        pieces.append(imag[:, :height] + real[:, height:])
    columns = split3(jnp.concatenate(pieces, axis=1))
    mask = mask_ref[0].astype(F32)
    table = ((col_hi[...].astype(F32) * mask).astype(BF16), (col_lo[...].astype(F32) * mask).astype(BF16))
    mixed = dot3(table, columns)
    total_re, total_im = 0.0, 0.0
    for c in range(coils):
        base = 2 * c * height
        cos_re, sin_re = mixed[:breadth, base : base + height], mixed[breadth:, base : base + height]
        cos_im, sin_im = (
            mixed[:breadth, base + height : base + 2 * height],
            mixed[breadth:, base + height : base + 2 * height],
        )
        inv_re, inv_im = cos_re - sin_im, sin_re + cos_im
        map_re, map_im = maps_ref[c, 0, :breadth], maps_ref[c, 0, breadth:]
        total_re += map_re * inv_re + map_im * inv_im
        total_im += map_re * inv_im - map_im * inv_re
        turn_ref[c, 0, pl.ds(here * breadth, breadth), :] = map_re
        turn_ref[c, 1, pl.ds(here * breadth, breadth), :] = map_im
    turn_ref[coils, 0, pl.ds(here * breadth, breadth), :] = total_re
    turn_ref[coils, 1, pl.ds(here * breadth, breadth), :] = total_im

    @pl.when(here == pl.num_programs(0) - 1)
    def _():
        for k in range(coils + 1):
            parts = [turn_ref[k, q].T for q in range(2)]
            wide = parts[0].shape[1]
            both = jnp.concatenate([x.reshape(height // 8, 8, wide) for x in parts], axis=1)
            send_ref[:, 16 * k : 16 * k + 16, :] = both.astype(BF16)


def apply_data_term(near_ref, project_ref, image, start, left_ref, spun_ref, breadth):
    result = []
    coils, groups = near_ref.shape[0], near_ref.shape[1]
    wide = near_ref.shape[3]
    for t in range(groups):
        image_re, image_im = image[t][:8], image[t][8:]

        def spread(i, carry, t=t, image_re=image_re, image_im=image_im):
            reals, imags = [], []
            for c in range(2):
                maps = near_ref[i, t, 16 * c : 16 * c + 16, :].astype(F32)
                map_re, map_im = maps[:8], maps[8:]
                reals.append(map_re * image_re - map_im * image_im)
                imags.append(map_re * image_im + map_im * image_re)
            rows = pl.ds(pl.multiple_of(16 * i, 16), 16)
            left_ref[rows, :wide] = jnp.concatenate(reals, axis=0).astype(BF16)
            left_ref[rows, wide:] = jnp.concatenate(imags, axis=0).astype(BF16)
            return carry

        lax.fori_loop(0, coils, spread, 0, unroll=4)
        spun_ref[...] = dot(left_ref[...], project_ref[t])

        def gather(i, carry, t=t):
            sum_re, sum_im = carry
            for c in range(2):
                maps = near_ref[i, t, 16 * c : 16 * c + 16, :].astype(F32)
                map_re, map_im = maps[:8], maps[8:]
                rows = pl.ds(pl.multiple_of(16 * i + 8 * c, 8), 8)
                spun_re, spun_im = spun_ref[rows, :wide], spun_ref[rows, wide:]
                sum_re += map_re * spun_re + map_im * spun_im
                sum_im += map_re * spun_im - map_im * spun_re
            return sum_re, sum_im

        zero = jnp.zeros((8, wide), F32)
        normal = jnp.concatenate(lax.fori_loop(0, coils, gather, (zero, zero), unroll=4), axis=0)
        result.append((normal, t))
    return [image[t] - STEP * (normal * (1.0 / breadth) - start[t]) for normal, t in result]


def to_rows(damped, out_ref, flip_ref, breadth):
    per_group = damped[0].shape[1] // breadth
    wide = damped[0].shape[1]
    lanes = lax.broadcasted_iota(jnp.int32, (16, LANES), 1)
    for t, value in enumerate(damped):
        for s in range(per_group):
            moved = value if s == 0 else pltpu.roll(value, wide - s * breadth, 1)
            moved = jnp.where(lanes < breadth, moved[:, :LANES], 0.0)
            for q in range(2):
                place = (t * per_group + s) * 2 + q
                for j in range(2):
                    part = moved[8 * q : 8 * q + 8, 128 * j : 128 * j + 128]
                    flip_ref[pl.ds(64 * j + place, 8, stride=8), :] = part
    for j in range(2):
        out_ref[:, 128 * j : 128 * j + 128] = flip_ref[64 * j : 64 * j + 64]


def from_rows(flip_ref, groups, per_group, breadth):
    wide = per_group * breadth
    result = []
    for t in range(groups):
        parts = []
        for q in range(2):
            value = jnp.zeros((8, wide), F32)
            for s in range(per_group):
                place = (t * per_group + s) * 2 + q
                halves = [flip_ref[pl.ds(64 * j + place, 8, stride=8), :] for j in range(2)]
                piece = jnp.concatenate(halves + [jnp.zeros((8, wide - LANES), F32)], axis=1)
                value += piece if s == 0 else pltpu.roll(piece, s * breadth, 1)
            parts.append(value)
        result.append(jnp.concatenate(parts, axis=0))
    return result


def write_edges(rows_ref, low_ref, high_ref):
    low_ref[...] = rows_ref[:16].astype(BF16)
    high_ref[...] = rows_ref[48:64].astype(BF16)


def second_kernel(near_ref, project_ref, rows_ref, low_ref, high_ref, start_ref, flip_ref, left_ref, spun_ref, *, breadth):
    coils, groups, _, wide = near_ref.shape
    start = []
    for t in range(groups):
        def add(i, total, t=t):
            return total + near_ref[i, t, 32:48, :].astype(F32)

        start.append(lax.fori_loop(0, coils, add, jnp.zeros((16, wide), F32), unroll=4))
        start_ref[t] = start[t]
    damped = apply_data_term(near_ref, project_ref, start, start, left_ref, spun_ref, breadth)
    to_rows(damped, rows_ref, flip_ref, breadth)
    write_edges(rows_ref, low_ref, high_ref)


def convolve(rows_ref, before_ref, after_ref, first_ref, bias_first_ref, second_ref, bias_second_ref, shift_ref, breadth):
    position = lax.axis_index("coil") * lax.axis_size("sect") + lax.axis_index("sect")
    last = lax.axis_size("coil") * lax.axis_size("sect") - 1
    for h in range(12):
        if h < 2:
            value = before_ref[...].astype(F32)[8 * h : 8 * h + 8]
        elif h < 10:
            value = rows_ref[8 * (h - 2) : 8 * (h - 2) + 8]
        else:
            value = after_ref[...].astype(F32)[8 * (h - 10) : 8 * (h - 10) + 8]
        shift_ref[24 * h : 24 * h + 8] = pltpu.roll(value, 1, 1)
        shift_ref[24 * h + 8 : 24 * h + 16] = value
        shift_ref[24 * h + 16 : 24 * h + 24] = pltpu.roll(value, LANES - 1, 1)
    lanes = lax.broadcasted_iota(jnp.int32, (1, LANES), 1)
    taps = []
    for g in range(10):
        columns = shift_ref[24 * g : 24 * g + 72].astype(BF16)
        hidden = dot(first_ref[...], columns)
        hidden = jnp.maximum(hidden + bias_first_ref[...], 0.0).astype(BF16)
        inside = lanes < breadth
        if g == 0:
            inside = inside & (position > 0)
        if g == 9:
            inside = inside & (position < last)
        taps.append(jnp.where(inside, dot(second_ref[...], hidden), 0.0))
    bias = jnp.where(lanes < breadth, bias_second_ref[...], 0.0)
    image = []
    for h in range(8):
        total = taps[h][:24] + taps[h + 1][24:48] + taps[h + 2][48:]
        update = pltpu.roll(total[:8], 1, 1) + total[8:16] + pltpu.roll(total[16:], LANES - 1, 1)
        update = jnp.where(lanes < breadth, update, 0.0)
        image.append(rows_ref[8 * h : 8 * h + 8] + (update + bias))
    return image


def third_kernel(
    rows_ref, before_ref, after_ref, first_ref, bias_first_ref, second_ref, bias_second_ref,
    near_ref, project_ref, start_ref,
    out_ref, low_ref, high_ref, shift_ref, flip_ref, left_ref, spun_ref, *, breadth,
):
    groups, _, wide = start_ref.shape
    image = convolve(
        rows_ref, before_ref, after_ref, first_ref, bias_first_ref, second_ref, bias_second_ref, shift_ref, breadth
    )
    for h in range(8):
        for j in range(2):
            flip_ref[64 * j + 8 * h : 64 * j + 8 * h + 8] = image[h][:, 128 * j : 128 * j + 128]
    image = from_rows(flip_ref, groups, wide // breadth, breadth)
    start = [start_ref[t] for t in range(groups)]
    damped = apply_data_term(near_ref, project_ref, image, start, left_ref, spun_ref, breadth)
    to_rows(damped, out_ref, flip_ref, breadth)
    write_edges(out_ref, low_ref, high_ref)


def last_kernel(
    rows_ref, before_ref, after_ref, first_ref, bias_first_ref, second_ref, bias_second_ref,
    keep_ref, send_ref, shift_ref, *, breadth,
):
    image = convolve(
        rows_ref, before_ref, after_ref, first_ref, bias_first_ref, second_ref, bias_second_ref, shift_ref, breadth
    )
    upper = lax.axis_index("sect") == 0
    for h in range(8):
        low, high = image[h][:4, :breadth], image[h][4:, :breadth]
        keep_ref[h] = jnp.where(upper, low, high)
        send_ref[h] = jnp.where(upper, high, low)


def fast_device(measured, coil_maps, sampling, conv_first, bias_first, conv_second, bias_second):
    height, coils_here, slices_here, _, breadth = coil_maps.shape
    ranks, sects = lax.axis_size("coil"), lax.axis_size("sect")
    count = ranks * sects
    slices = slices_here * sects
    wide = slices_here * breadth
    features = conv_first.shape[0]
    both = ("coil", "sect")
    f32 = lambda *dims: jax.ShapeDtypeStruct(dims, F32)
    bf16 = lambda *dims: jax.ShapeDtypeStruct(dims, BF16)

    row_cos, row_sin = dft_tables(height)
    col_cos, col_sin = dft_tables(breadth)
    row_pair = bf16_pair(np.concatenate([row_cos, row_sin], axis=1) / math.sqrt(height))
    col_pair = bf16_pair(np.concatenate([col_cos, col_sin], axis=0) / math.sqrt(breadth))
    by_coil = lambda x: jnp.transpose(x, (1, 2, 3, 4, 0)).reshape(coils_here, slices_here, 2 * breadth, height)
    slab = pl.BlockSpec((coils_here, 1, 2 * breadth, height), lambda s: (0, s, 0, 0))
    whole = lambda dims: pl.BlockSpec(dims, lambda s: (0,) * len(dims))
    block_rows = 16 * (coils_here + 1)
    send = pl.pallas_call(
        first_kernel,
        grid=(slices_here,),
        in_specs=[
            slab, slab, pl.BlockSpec((1, 1, breadth), lambda s: (s, 0, 0)),
            whole((height, 2 * height)), whole((height, 2 * height)),
            whole((2 * breadth, breadth)), whole((2 * breadth, breadth)),
        ],
        out_specs=whole((count, block_rows, wide)),
        out_shape=bf16(count, block_rows, wide),
        scratch_shapes=[pltpu.VMEM((coils_here + 1, 2, wide, height), F32)],
    )(
        by_coil(measured), by_coil(coil_maps), sampling.reshape(slices_here, 1, breadth),
        *map(jnp.asarray, row_pair), *map(jnp.asarray, col_pair),
    )
    near = lax.all_to_all(send, both, 0, 0, tiled=True).reshape(ranks, sects, block_rows, wide)

    mask = sampling.astype(BF16)
    other = lax.ppermute(mask, "sect", [(0, 1), (1, 0)])
    pair = jnp.stack([mask, other])
    masks = jnp.where(lax.axis_index("sect") == 0, pair, pair[::-1]).astype(F32)
    angle = jnp.asarray(np.stack([col_cos, col_sin]), F32)
    mixed = jnp.einsum("tsl,alj,blv->abtsjv", masks, angle, angle, precision=HIGH)
    project_re = mixed[0, 0] + mixed[1, 1]
    project_im = mixed[0, 1] - mixed[1, 0]
    eye = jnp.asarray(np.eye(slices_here), F32)
    project = jnp.stack([jnp.stack([project_re, project_im], 3), jnp.stack([-project_im, project_re], 3)], 1)
    project = jnp.einsum("tasjbv,sz->tasjbzv", project, eye, precision=lax.Precision.HIGHEST)
    project = project.reshape(sects, 2 * wide, 2 * wide).astype(BF16)

    place = np.zeros((3, slices, slices))
    for s in range(slices):
        for b in range(3):
            if 0 <= s + b - 1 < slices:
                place[b, s, s + b - 1] = 1.0
    place = jnp.asarray(place, BF16)
    taps = conv_first.reshape(features, 3, 3, 3, 2)
    matrix_first = jnp.einsum("oabeq,bsz->soaezq", taps, place).reshape(slices * features, 18 * slices)
    taps = conv_second.reshape(3, 3, 3, 2, features)
    matrix_second = jnp.einsum("abepo,bsz->aespzo", taps, place).reshape(18 * slices, slices * features)
    wide_bias = jnp.broadcast_to(jnp.tile(bias_first, slices)[:, None], (slices * features, LANES))
    out_bias = jnp.broadcast_to(jnp.tile(bias_second, slices)[:, None], (2 * slices, LANES))
    weights = (matrix_first, wide_bias, matrix_second, out_bias)

    edge = 4 * slices
    up = [(i, i + 1) for i in range(count - 1)]
    down = [(j, i) for i, j in up]

    def swap_edges(low, high):
        return lax.ppermute(high, both, up), lax.ppermute(low, both, down)

    work = [pltpu.VMEM((32 * slices, 128), F32)]
    work += [pltpu.VMEM((16 * ranks, 2 * wide), BF16), pltpu.VMEM((16 * ranks, 2 * wide), F32)]
    shift = pltpu.VMEM((12 * 6 * slices, LANES), F32)
    row_shapes = [f32(16 * slices, LANES), bf16(edge, LANES), bf16(edge, LANES)]
    rows, low, high, start = pl.pallas_call(
        functools.partial(second_kernel, breadth=breadth),
        in_specs=vmem(2), out_specs=vmem(4),
        out_shape=row_shapes + [f32(sects, 16, wide)], scratch_shapes=work,
    )(near, project)
    for _ in range(ITERS - 1):
        before, after = swap_edges(low, high)
        rows, low, high = pl.pallas_call(
            functools.partial(third_kernel, breadth=breadth),
            in_specs=vmem(10), out_specs=vmem(3), out_shape=row_shapes,
            scratch_shapes=[shift] + work,
        )(rows, before, after, *weights, near, project, start)
    before, after = swap_edges(low, high)
    piece = f32(8, 2 * slices_here, breadth)
    keep, give = pl.pallas_call(
        functools.partial(last_kernel, breadth=breadth),
        in_specs=vmem(7), out_specs=vmem(2), out_shape=[piece, piece], scratch_shapes=[shift],
    )(rows, before, after, *weights)
    got = lax.ppermute(give, "sect", [(0, 1), (1, 0)])
    upper = lax.axis_index("sect") == 0
    out = jnp.concatenate([jnp.where(upper, keep, got), jnp.where(upper, got, keep)], axis=0)
    return out.reshape(16, slices_here, 2, breadth)


def per_device_any(measured, coil_maps, *rest):
    height, coils_here, slices_here, _, breadth = coil_maps.shape
    ranks, sects = lax.axis_size("coil"), lax.axis_size("sect")
    fits = (
        sects == 2 and slices_here == 2 and coils_here == 2 and height == 8 * ranks * sects
        and 2 * breadth % 128 == 0 and 128 < breadth < LANES and breadth % 16 == 0
    )
    return (fast_device if fits else per_device)(measured, coil_maps, *rest)


def solution(mesh):
    coil_spec = P(None, "coil", "sect", None, None)
    in_specs = (coil_spec, coil_spec, P("sect", None), P(), P(), P(), P())
    return jax.shard_map(
        per_device_any,
        mesh=mesh,
        in_specs=in_specs,
        out_specs=P("coil", "sect", None, None),
        check_vma=False,
    )
```

```python
import functools
import math

import jax
import jax.numpy as jnp
import numpy as np
from jax import lax
from jax.experimental import pallas as pl
from jax.experimental.pallas import tpu as pltpu
from jax.sharding import PartitionSpec as P

ITERS = 2
STEP = 0.5
F32 = jnp.float32
BF16 = jnp.bfloat16
HIGH = lax.Precision.HIGH
LANES = 256


def dft_tables(length):
    index = np.arange(length)
    angle = (index[:, None] * index[None, :] % length) * (2.0 * math.pi / length)
    return np.cos(angle), np.sin(angle)


def with_halo(x, sides, width):
    for axis, dim in sides:
        count, length = lax.axis_size(axis), x.shape[dim]
        up = [(i, i + 1) for i in range(count - 1)]
        down = [(j, i) for i, j in up]
        before = lax.ppermute(lax.slice_in_dim(x, length - width, length, axis=dim), axis, up)
        after = lax.ppermute(lax.slice_in_dim(x, 0, width, axis=dim), axis, down)
        x = jnp.concatenate([before, x, after], axis=dim)
    return x


def stack_taps(padded, rows, slices, breadth):
    return jnp.concatenate(
        [
            padded[a : a + rows, b : b + slices, :, e : e + breadth]
            for a in range(3)
            for b in range(3)
            for e in range(3)
        ],
        axis=2,
    )


def tap_sum(taps, rows, slices, breadth):
    result = jnp.zeros((rows, slices, 2, breadth), F32)
    for place in range(27):
        a, b, e = place // 9, place // 3 % 3, place % 3
        result += taps[a : a + rows, b : b + slices, 2 * place : 2 * place + 2, e : e + breadth]
    return result


def regularize(damped, height, conv_first, bias_first, conv_second, bias_second):
    rows, slices, _, breadth = damped.shape
    extended = with_halo(damped.astype(BF16), (("coil", 0), ("sect", 1)), 2)
    padded = jnp.pad(extended, ((0, 0), (0, 0), (0, 0), (1, 1)))
    columns = stack_taps(padded, rows + 2, slices + 2, breadth)
    hidden = jnp.einsum("oc,rscw->rsow", conv_first, columns, preferred_element_type=F32)
    hidden = jax.nn.relu(hidden + bias_first[None, None, :, None]).astype(BF16)
    row_index = lax.axis_index("coil") * rows - 1 + jnp.arange(rows + 2)
    slice_index = lax.axis_index("sect") * slices - 1 + jnp.arange(slices + 2)
    row_valid = (row_index >= 0) & (row_index < height)
    slice_valid = (slice_index >= 0) & (slice_index < lax.axis_size("sect") * slices)
    inside = row_valid[:, None] & slice_valid[None, :]
    hidden = jnp.where(inside[:, :, None, None], hidden, jnp.zeros_like(hidden))
    hidden = jnp.pad(hidden, ((0, 0), (0, 0), (0, 0), (1, 1)))
    taps = jnp.einsum("tc,rscw->rstw", conv_second, hidden, preferred_element_type=F32)
    return tap_sum(taps, rows, slices, breadth) + bias_second[None, None, :, None]


def per_device(measured, coil_maps, sampling, conv_first, bias_first, conv_second, bias_second):
    height, coils_here, slices_here, _, breadth = coil_maps.shape
    count = lax.axis_size("coil")
    rows = height // count
    mask = sampling.astype(F32)

    def exchange(x):
        split = x.astype(BF16).reshape((count, rows) + x.shape[1:])
        return lax.all_to_all(split, "coil", 0, 0, tiled=True)

    row_cos, row_sin = dft_tables(height)
    col_cos, col_sin = dft_tables(breadth)
    row_table = jnp.asarray(np.stack([row_cos, row_sin]) / math.sqrt(height), F32)
    col_table = jnp.asarray(
        np.block([[col_cos, col_sin], [-col_sin, col_cos]]) / math.sqrt(breadth), F32
    ).reshape(2, breadth, 2, breadth)

    spread = jnp.einsum("tkh,kcsqw->tcsqwh", row_table, measured, precision=HIGH)
    spread = jnp.stack(
        [spread[0, :, :, 0] - spread[1, :, :, 1], spread[0, :, :, 1] + spread[1, :, :, 0]], axis=2
    )
    spread = spread * mask[None, :, None, :, None]
    inverse = jnp.einsum("qwpv,csqwh->csphv", col_table, spread, precision=HIGH)
    maps = jnp.transpose(coil_maps, (1, 2, 3, 0, 4))
    part_re = jnp.sum(maps[:, :, 0] * inverse[:, :, 0] + maps[:, :, 1] * inverse[:, :, 1], axis=0)
    part_im = jnp.sum(maps[:, :, 0] * inverse[:, :, 1] - maps[:, :, 1] * inverse[:, :, 0], axis=0)
    partial = jnp.transpose(jnp.stack([part_re, part_im], axis=1), (2, 0, 1, 3))
    first = jnp.sum(exchange(partial).astype(F32), axis=0)
    near = exchange(coil_maps).astype(F32)
    near_re, near_im = near[..., 0, :], near[..., 1, :]

    angle = jnp.asarray(np.stack([col_cos, col_sin]), F32)
    both = jnp.einsum("sl,alj,blv->absjv", mask, angle, angle, precision=HIGH) / breadth
    project_re = both[0, 0] + both[1, 1]
    project_im = both[0, 1] - both[1, 0]
    project = jnp.stack(
        [jnp.stack([project_re, project_im], 2), jnp.stack([-project_im, project_re], 2)]
    )

    image = first
    for _ in range(ITERS):
        image_re, image_im = image[:, :, 0], image[:, :, 1]
        product = jnp.stack(
            [near_re * image_re[:, None] - near_im * image_im[:, None],
             near_re * image_im[:, None] + near_im * image_re[:, None]]
        )
        spun = jnp.einsum("qnrcsj,qsjpv->pnrcsv", product, project, precision=HIGH)
        normal_re = jnp.sum(near_re * spun[0] + near_im * spun[1], axis=(0, 2))
        normal_im = jnp.sum(near_re * spun[1] - near_im * spun[0], axis=(0, 2))
        normal = jnp.stack([normal_re, normal_im], axis=2)
        damped = image - STEP * (normal - first)
        image = damped + regularize(
            damped, height, conv_first, bias_first, conv_second, bias_second
        )
    return image


def bf16_pair(table):
    high = table.astype(BF16)
    return high, (table - high.astype(np.float64)).astype(BF16)


def split3(x):
    high = x.astype(BF16)
    return high, (x - high.astype(F32)).astype(BF16)


def dot(x, y):
    return jnp.dot(x, y, preferred_element_type=F32)


def dot3(x, y):
    return dot(x[0], y[0]) + dot(x[1], y[0]) + dot(x[0], y[1])


def vmem(count):
    return [pl.BlockSpec(memory_space=pltpu.VMEM)] * count


def column_of(row):
    shape = (row.shape[1], row.shape[1])
    diagonal = lax.broadcasted_iota(jnp.int32, shape, 0) == lax.broadcasted_iota(jnp.int32, shape, 1)
    return jnp.sum(jnp.where(diagonal, jnp.broadcast_to(row, shape), 0.0), axis=1, keepdims=True)


def first_kernel(data_ref, maps_ref, mask_ref, row_ref, column_ref, send_ref, mask_out_ref, total_ref):
    _, slices, double, height = data_ref.shape
    breadth, wide = double // 2, slices * double // 2
    here, last = pl.program_id(0), pl.num_programs(0) - 1

    def emit(slot, parts):
        turned = [x.T.reshape(height // 8, 8, wide) for x in parts]
        rows = pl.ds(pl.multiple_of(16 * slot, 16), 16)
        send_ref[:, rows, :] = jnp.concatenate(turned, axis=1).astype(BF16)

    maps = [[maps_ref[0, s, q * breadth : (q + 1) * breadth] for s in range(slices)] for q in range(2)]
    emit(here, [jnp.concatenate(x, axis=0) for x in maps])
    mask = mask_ref[...].astype(F32)
    mask_out_ref[...] = mask.astype(BF16)

    high, low = split3(data_ref[0].reshape(slices * double, height))
    spread = dot(jnp.concatenate([high, low, high], axis=1), row_ref[...])
    pieces = []
    for s in range(slices):
        keep = column_of(mask[s : s + 1])
        real = spread[s * double : s * double + breadth]
        imag = spread[s * double + breadth : (s + 1) * double]
        pieces.append((real[:, :height] - imag[:, height:]) * keep)
        pieces.append((imag[:, :height] + real[:, height:]) * keep)
    high, low = split3(jnp.concatenate(pieces, axis=1))
    mixed = dot(column_ref[...], jnp.concatenate([high, low, high], axis=0))
    for s in range(slices):
        cos_re, cos_im = [mixed[:breadth, (2 * s + q) * height : (2 * s + q + 1) * height] for q in range(2)]
        sin_re, sin_im = [mixed[breadth:, (2 * s + q) * height : (2 * s + q + 1) * height] for q in range(2)]
        inv_re, inv_im = cos_re - sin_im, sin_re + cos_im
        map_re, map_im = maps[0][s], maps[1][s]
        sums = (map_re * inv_re + map_im * inv_im, map_re * inv_im - map_im * inv_re)
        for q in range(2):
            rows = slice(s * breadth, (s + 1) * breadth)
            total_ref[q, rows] = sums[q] + jnp.where(here == 0, 0.0, total_ref[q, rows])

    @pl.when(here == last)
    def _():
        emit(last + 1, [total_ref[q] for q in range(2)])


def table_kernel(
    own_ref, other_ref, angle_ref, first_ref, bias_ref, second_ref, pick_first_ref, pick_second_ref, place_ref,
    project_ref, first_out_ref, second_out_ref,
):
    slices, breadth = own_ref.shape
    wide = slices * breadth
    here = lax.axis_index("sect")
    angle = angle_ref[...]
    swapped = jnp.concatenate([angle[:, wide:], -angle[:, :wide]], axis=1)
    cosine, sine = angle[:, :breadth], angle[:, wide : wide + breadth]
    angle, swapped = split3(angle), split3(swapped)
    for t in range(project_ref.shape[0]):
        mask = jnp.where(here == t, own_ref[...].astype(F32), other_ref[...].astype(F32))
        for s in range(slices):
            row = mask[s : s + 1]
            block = dot3(split3(cosine * row), angle) + dot3(split3(sine * row), swapped)
            if s:
                block = pltpu.roll(block, s * breadth, 1)
            rows = slice(s * breadth, (s + 1) * breadth)
            project_ref[t, rows] = block.astype(BF16)
            rows = slice(wide + s * breadth, wide + (s + 1) * breadth)
            project_ref[t, rows] = jnp.concatenate([-block[:, wide:], block[:, :wide]], axis=1).astype(BF16)

    groups, _, depth = pick_first_ref.shape
    features = first_ref.shape[1]
    bias = column_of(bias_ref[...])
    parts = []
    for _ in range(3):
        parts.append(bias.astype(BF16).astype(F32))
        bias = bias - parts[-1]
    lane = lax.broadcasted_iota(jnp.int32, (features, depth), 1)
    second = 0.0
    for s in range(groups):
        block = lax.dot_general(
            first_ref[...], pick_first_ref[s], (((0,), (0,)), ((), ())), preferred_element_type=F32
        )
        for i in range(3):
            block = jnp.where(lane == depth - 8 + i, parts[i], block)
        first_out_ref[s * features : (s + 1) * features] = block.astype(BF16)
        second += dot(dot(pick_second_ref[s], second_ref[...]).astype(BF16), place_ref[s])
    second_out_ref[...] = second.astype(BF16)


def apply_data_term(near_ref, project_ref, image, start, left_ref, spun_ref, breadth):
    result = []
    coils, groups = near_ref.shape[0], near_ref.shape[1]
    wide = near_ref.shape[3]
    for t in range(groups):
        image_re, image_im = image[t][:8], image[t][8:]

        def spread(i, carry, t=t, image_re=image_re, image_im=image_im):
            reals, imags = [], []
            for c in range(2):
                maps = near_ref[i, t, 16 * c : 16 * c + 16, :].astype(F32)
                map_re, map_im = maps[:8], maps[8:]
                reals.append(map_re * image_re - map_im * image_im)
                imags.append(map_re * image_im + map_im * image_re)
            rows = pl.ds(pl.multiple_of(16 * i, 16), 16)
            left_ref[rows, :wide] = jnp.concatenate(reals, axis=0).astype(BF16)
            left_ref[rows, wide:] = jnp.concatenate(imags, axis=0).astype(BF16)
            return carry

        lax.fori_loop(0, coils, spread, 0, unroll=4)
        spun_ref[...] = dot(left_ref[...], project_ref[t])

        def gather(i, carry, t=t):
            sum_re, sum_im = carry
            for c in range(2):
                maps = near_ref[i, t, 16 * c : 16 * c + 16, :].astype(F32)
                map_re, map_im = maps[:8], maps[8:]
                rows = pl.ds(pl.multiple_of(16 * i + 8 * c, 8), 8)
                spun_re, spun_im = spun_ref[rows, :wide], spun_ref[rows, wide:]
                sum_re += map_re * spun_re + map_im * spun_im
                sum_im += map_re * spun_im - map_im * spun_re
            return sum_re, sum_im

        zero = jnp.zeros((8, wide), F32)
        normal = jnp.concatenate(lax.fori_loop(0, coils, gather, (zero, zero), unroll=4), axis=0)
        result.append((normal, t))
    return [image[t] - STEP * (normal * (1.0 / breadth) - start[t]) for normal, t in result]


def to_rows(damped, out_ref, flip_ref, breadth):
    per_group = damped[0].shape[1] // breadth
    wide = damped[0].shape[1]
    lanes = lax.broadcasted_iota(jnp.int32, (16, LANES), 1)
    for t, value in enumerate(damped):
        for s in range(per_group):
            moved = value if s == 0 else pltpu.roll(value, wide - s * breadth, 1)
            moved = jnp.where(lanes < breadth, moved[:, :LANES], 0.0)
            for q in range(2):
                place = (t * per_group + s) * 2 + q
                for j in range(2):
                    part = moved[8 * q : 8 * q + 8, 128 * j : 128 * j + 128]
                    flip_ref[pl.ds(64 * j + place, 8, stride=8), :] = part
    for j in range(2):
        out_ref[:, 128 * j : 128 * j + 128] = flip_ref[64 * j : 64 * j + 64]


def from_rows(flip_ref, groups, per_group, breadth):
    wide = per_group * breadth
    result = []
    for t in range(groups):
        parts = []
        for q in range(2):
            value = jnp.zeros((8, wide), F32)
            for s in range(per_group):
                place = (t * per_group + s) * 2 + q
                halves = [flip_ref[pl.ds(64 * j + place, 8, stride=8), :] for j in range(2)]
                piece = jnp.concatenate(halves + [jnp.zeros((8, wide - LANES), F32)], axis=1)
                value += piece if s == 0 else pltpu.roll(piece, s * breadth, 1)
            parts.append(value)
        result.append(jnp.concatenate(parts, axis=0))
    return result


def write_edges(rows_ref, low_ref, high_ref):
    low_ref[...] = rows_ref[:16].astype(BF16)
    high_ref[...] = rows_ref[48:64].astype(BF16)


def second_kernel(near_ref, project_ref, rows_ref, low_ref, high_ref, start_ref, flip_ref, left_ref, spun_ref, *, breadth):
    coils, groups, _, wide = near_ref.shape
    start = []
    for t in range(groups):
        def add(i, total, t=t):
            return total + near_ref[i, t, 32:48, :].astype(F32)

        start.append(lax.fori_loop(0, coils, add, jnp.zeros((16, wide), F32), unroll=4))
        start_ref[t] = start[t]
    damped = apply_data_term(near_ref, project_ref, start, start, left_ref, spun_ref, breadth)
    to_rows(damped, rows_ref, flip_ref, breadth)
    write_edges(rows_ref, low_ref, high_ref)


def convolve(rows_ref, before_ref, after_ref, first_ref, second_ref, bias_ref, shift_ref, hidden_ref, breadth):
    position = lax.axis_index("coil") * lax.axis_size("sect") + lax.axis_index("sect")
    last = lax.axis_size("coil") * lax.axis_size("sect") - 1
    before, after = before_ref[...].astype(F32), after_ref[...].astype(F32)
    for h in range(12):
        if h < 2:
            value = before[8 * h : 8 * h + 8]
        elif h < 10:
            value = rows_ref[8 * (h - 2) : 8 * (h - 2) + 8]
        else:
            value = after[8 * (h - 10) : 8 * (h - 10) + 8]
        shift_ref[24 * h : 24 * h + 8] = pltpu.roll(value, 1, 1)
        shift_ref[24 * h + 8 : 24 * h + 16] = value
        shift_ref[24 * h + 16 : 24 * h + 24] = pltpu.roll(value, LANES - 1, 1)
    ones = jnp.ones((8, LANES), F32)
    for g in range(10):
        columns = jnp.concatenate([shift_ref[24 * g : 24 * g + 72], ones], axis=0).astype(BF16)
        hidden = dot(first_ref[...], columns).astype(BF16)
        hidden_ref[g] = jnp.maximum(hidden, jnp.zeros_like(hidden))
    lanes = lax.broadcasted_iota(jnp.int32, (1, LANES), 1)
    taps = []
    for g in range(10):
        inside = lanes < breadth
        if g == 0:
            inside = inside & (position > 0)
        if g == 9:
            inside = inside & (position < last)
        taps.append(jnp.where(inside, dot(second_ref[...], hidden_ref[g]), 0.0))
    odd = lax.broadcasted_iota(jnp.int32, (8, LANES), 0) % 2 == 1
    bias = jnp.where(odd, bias_ref[1], bias_ref[0])
    image = []
    for h in range(8):
        total = taps[h][:24] + taps[h + 1][24:48] + taps[h + 2][48:]
        update = pltpu.roll(total[:8], 1, 1) + total[8:16] + pltpu.roll(total[16:], LANES - 1, 1)
        update = jnp.where(lanes < breadth, update + bias, 0.0)
        image.append(rows_ref[8 * h : 8 * h + 8] + update)
    return image


def third_kernel(
    rows_ref, before_ref, after_ref, first_ref, second_ref, bias_ref,
    near_ref, project_ref, start_ref,
    out_ref, low_ref, high_ref, shift_ref, hidden_ref, flip_ref, left_ref, spun_ref, *, breadth,
):
    groups, _, wide = start_ref.shape
    image = convolve(
        rows_ref, before_ref, after_ref, first_ref, second_ref, bias_ref, shift_ref, hidden_ref, breadth
    )
    for h in range(8):
        for j in range(2):
            flip_ref[64 * j + 8 * h : 64 * j + 8 * h + 8] = image[h][:, 128 * j : 128 * j + 128]
    image = from_rows(flip_ref, groups, wide // breadth, breadth)
    start = [start_ref[t] for t in range(groups)]
    damped = apply_data_term(near_ref, project_ref, image, start, left_ref, spun_ref, breadth)
    to_rows(damped, out_ref, flip_ref, breadth)
    write_edges(out_ref, low_ref, high_ref)


def last_kernel(
    rows_ref, before_ref, after_ref, first_ref, second_ref, bias_ref,
    keep_ref, send_ref, shift_ref, hidden_ref, *, breadth,
):
    image = convolve(
        rows_ref, before_ref, after_ref, first_ref, second_ref, bias_ref, shift_ref, hidden_ref, breadth
    )
    upper = lax.axis_index("sect") == 0
    for h in range(8):
        low, high = image[h][:4, :breadth], image[h][4:, :breadth]
        keep_ref[h] = jnp.where(upper, low, high)
        send_ref[h] = jnp.where(upper, high, low)


def fast_device(measured, coil_maps, sampling, conv_first, bias_first, conv_second, bias_second):
    height, coils_here, slices_here, _, breadth = coil_maps.shape
    ranks, sects = lax.axis_size("coil"), lax.axis_size("sect")
    count = ranks * sects
    slices = slices_here * sects
    wide = slices_here * breadth
    features = conv_first.shape[0]
    both = ("coil", "sect")
    f32 = lambda *dims: jax.ShapeDtypeStruct(dims, F32)
    bf16 = lambda *dims: jax.ShapeDtypeStruct(dims, BF16)

    row_cos, row_sin = dft_tables(height)
    col_cos, col_sin = dft_tables(breadth)
    row_high, row_low = bf16_pair(np.concatenate([row_cos, row_sin], axis=1) / math.sqrt(height))
    column_high, column_low = bf16_pair(np.concatenate([col_cos, col_sin], axis=0) / math.sqrt(breadth))
    row_table = jnp.asarray(np.concatenate([row_high, row_high, row_low], axis=0))
    column_table = jnp.asarray(np.concatenate([column_high, column_high, column_low], axis=1))
    by_coil = lambda x: jnp.transpose(x, (1, 2, 3, 4, 0)).reshape(coils_here, slices_here, 2 * breadth, height)
    slab = pl.BlockSpec((1, slices_here, 2 * breadth, height), lambda c: (c, 0, 0, 0))
    whole = lambda *dims: pl.BlockSpec(dims, lambda c: (0,) * len(dims))
    block_rows = 16 * (coils_here + 1)
    send, mask = pl.pallas_call(
        first_kernel,
        grid=(coils_here,),
        in_specs=[
            slab, slab, whole(slices_here, breadth), whole(*row_table.shape), whole(*column_table.shape),
        ],
        out_specs=[whole(count, block_rows, wide), whole(slices_here, breadth)],
        out_shape=[bf16(count, block_rows, wide), bf16(slices_here, breadth)],
        scratch_shapes=[pltpu.VMEM((2, wide, height), F32)],
    )(by_coil(measured), by_coil(coil_maps), sampling, row_table, column_table)
    near = lax.all_to_all(send, both, 0, 0, tiled=True).reshape(ranks, sects, block_rows, wide)

    other = lax.ppermute(mask, "sect", [(0, 1), (1, 0)])
    blank = np.zeros((breadth, wide - breadth))
    angle = np.concatenate([col_cos, blank, col_sin, blank], axis=1).astype(np.float32)
    span = 18 * slices
    pick_first = np.zeros((slices, 54, span + 8))
    pick_second = np.zeros((slices, span, 54))
    for a, b, e, q, s in np.ndindex(3, 3, 3, 2, slices):
        tap = 2 * (9 * a + 3 * b + e) + q
        if 0 <= s + b - 1 < slices:
            pick_first[s, tap, ((a * 3 + e) * slices + s + b - 1) * 2 + q] = 1.0
            pick_second[s + b - 1, ((a * 3 + e) * slices + s) * 2 + q, tap] = 1.0
    place = np.eye(slices * features).reshape(slices, features, slices * features)
    project, matrix_first, matrix_second = pl.pallas_call(
        table_kernel,
        in_specs=vmem(9), out_specs=vmem(3),
        out_shape=[
            bf16(sects, 2 * wide, 2 * wide), bf16(slices * features, span + 8), bf16(span, slices * features),
        ],
    )(
        mask, other, jnp.asarray(angle), conv_first.T, bias_first.reshape(1, features), conv_second,
        *[jnp.asarray(x.astype(BF16)) for x in (pick_first, pick_second, place)],
    )
    weights = (matrix_first, matrix_second, bias_second)
    weight_specs = vmem(2) + [pl.BlockSpec(memory_space=pltpu.SMEM)]

    edge = 4 * slices
    up = [(i, i + 1) for i in range(count - 1)]
    down = [(j, i) for i, j in up]

    def swap_edges(low, high):
        return lax.ppermute(high, both, up), lax.ppermute(low, both, down)

    work = [pltpu.VMEM((32 * slices, 128), F32)]
    work += [pltpu.VMEM((16 * ranks, 2 * wide), BF16), pltpu.VMEM((16 * ranks, 2 * wide), F32)]
    shift = [pltpu.VMEM((12 * 6 * slices, LANES), F32), pltpu.VMEM((10, slices * features, LANES), BF16)]
    row_shapes = [f32(16 * slices, LANES), bf16(edge, LANES), bf16(edge, LANES)]
    rows, low, high, start = pl.pallas_call(
        functools.partial(second_kernel, breadth=breadth),
        in_specs=vmem(2), out_specs=vmem(4),
        out_shape=row_shapes + [f32(sects, 16, wide)], scratch_shapes=work,
    )(near, project)
    for _ in range(ITERS - 1):
        before, after = swap_edges(low, high)
        rows, low, high = pl.pallas_call(
            functools.partial(third_kernel, breadth=breadth),
            in_specs=vmem(3) + weight_specs + vmem(3), out_specs=vmem(3), out_shape=row_shapes,
            scratch_shapes=shift + work,
        )(rows, before, after, *weights, near, project, start)
    before, after = swap_edges(low, high)
    piece = f32(8, 2 * slices_here, breadth)
    keep, give = pl.pallas_call(
        functools.partial(last_kernel, breadth=breadth),
        in_specs=vmem(3) + weight_specs, out_specs=vmem(2), out_shape=[piece, piece], scratch_shapes=shift,
    )(rows, before, after, *weights)
    got = lax.ppermute(give, "sect", [(0, 1), (1, 0)])
    upper = lax.axis_index("sect") == 0
    out = jnp.concatenate([jnp.where(upper, keep, got), jnp.where(upper, got, keep)], axis=0)
    return out.reshape(16, slices_here, 2, breadth)


def per_device_any(measured, coil_maps, *rest):
    height, coils_here, slices_here, _, breadth = coil_maps.shape
    ranks, sects = lax.axis_size("coil"), lax.axis_size("sect")
    fits = (
        sects == 2 and slices_here == 2 and coils_here == 2 and height == 8 * ranks * sects
        and 2 * breadth % 128 == 0 and 128 < breadth < LANES and breadth % 16 == 0
    )
    return (fast_device if fits else per_device)(measured, coil_maps, *rest)


def solution(mesh):
    coil_spec = P(None, "coil", "sect", None, None)
    in_specs = (coil_spec, coil_spec, P("sect", None), P(), P(), P(), P())
    return jax.shard_map(
        per_device_any,
        mesh=mesh,
        in_specs=in_specs,
        out_specs=P("coil", "sect", None, None),
        check_vma=False,
    )
```

```python
import functools
import math

import jax
import jax.numpy as jnp
import numpy as np
from jax import lax
from jax.experimental import pallas as pl
from jax.experimental.pallas import tpu as pltpu
from jax.sharding import PartitionSpec as P

ITERS = 2
STEP = 0.5
F32 = jnp.float32
BF16 = jnp.bfloat16
HIGH = lax.Precision.HIGH
LANES = 256
MODEST = pltpu.CompilerParams(vmem_limit_bytes=24 << 20)


def dft_tables(length):
    index = np.arange(length)
    angle = (index[:, None] * index[None, :] % length) * (2.0 * math.pi / length)
    return np.cos(angle), np.sin(angle)


def with_halo(x, sides, width):
    for axis, dim in sides:
        count, length = lax.axis_size(axis), x.shape[dim]
        up = [(i, i + 1) for i in range(count - 1)]
        down = [(j, i) for i, j in up]
        before = lax.ppermute(lax.slice_in_dim(x, length - width, length, axis=dim), axis, up)
        after = lax.ppermute(lax.slice_in_dim(x, 0, width, axis=dim), axis, down)
        x = jnp.concatenate([before, x, after], axis=dim)
    return x


def stack_taps(padded, rows, slices, breadth):
    return jnp.concatenate(
        [
            padded[a : a + rows, b : b + slices, :, e : e + breadth]
            for a in range(3)
            for b in range(3)
            for e in range(3)
        ],
        axis=2,
    )


def tap_sum(taps, rows, slices, breadth):
    result = jnp.zeros((rows, slices, 2, breadth), F32)
    for place in range(27):
        a, b, e = place // 9, place // 3 % 3, place % 3
        result += taps[a : a + rows, b : b + slices, 2 * place : 2 * place + 2, e : e + breadth]
    return result


def regularize(damped, height, conv_first, bias_first, conv_second, bias_second):
    rows, slices, _, breadth = damped.shape
    extended = with_halo(damped.astype(BF16), (("coil", 0), ("sect", 1)), 2)
    padded = jnp.pad(extended, ((0, 0), (0, 0), (0, 0), (1, 1)))
    columns = stack_taps(padded, rows + 2, slices + 2, breadth)
    hidden = jnp.einsum("oc,rscw->rsow", conv_first, columns, preferred_element_type=F32)
    hidden = jax.nn.relu(hidden + bias_first[None, None, :, None]).astype(BF16)
    row_index = lax.axis_index("coil") * rows - 1 + jnp.arange(rows + 2)
    slice_index = lax.axis_index("sect") * slices - 1 + jnp.arange(slices + 2)
    row_valid = (row_index >= 0) & (row_index < height)
    slice_valid = (slice_index >= 0) & (slice_index < lax.axis_size("sect") * slices)
    inside = row_valid[:, None] & slice_valid[None, :]
    hidden = jnp.where(inside[:, :, None, None], hidden, jnp.zeros_like(hidden))
    hidden = jnp.pad(hidden, ((0, 0), (0, 0), (0, 0), (1, 1)))
    taps = jnp.einsum("tc,rscw->rstw", conv_second, hidden, preferred_element_type=F32)
    return tap_sum(taps, rows, slices, breadth) + bias_second[None, None, :, None]


def per_device(measured, coil_maps, sampling, conv_first, bias_first, conv_second, bias_second):
    height, coils_here, slices_here, _, breadth = coil_maps.shape
    count = lax.axis_size("coil")
    rows = height // count
    mask = sampling.astype(F32)

    def exchange(x):
        split = x.astype(BF16).reshape((count, rows) + x.shape[1:])
        return lax.all_to_all(split, "coil", 0, 0, tiled=True)

    row_cos, row_sin = dft_tables(height)
    col_cos, col_sin = dft_tables(breadth)
    row_table = jnp.asarray(np.stack([row_cos, row_sin]) / math.sqrt(height), F32)
    col_table = jnp.asarray(
        np.block([[col_cos, col_sin], [-col_sin, col_cos]]) / math.sqrt(breadth), F32
    ).reshape(2, breadth, 2, breadth)

    spread = jnp.einsum("tkh,kcsqw->tcsqwh", row_table, measured, precision=HIGH)
    spread = jnp.stack(
        [spread[0, :, :, 0] - spread[1, :, :, 1], spread[0, :, :, 1] + spread[1, :, :, 0]], axis=2
    )
    spread = spread * mask[None, :, None, :, None]
    inverse = jnp.einsum("qwpv,csqwh->csphv", col_table, spread, precision=HIGH)
    maps = jnp.transpose(coil_maps, (1, 2, 3, 0, 4))
    part_re = jnp.sum(maps[:, :, 0] * inverse[:, :, 0] + maps[:, :, 1] * inverse[:, :, 1], axis=0)
    part_im = jnp.sum(maps[:, :, 0] * inverse[:, :, 1] - maps[:, :, 1] * inverse[:, :, 0], axis=0)
    partial = jnp.transpose(jnp.stack([part_re, part_im], axis=1), (2, 0, 1, 3))
    first = jnp.sum(exchange(partial).astype(F32), axis=0)
    near = exchange(coil_maps).astype(F32)
    near_re, near_im = near[..., 0, :], near[..., 1, :]

    angle = jnp.asarray(np.stack([col_cos, col_sin]), F32)
    both = jnp.einsum("sl,alj,blv->absjv", mask, angle, angle, precision=HIGH) / breadth
    project_re = both[0, 0] + both[1, 1]
    project_im = both[0, 1] - both[1, 0]
    project = jnp.stack(
        [jnp.stack([project_re, project_im], 2), jnp.stack([-project_im, project_re], 2)]
    )

    image = first
    for _ in range(ITERS):
        image_re, image_im = image[:, :, 0], image[:, :, 1]
        product = jnp.stack(
            [near_re * image_re[:, None] - near_im * image_im[:, None],
             near_re * image_im[:, None] + near_im * image_re[:, None]]
        )
        spun = jnp.einsum("qnrcsj,qsjpv->pnrcsv", product, project, precision=HIGH)
        normal_re = jnp.sum(near_re * spun[0] + near_im * spun[1], axis=(0, 2))
        normal_im = jnp.sum(near_re * spun[1] - near_im * spun[0], axis=(0, 2))
        normal = jnp.stack([normal_re, normal_im], axis=2)
        damped = image - STEP * (normal - first)
        image = damped + regularize(
            damped, height, conv_first, bias_first, conv_second, bias_second
        )
    return image


def bf16_pair(table):
    high = table.astype(BF16)
    return high, (table - high.astype(np.float64)).astype(BF16)


def split3(x):
    high = x.astype(BF16)
    return high, (x - high.astype(F32)).astype(BF16)


def dot(x, y):
    return jnp.dot(x, y, preferred_element_type=F32)


def dot3(x, y):
    return dot(x[0], y[0]) + dot(x[1], y[0]) + dot(x[0], y[1])


def vmem(count):
    return [pl.BlockSpec(memory_space=pltpu.VMEM)] * count


def column_of(row):
    shape = (row.shape[1], row.shape[1])
    diagonal = lax.broadcasted_iota(jnp.int32, shape, 0) == lax.broadcasted_iota(jnp.int32, shape, 1)
    return jnp.sum(jnp.where(diagonal, jnp.broadcast_to(row, shape), 0.0), axis=1, keepdims=True)


def block_of(coil, sect):
    return 2 * coil + (sect + coil) % 2


def first_kernel(data_ref, maps_ref, mask_ref, row_ref, column_ref, send_ref, mask_out_ref, total_ref):
    _, slices, double, height = data_ref.shape
    breadth, wide = double // 2, slices * double // 2
    here, last = pl.program_id(0), pl.num_programs(0) - 1

    def emit(slot, parts):
        turned = [x.T.reshape(height // 8, 8, wide) for x in parts]
        rows = pl.ds(pl.multiple_of(16 * slot, 16), 16)
        both = jnp.concatenate(turned, axis=1).astype(BF16)
        for p in range(height // 8):
            send_ref[p, rows, :] = both[block_of(p // 2, p % 2)]

    maps = [[maps_ref[0, s, q * breadth : (q + 1) * breadth] for s in range(slices)] for q in range(2)]
    emit(here, [jnp.concatenate(x, axis=0) for x in maps])
    mask = mask_ref[...].astype(F32)
    mask_out_ref[...] = mask.astype(BF16)

    spreads, mixes = [], []
    for s in range(slices):
        high, low = split3(data_ref[0, s])
        spreads.append(dot(jnp.concatenate([high, low, high], axis=1), row_ref[...]))
    for s, spread in enumerate(spreads):
        keep = column_of(mask[s : s + 1])
        real, imag = spread[:breadth], spread[breadth:]
        pieces = [
            (real[:, :height] - imag[:, height:]) * keep, (imag[:, :height] + real[:, height:]) * keep,
        ]
        high, low = split3(jnp.concatenate(pieces, axis=1))
        mixes.append(jnp.concatenate([high, low, high], axis=0))
    mixes = [dot(column_ref[...], x) for x in mixes]
    for s, mixed in enumerate(mixes):
        cos_re, cos_im = mixed[:breadth, :height], mixed[:breadth, height:]
        sin_re, sin_im = mixed[breadth:, :height], mixed[breadth:, height:]
        inv_re, inv_im = cos_re - sin_im, sin_re + cos_im
        map_re, map_im = maps[0][s], maps[1][s]
        sums = (map_re * inv_re + map_im * inv_im, map_re * inv_im - map_im * inv_re)
        for q in range(2):
            rows = slice(s * breadth, (s + 1) * breadth)
            total_ref[q, rows] = sums[q] + jnp.where(here == 0, 0.0, total_ref[q, rows])

    @pl.when(here == last)
    def _():
        emit(last + 1, [total_ref[q] for q in range(2)])


def table_kernel(
    own_ref, other_ref, angle_ref, first_ref, bias_ref, second_ref, pick_first_ref, pick_second_ref, place_ref,
    project_ref, first_out_ref, second_out_ref,
):
    slices, breadth = own_ref.shape
    wide = slices * breadth
    here = lax.axis_index("sect")
    angle = angle_ref[...]
    swapped = jnp.concatenate([angle[:, wide:], -angle[:, :wide]], axis=1)
    cosine, sine = angle[:, :breadth], angle[:, wide : wide + breadth]
    angle, swapped = split3(angle), split3(swapped)
    for t in range(project_ref.shape[0]):
        mask = jnp.where(here == t, own_ref[...].astype(F32), other_ref[...].astype(F32))
        for s in range(slices):
            row = mask[s : s + 1]
            block = dot3(split3(cosine * row), angle) + dot3(split3(sine * row), swapped)
            if s:
                block = pltpu.roll(block, s * breadth, 1)
            rows = slice(s * breadth, (s + 1) * breadth)
            project_ref[t, rows] = block.astype(BF16)
            rows = slice(wide + s * breadth, wide + (s + 1) * breadth)
            project_ref[t, rows] = jnp.concatenate([-block[:, wide:], block[:, :wide]], axis=1).astype(BF16)

    groups, _, depth = pick_first_ref.shape
    features = first_ref.shape[1]
    bias = column_of(bias_ref[...])
    parts = []
    for _ in range(3):
        parts.append(bias.astype(BF16).astype(F32))
        bias = bias - parts[-1]
    lane = lax.broadcasted_iota(jnp.int32, (features, depth), 1)
    second = 0.0
    for s in range(groups):
        block = lax.dot_general(
            first_ref[...], pick_first_ref[s], (((0,), (0,)), ((), ())), preferred_element_type=F32
        )
        for i in range(3):
            block = jnp.where(lane == depth - 8 + i, parts[i], block)
        first_out_ref[s * features : (s + 1) * features] = block.astype(BF16)
        second += dot(dot(pick_second_ref[s], second_ref[...]).astype(BF16), place_ref[s])
    second_out_ref[...] = second.astype(BF16)


def apply_data_term(near_ref, project_ref, image, start, left_ref, spun_ref, breadth):
    result = []
    coils, groups = near_ref.shape[0], near_ref.shape[1]
    wide = near_ref.shape[3]
    for t in range(groups):
        image_re, image_im = image[t][:8], image[t][8:]

        def spread(i, carry, t=t, image_re=image_re, image_im=image_im):
            reals, imags = [], []
            for c in range(2):
                maps = near_ref[i, t, 16 * c : 16 * c + 16, :].astype(F32)
                map_re, map_im = maps[:8], maps[8:]
                reals.append(map_re * image_re - map_im * image_im)
                imags.append(map_re * image_im + map_im * image_re)
            rows = pl.ds(pl.multiple_of(16 * i, 16), 16)
            left_ref[rows, :wide] = jnp.concatenate(reals, axis=0).astype(BF16)
            left_ref[rows, wide:] = jnp.concatenate(imags, axis=0).astype(BF16)
            return carry

        lax.fori_loop(0, coils, spread, 0, unroll=4)
        spun_ref[...] = dot(left_ref[...], project_ref[t])

        def gather(i, carry, t=t):
            sum_re, sum_im = carry
            for c in range(2):
                maps = near_ref[i, t, 16 * c : 16 * c + 16, :].astype(F32)
                map_re, map_im = maps[:8], maps[8:]
                rows = pl.ds(pl.multiple_of(16 * i + 8 * c, 8), 8)
                spun_re, spun_im = spun_ref[rows, :wide], spun_ref[rows, wide:]
                sum_re += map_re * spun_re + map_im * spun_im
                sum_im += map_re * spun_im - map_im * spun_re
            return sum_re, sum_im

        zero = jnp.zeros((8, wide), F32)
        normal = jnp.concatenate(lax.fori_loop(0, coils, gather, (zero, zero), unroll=4), axis=0)
        result.append((normal, t))
    return [image[t] - STEP * (normal * (1.0 / breadth) - start[t]) for normal, t in result]


def to_rows(damped, out_ref, flip_ref, breadth):
    per_group = damped[0].shape[1] // breadth
    wide = damped[0].shape[1]
    lanes = lax.broadcasted_iota(jnp.int32, (16, LANES), 1)
    for t, value in enumerate(damped):
        for s in range(per_group):
            moved = value if s == 0 else pltpu.roll(value, wide - s * breadth, 1)
            moved = jnp.where(lanes < breadth, moved[:, :LANES], 0.0)
            for q in range(2):
                place = (t * per_group + s) * 2 + q
                for j in range(2):
                    part = moved[8 * q : 8 * q + 8, 128 * j : 128 * j + 128]
                    flip_ref[pl.ds(64 * j + place, 8, stride=8), :] = part
    for j in range(2):
        out_ref[:, 128 * j : 128 * j + 128] = flip_ref[64 * j : 64 * j + 64]


def from_rows(flip_ref, groups, per_group, breadth):
    wide = per_group * breadth
    result = []
    for t in range(groups):
        parts = []
        for q in range(2):
            value = jnp.zeros((8, wide), F32)
            for s in range(per_group):
                place = (t * per_group + s) * 2 + q
                halves = [flip_ref[pl.ds(64 * j + place, 8, stride=8), :] for j in range(2)]
                piece = jnp.concatenate(halves + [jnp.zeros((8, wide - LANES), F32)], axis=1)
                value += piece if s == 0 else pltpu.roll(piece, s * breadth, 1)
            parts.append(value)
        result.append(jnp.concatenate(parts, axis=0))
    return result


def position_of():
    return block_of(lax.axis_index("coil"), lax.axis_index("sect"))


def write_edges(rows_ref, inner_ref, outer_ref):
    odd = position_of() % 2 == 1
    low, high = rows_ref[:16], rows_ref[48:64]
    inner_ref[...] = jnp.where(odd, low, high).astype(BF16)
    outer_ref[...] = jnp.where(odd, high, low).astype(BF16)


def keep_close(*arrays):
    return [pltpu.with_memory_space_constraint(x, pltpu.VMEM) for x in arrays]


def second_kernel(
    near_ref, project_ref, rows_ref, inner_ref, outer_ref, start_ref,
    flip_ref, left_ref, spun_ref, *, breadth,
):
    coils, groups, _, wide = near_ref.shape
    start = []
    for t in range(groups):
        def add(i, total, t=t):
            return total + near_ref[i, t, 32:48, :].astype(F32)

        start.append(lax.fori_loop(0, coils, add, jnp.zeros((16, wide), F32), unroll=4))
        start_ref[t] = start[t]
    damped = apply_data_term(near_ref, project_ref, start, start, left_ref, spun_ref, breadth)
    to_rows(damped, rows_ref, flip_ref, breadth)
    write_edges(rows_ref, inner_ref, outer_ref)


def convolve(values, first_ref, second_ref, bias_ref, top, bottom, shift_ref, hidden_ref, breadth):
    count = len(values)
    for h, value in enumerate(values):
        shift_ref[24 * h : 24 * h + 8] = pltpu.roll(value, 1, 1)
        shift_ref[24 * h + 8 : 24 * h + 16] = value
        shift_ref[24 * h + 16 : 24 * h + 24] = pltpu.roll(value, LANES - 1, 1)
    ones = jnp.ones((8, LANES), F32)
    for g in range(count - 2):
        columns = jnp.concatenate([shift_ref[24 * g : 24 * g + 72], ones], axis=0).astype(BF16)
        hidden = dot(first_ref[...], columns).astype(BF16)
        hidden_ref[g] = jnp.maximum(hidden, jnp.zeros_like(hidden))
    lanes = lax.broadcasted_iota(jnp.int32, (1, LANES), 1)
    taps = []
    for g in range(count - 2):
        inside = lanes < breadth
        if g == 0:
            inside = inside & top
        if g == count - 3:
            inside = inside & bottom
        taps.append(jnp.where(inside, dot(second_ref[...], hidden_ref[g]), 0.0))
    odd = lax.broadcasted_iota(jnp.int32, (8, LANES), 0) % 2 == 1
    bias = jnp.where(odd, bias_ref[1], bias_ref[0])
    updates = []
    for h in range(count - 4):
        total = taps[h][:24] + taps[h + 1][24:48] + taps[h + 2][48:]
        update = pltpu.roll(total[:8], 1, 1) + total[8:16] + pltpu.roll(total[16:], LANES - 1, 1)
        updates.append(jnp.where(lanes < breadth, update + bias, 0.0))
    return updates


def edge_rows(first, second):
    value = jnp.where(position_of() % 2 == 1, first.astype(F32), second.astype(F32))
    return [value[:8], value[8:]]


def third_kernel(
    rows_ref, inner_ref, outer_ref, first_ref, second_ref, bias_ref, near_ref, project_ref, start_ref,
    out_ref, inner_out_ref, outer_out_ref,
    shift_ref, hidden_ref, flip_ref, left_ref, spun_ref, *, breadth,
):
    groups, _, wide = start_ref.shape
    inner, outer = inner_ref[...], outer_ref[...]
    own = [rows_ref[8 * h : 8 * h + 8] for h in range(8)]
    values = edge_rows(inner, outer) + own + edge_rows(outer, inner)
    last = 2 * lax.axis_size("coil") - 1
    updates = convolve(
        values, first_ref, second_ref, bias_ref, position_of() > 0, position_of() < last,
        shift_ref, hidden_ref, breadth,
    )
    for h in range(8):
        image = own[h] + updates[h]
        for j in range(2):
            flip_ref[64 * j + 8 * h : 64 * j + 8 * h + 8] = image[:, 128 * j : 128 * j + 128]
    image = from_rows(flip_ref, groups, wide // breadth, breadth)
    start = [start_ref[t] for t in range(groups)]
    damped = apply_data_term(near_ref, project_ref, image, start, left_ref, spun_ref, breadth)
    to_rows(damped, out_ref, flip_ref, breadth)
    write_edges(out_ref, inner_out_ref, outer_out_ref)


def last_kernel(
    rows_ref, partner_ref, outer_ref, skip_ref, first_ref, second_ref, bias_ref, out_ref,
    shift_ref, hidden_ref, *, breadth,
):
    odd = position_of() % 2 == 1
    coil = lax.axis_index("coil")
    pairs = [
        (rows_ref[8 * h : 8 * h + 8], partner_ref[8 * h : 8 * h + 8]) for h in range(8)
    ]
    own = [jnp.where(odd, b, a) for a, b in pairs] + [jnp.where(odd, a, b) for a, b in pairs]
    outer, skip = outer_ref[...], skip_ref[...]
    values = edge_rows(skip, outer) + own + edge_rows(outer, skip)
    updates = convolve(
        values, first_ref, second_ref, bias_ref, coil > 0, coil < lax.axis_size("coil") - 1,
        shift_ref, hidden_ref, breadth,
    )
    upper = lax.axis_index("sect") == 0
    for h in range(16):
        image = (own[h] + updates[h])[:, :breadth]
        image = jnp.where(upper, image[:4], image[4:])
        for s in range(2):
            out_ref[h, s] = image[2 * s : 2 * s + 2]


def fast_device(measured, coil_maps, sampling, conv_first, bias_first, conv_second, bias_second):
    height, coils_here, slices_here, _, breadth = coil_maps.shape
    ranks, sects = lax.axis_size("coil"), lax.axis_size("sect")
    count = ranks * sects
    slices = slices_here * sects
    wide = slices_here * breadth
    features = conv_first.shape[0]
    both = ("coil", "sect")
    f32 = lambda *dims: jax.ShapeDtypeStruct(dims, F32)
    bf16 = lambda *dims: jax.ShapeDtypeStruct(dims, BF16)

    row_cos, row_sin = dft_tables(height)
    col_cos, col_sin = dft_tables(breadth)
    row_high, row_low = bf16_pair(np.concatenate([row_cos, row_sin], axis=1) / math.sqrt(height))
    column_high, column_low = bf16_pair(np.concatenate([col_cos, col_sin], axis=0) / math.sqrt(breadth))
    row_table = jnp.asarray(np.concatenate([row_high, row_high, row_low], axis=0))
    column_table = jnp.asarray(np.concatenate([column_high, column_high, column_low], axis=1))
    by_coil = lambda x: jnp.transpose(x, (1, 2, 3, 4, 0)).reshape(coils_here, slices_here, 2 * breadth, height)
    slab = pl.BlockSpec((1, slices_here, 2 * breadth, height), lambda c: (c, 0, 0, 0))
    whole = lambda *dims: pl.BlockSpec(dims, lambda c: (0,) * len(dims))
    block_rows = 16 * (coils_here + 1)
    send, mask = pl.pallas_call(
        first_kernel,
        grid=(coils_here,),
        in_specs=[
            slab, slab, whole(slices_here, breadth), whole(*row_table.shape), whole(*column_table.shape),
        ],
        out_specs=[whole(count, block_rows, wide), whole(slices_here, breadth)],
        out_shape=[bf16(count, block_rows, wide), bf16(slices_here, breadth)],
        scratch_shapes=[pltpu.VMEM((2, wide, height), F32)],
    )(by_coil(measured), by_coil(coil_maps), sampling, row_table, column_table)
    near = lax.all_to_all(send, both, 0, 0, tiled=True).reshape(ranks, sects, block_rows, wide)

    other = lax.ppermute(mask, "sect", [(0, 1), (1, 0)])
    blank = np.zeros((breadth, wide - breadth))
    angle = np.concatenate([col_cos, blank, col_sin, blank], axis=1).astype(np.float32)
    span = 18 * slices
    pick_first = np.zeros((slices, 54, span + 8))
    pick_second = np.zeros((slices, span, 54))
    for a, b, e, q, s in np.ndindex(3, 3, 3, 2, slices):
        tap = 2 * (9 * a + 3 * b + e) + q
        if 0 <= s + b - 1 < slices:
            pick_first[s, tap, ((a * 3 + e) * slices + s + b - 1) * 2 + q] = 1.0
            pick_second[s + b - 1, ((a * 3 + e) * slices + s) * 2 + q, tap] = 1.0
    place = np.eye(slices * features).reshape(slices, features, slices * features)
    project, matrix_first, matrix_second = pl.pallas_call(
        table_kernel,
        compiler_params=MODEST,
        in_specs=vmem(9), out_specs=vmem(3),
        out_shape=[
            pltpu.VMEM(dims, BF16)
            for dims in (
                (sects, 2 * wide, 2 * wide), (slices * features, span + 8), (span, slices * features),
            )
        ],
    )(
        mask, other, jnp.asarray(angle), conv_first.T, bias_first.reshape(1, features), conv_second,
        *[jnp.asarray(x.astype(BF16)) for x in (pick_first, pick_second, place)],
    )
    weights = (*keep_close(matrix_first, matrix_second), bias_second)
    weight_specs = vmem(2) + [pl.BlockSpec(memory_space=pltpu.SMEM)]

    owner = {block_of(i, y): 2 * i + y for i in range(ranks) for y in range(2)}
    near_pairs, skip_pairs = [], []
    for block in range(1, count - 1, 2):
        near_pairs += [(owner[block], owner[block + 1]), (owner[block + 1], owner[block])]
        skip_pairs += [(owner[block], owner[block + 2]), (owner[block + 1], owner[block - 1])]
    swap = lambda x: lax.ppermute(x, "sect", [(0, 1), (1, 0)])

    edge = 4 * slices
    work = [
        pltpu.VMEM((32 * slices, 128), F32),
        pltpu.VMEM((16 * ranks, 2 * wide), BF16), pltpu.VMEM((16 * ranks, 2 * wide), F32),
    ]

    def room(rows):
        return [
            pltpu.VMEM(((rows + 4) * 6 * slices, LANES), F32),
            pltpu.VMEM((rows + 2, slices * features, LANES), BF16),
        ]

    row_shapes = [f32(16 * slices, LANES), bf16(edge, LANES), bf16(edge, LANES)]
    rows, inner, outer, start = pl.pallas_call(
        functools.partial(second_kernel, breadth=breadth),
        compiler_params=MODEST,
        in_specs=vmem(2), out_specs=vmem(4),
        out_shape=row_shapes + [pltpu.VMEM((sects, 16, wide), F32)], scratch_shapes=work,
    )(*keep_close(near, project))
    for _ in range(ITERS - 1):
        rows, inner, outer = pl.pallas_call(
            functools.partial(third_kernel, breadth=breadth),
            compiler_params=MODEST,
            in_specs=vmem(3) + weight_specs + vmem(3), out_specs=vmem(3), out_shape=row_shapes,
            scratch_shapes=room(8) + work,
        )(*keep_close(rows, swap(inner), lax.ppermute(outer, both, near_pairs)), *weights, *keep_close(near, project, start))
    return pl.pallas_call(
        functools.partial(last_kernel, breadth=breadth),
        compiler_params=MODEST,
        in_specs=vmem(4) + weight_specs, out_specs=vmem(1)[0],
        out_shape=f32(16, slices_here, 2, breadth), scratch_shapes=room(16),
    )(
        *keep_close(
            rows, swap(rows), lax.ppermute(outer, both, near_pairs), lax.ppermute(outer, both, skip_pairs)
        ),
        *weights,
    )


def per_device_any(measured, coil_maps, *rest):
    height, coils_here, slices_here, _, breadth = coil_maps.shape
    ranks, sects = lax.axis_size("coil"), lax.axis_size("sect")
    fits = (
        sects == 2 and slices_here == 2 and coils_here == 2 and height == 8 * ranks * sects
        and 2 * breadth % 128 == 0 and 128 < breadth < LANES and breadth % 16 == 0
    )
    return (fast_device if fits else per_device)(measured, coil_maps, *rest)


def solution(mesh):
    coil_spec = P(None, "coil", "sect", None, None)
    in_specs = (coil_spec, coil_spec, P("sect", None), P(), P(), P(), P())
    return jax.shard_map(
        per_device_any,
        mesh=mesh,
        in_specs=in_specs,
        out_specs=P("coil", "sect", None, None),
        check_vma=False,
    )
```

```python
import functools
import math

import jax
import jax.numpy as jnp
import numpy as np
from jax import lax
from jax.experimental import pallas as pl
from jax.experimental.pallas import tpu as pltpu
from jax.sharding import PartitionSpec as P

ITERS = 2
STEP = 0.5
F32 = jnp.float32
BF16 = jnp.bfloat16
HIGH = lax.Precision.HIGH
LANES = 256
MODEST = pltpu.CompilerParams(vmem_limit_bytes=24 << 20)


def dft_tables(length):
    index = np.arange(length)
    angle = (index[:, None] * index[None, :] % length) * (2.0 * math.pi / length)
    return np.cos(angle), np.sin(angle)


def with_halo(x, sides, width):
    for axis, dim in sides:
        count, length = lax.axis_size(axis), x.shape[dim]
        up = [(i, i + 1) for i in range(count - 1)]
        down = [(j, i) for i, j in up]
        before = lax.ppermute(lax.slice_in_dim(x, length - width, length, axis=dim), axis, up)
        after = lax.ppermute(lax.slice_in_dim(x, 0, width, axis=dim), axis, down)
        x = jnp.concatenate([before, x, after], axis=dim)
    return x


def stack_taps(padded, rows, slices, breadth):
    return jnp.concatenate(
        [
            padded[a : a + rows, b : b + slices, :, e : e + breadth]
            for a in range(3)
            for b in range(3)
            for e in range(3)
        ],
        axis=2,
    )


def tap_sum(taps, rows, slices, breadth):
    result = jnp.zeros((rows, slices, 2, breadth), F32)
    for place in range(27):
        a, b, e = place // 9, place // 3 % 3, place % 3
        result += taps[a : a + rows, b : b + slices, 2 * place : 2 * place + 2, e : e + breadth]
    return result


def regularize(damped, height, conv_first, bias_first, conv_second, bias_second):
    rows, slices, _, breadth = damped.shape
    extended = with_halo(damped.astype(BF16), (("coil", 0), ("sect", 1)), 2)
    padded = jnp.pad(extended, ((0, 0), (0, 0), (0, 0), (1, 1)))
    columns = stack_taps(padded, rows + 2, slices + 2, breadth)
    hidden = jnp.einsum("oc,rscw->rsow", conv_first, columns, preferred_element_type=F32)
    hidden = jax.nn.relu(hidden + bias_first[None, None, :, None]).astype(BF16)
    row_index = lax.axis_index("coil") * rows - 1 + jnp.arange(rows + 2)
    slice_index = lax.axis_index("sect") * slices - 1 + jnp.arange(slices + 2)
    row_valid = (row_index >= 0) & (row_index < height)
    slice_valid = (slice_index >= 0) & (slice_index < lax.axis_size("sect") * slices)
    inside = row_valid[:, None] & slice_valid[None, :]
    hidden = jnp.where(inside[:, :, None, None], hidden, jnp.zeros_like(hidden))
    hidden = jnp.pad(hidden, ((0, 0), (0, 0), (0, 0), (1, 1)))
    taps = jnp.einsum("tc,rscw->rstw", conv_second, hidden, preferred_element_type=F32)
    return tap_sum(taps, rows, slices, breadth) + bias_second[None, None, :, None]


def per_device(measured, coil_maps, sampling, conv_first, bias_first, conv_second, bias_second):
    height, coils_here, slices_here, _, breadth = coil_maps.shape
    count = lax.axis_size("coil")
    rows = height // count
    mask = sampling.astype(F32)

    def exchange(x):
        split = x.astype(BF16).reshape((count, rows) + x.shape[1:])
        return lax.all_to_all(split, "coil", 0, 0, tiled=True)

    row_cos, row_sin = dft_tables(height)
    col_cos, col_sin = dft_tables(breadth)
    row_table = jnp.asarray(np.stack([row_cos, row_sin]) / math.sqrt(height), F32)
    col_table = jnp.asarray(
        np.block([[col_cos, col_sin], [-col_sin, col_cos]]) / math.sqrt(breadth), F32
    ).reshape(2, breadth, 2, breadth)

    spread = jnp.einsum("tkh,kcsqw->tcsqwh", row_table, measured, precision=HIGH)
    spread = jnp.stack(
        [spread[0, :, :, 0] - spread[1, :, :, 1], spread[0, :, :, 1] + spread[1, :, :, 0]], axis=2
    )
    spread = spread * mask[None, :, None, :, None]
    inverse = jnp.einsum("qwpv,csqwh->csphv", col_table, spread, precision=HIGH)
    maps = jnp.transpose(coil_maps, (1, 2, 3, 0, 4))
    part_re = jnp.sum(maps[:, :, 0] * inverse[:, :, 0] + maps[:, :, 1] * inverse[:, :, 1], axis=0)
    part_im = jnp.sum(maps[:, :, 0] * inverse[:, :, 1] - maps[:, :, 1] * inverse[:, :, 0], axis=0)
    partial = jnp.transpose(jnp.stack([part_re, part_im], axis=1), (2, 0, 1, 3))
    first = jnp.sum(exchange(partial).astype(F32), axis=0)
    near = exchange(coil_maps).astype(F32)
    near_re, near_im = near[..., 0, :], near[..., 1, :]

    angle = jnp.asarray(np.stack([col_cos, col_sin]), F32)
    both = jnp.einsum("sl,alj,blv->absjv", mask, angle, angle, precision=HIGH) / breadth
    project_re = both[0, 0] + both[1, 1]
    project_im = both[0, 1] - both[1, 0]
    project = jnp.stack(
        [jnp.stack([project_re, project_im], 2), jnp.stack([-project_im, project_re], 2)]
    )

    image = first
    for _ in range(ITERS):
        image_re, image_im = image[:, :, 0], image[:, :, 1]
        product = jnp.stack(
            [near_re * image_re[:, None] - near_im * image_im[:, None],
             near_re * image_im[:, None] + near_im * image_re[:, None]]
        )
        spun = jnp.einsum("qnrcsj,qsjpv->pnrcsv", product, project, precision=HIGH)
        normal_re = jnp.sum(near_re * spun[0] + near_im * spun[1], axis=(0, 2))
        normal_im = jnp.sum(near_re * spun[1] - near_im * spun[0], axis=(0, 2))
        normal = jnp.stack([normal_re, normal_im], axis=2)
        damped = image - STEP * (normal - first)
        image = damped + regularize(
            damped, height, conv_first, bias_first, conv_second, bias_second
        )
    return image


def bf16_pair(table):
    high = table.astype(BF16)
    return high, (table - high.astype(np.float64)).astype(BF16)


def split3(x):
    high = x.astype(BF16)
    return high, (x - high.astype(F32)).astype(BF16)


def dot(x, y):
    return jnp.dot(x, y, preferred_element_type=F32)


def dot3(x, y):
    return dot(x[0], y[0]) + dot(x[1], y[0]) + dot(x[0], y[1])


def vmem(count):
    return [pl.BlockSpec(memory_space=pltpu.VMEM)] * count


def column_of(row):
    shape = (row.shape[1], row.shape[1])
    diagonal = lax.broadcasted_iota(jnp.int32, shape, 0) == lax.broadcasted_iota(jnp.int32, shape, 1)
    return jnp.sum(jnp.where(diagonal, jnp.broadcast_to(row, shape), 0.0), axis=1, keepdims=True)


def block_of(coil, sect):
    return 2 * coil + (sect + coil) % 2


def first_kernel(
    data_ref, maps_ref, mask_far_ref, row_far_ref, column_far_ref, send_ref, mask_out_ref,
    data_copy, maps_copy, mask_ref, row_ref, column_ref, total_ref, out_copy, sems, table_sems, send_sems,
):
    coils, slices, double, height = data_ref.shape
    breadth, wide = double // 2, slices * double // 2
    chains = [(c, s) for s in range(slices) for c in range(coils)]
    tables = ((mask_far_ref, mask_ref), (row_far_ref, row_ref), (column_far_ref, column_ref))
    tables = [pltpu.make_async_copy(x, y, table_sems.at[i]) for i, (x, y) in enumerate(tables)]
    copies = [
        [
            pltpu.make_async_copy(source.at[c, s], target.at[c, s], sems.at[k, i])
            for i, (c, s) in enumerate(chains)
        ]
        for k, (source, target) in enumerate(((data_ref, data_copy), (maps_ref, maps_copy)))
    ]
    sends = []
    pair = 2
    early = tables[:2] + copies[0][:pair]
    late = copies[0][pair:] + tables[2:] + copies[1]
    for copy in early:
        copy.start()
    for copy in late:
        copy.start()
    tables[0].wait()
    mask = mask_ref[...].astype(F32)
    mask_out_ref[...] = mask.astype(BF16)
    keep = [column_of(mask[s : s + 1]) for s in range(slices)]

    def along_rows(i):
        high, low = split3(data_copy[chains[i]])
        return dot(jnp.concatenate([high, low, high], axis=1), row_ref[...])

    def combine(i, spread):
        real, imag = spread[:breadth], spread[breadth:]
        here = keep[chains[i][1]]
        pieces = [
            (real[:, :height] - imag[:, height:]) * here, (imag[:, :height] + real[:, height:]) * here,
        ]
        high, low = split3(jnp.concatenate(pieces, axis=1))
        return jnp.concatenate([high, low, high], axis=0)

    def along_columns(right):
        return dot(column_ref[...], right)

    def finish(i, mixed):
        c, s = chains[i]
        inv_re = mixed[:breadth, :height] - mixed[breadth:, height:]
        inv_im = mixed[breadth:, :height] + mixed[:breadth, height:]
        map_re, map_im = maps_copy[c, s, :breadth], maps_copy[c, s, breadth:]
        rows = slice(s * breadth, (s + 1) * breadth)
        for q, value in enumerate((map_re * inv_re + map_im * inv_im, map_re * inv_im - map_im * inv_re)):
            total_ref[q, rows] = value + total_ref[q, rows] if c else value

    def emit(slot, parts):
        turned = [x.T.reshape(height // 8, 8, wide) for x in parts]
        both = jnp.concatenate(turned, axis=1).astype(BF16)
        for p in range(height // 8):
            out_copy[slot, p] = both[block_of(p // 2, p % 2)]
        rows = send_ref.at[:, 16 * slot : 16 * slot + 16, :]
        sends.append(pltpu.make_async_copy(out_copy.at[slot], rows, send_sems.at[slot]))
        sends[-1].start()

    def emit_maps(c):
        emit(c, [
            jnp.concatenate([maps_copy[c, s, q * breadth : (q + 1) * breadth] for s in range(slices)], axis=0)
            for q in range(2)
        ])

    count = len(chains)
    spread, right, mixed = {}, {}, {}
    for step in range(0, count + 3 * pair, pair):
        for copy in early[1:] if step == 0 else late if step == pair else []:
            copy.wait()
        for i in range(step, step + pair):
            if i < count:
                spread[i] = along_rows(i)
            if 0 <= i - 2 * pair < count:
                mixed[i - 2 * pair] = along_columns(right.pop(i - 2 * pair))
        if 0 < step <= pair * coils:
            emit_maps(step // pair - 1)
        for i in range(step, step + pair):
            if 0 <= i - pair < count:
                right[i - pair] = combine(i - pair, spread.pop(i - pair))
            if 0 <= i - 3 * pair < count:
                finish(i - 3 * pair, mixed.pop(i - 3 * pair))
    emit(coils, [total_ref[q] for q in range(2)])
    for copy in sends:
        copy.wait()


def table_kernel(
    own_ref, other_ref, angle_ref, first_ref, bias_ref, second_ref, pick_first_ref, pick_second_ref, place_ref,
    project_ref, first_out_ref, second_out_ref,
):
    slices, breadth = own_ref.shape
    wide = slices * breadth
    here = lax.axis_index("sect")
    angle = angle_ref[...]
    swapped = jnp.concatenate([angle[:, wide:], -angle[:, :wide]], axis=1)
    cosine, sine = angle[:, :breadth], angle[:, wide : wide + breadth]
    angle, swapped = split3(angle), split3(swapped)
    for t in range(project_ref.shape[0]):
        mask = jnp.where(here == t, own_ref[...].astype(F32), other_ref[...].astype(F32))
        for s in range(slices):
            row = mask[s : s + 1]
            block = dot3(split3(cosine * row), angle) + dot3(split3(sine * row), swapped)
            if s:
                block = pltpu.roll(block, s * breadth, 1)
            rows = slice(s * breadth, (s + 1) * breadth)
            project_ref[t, rows] = block.astype(BF16)
            rows = slice(wide + s * breadth, wide + (s + 1) * breadth)
            project_ref[t, rows] = jnp.concatenate([-block[:, wide:], block[:, :wide]], axis=1).astype(BF16)

    groups, _, depth = pick_first_ref.shape
    features = first_ref.shape[1]
    bias = column_of(bias_ref[...])
    parts = []
    for _ in range(3):
        parts.append(bias.astype(BF16).astype(F32))
        bias = bias - parts[-1]
    lane = lax.broadcasted_iota(jnp.int32, (features, depth), 1)
    second = 0.0
    for s in range(groups):
        block = lax.dot_general(
            first_ref[...], pick_first_ref[s], (((0,), (0,)), ((), ())), preferred_element_type=F32
        )
        for i in range(3):
            block = jnp.where(lane == depth - 8 + i, parts[i], block)
        first_out_ref[s * features : (s + 1) * features] = block.astype(BF16)
        second += dot(dot(pick_second_ref[s], second_ref[...]).astype(BF16), place_ref[s])
    second_out_ref[...] = second.astype(BF16)


def apply_data_term(near_ref, project_ref, image, start, left_ref, spun_ref, breadth):
    result = []
    coils, groups = near_ref.shape[0], near_ref.shape[1]
    wide = near_ref.shape[3]
    for t in range(groups):
        image_re, image_im = image[t][:8], image[t][8:]

        def spread(i, carry, t=t, image_re=image_re, image_im=image_im):
            reals, imags = [], []
            for c in range(2):
                maps = near_ref[i, t, 16 * c : 16 * c + 16, :].astype(F32)
                map_re, map_im = maps[:8], maps[8:]
                reals.append(map_re * image_re - map_im * image_im)
                imags.append(map_re * image_im + map_im * image_re)
            rows = pl.ds(pl.multiple_of(16 * i, 16), 16)
            left_ref[rows, :wide] = jnp.concatenate(reals, axis=0).astype(BF16)
            left_ref[rows, wide:] = jnp.concatenate(imags, axis=0).astype(BF16)
            return carry

        lax.fori_loop(0, coils, spread, 0, unroll=4)
        spun_ref[...] = dot(left_ref[...], project_ref[t])

        def gather(i, carry, t=t):
            sum_re, sum_im = carry
            for c in range(2):
                maps = near_ref[i, t, 16 * c : 16 * c + 16, :].astype(F32)
                map_re, map_im = maps[:8], maps[8:]
                rows = pl.ds(pl.multiple_of(16 * i + 8 * c, 8), 8)
                spun_re, spun_im = spun_ref[rows, :wide], spun_ref[rows, wide:]
                sum_re += map_re * spun_re + map_im * spun_im
                sum_im += map_re * spun_im - map_im * spun_re
            return sum_re, sum_im

        zero = jnp.zeros((8, wide), F32)
        normal = jnp.concatenate(lax.fori_loop(0, coils, gather, (zero, zero), unroll=4), axis=0)
        result.append((normal, t))
    return [image[t] - STEP * (normal * (1.0 / breadth) - start[t]) for normal, t in result]


def to_rows(damped, out_ref, flip_ref, breadth):
    per_group = damped[0].shape[1] // breadth
    wide = damped[0].shape[1]
    lanes = lax.broadcasted_iota(jnp.int32, (16, LANES), 1)
    for t, value in enumerate(damped):
        for s in range(per_group):
            moved = value if s == 0 else pltpu.roll(value, wide - s * breadth, 1)
            moved = jnp.where(lanes < breadth, moved[:, :LANES], 0.0)
            for q in range(2):
                place = (t * per_group + s) * 2 + q
                for j in range(2):
                    part = moved[8 * q : 8 * q + 8, 128 * j : 128 * j + 128]
                    flip_ref[pl.ds(64 * j + place, 8, stride=8), :] = part
    for j in range(2):
        out_ref[:, 128 * j : 128 * j + 128] = flip_ref[64 * j : 64 * j + 64]


def from_rows(flip_ref, groups, per_group, breadth):
    wide = per_group * breadth
    result = []
    for t in range(groups):
        parts = []
        for q in range(2):
            value = jnp.zeros((8, wide), F32)
            for s in range(per_group):
                place = (t * per_group + s) * 2 + q
                halves = [flip_ref[pl.ds(64 * j + place, 8, stride=8), :] for j in range(2)]
                piece = jnp.concatenate(halves + [jnp.zeros((8, wide - LANES), F32)], axis=1)
                value += piece if s == 0 else pltpu.roll(piece, s * breadth, 1)
            parts.append(value)
        result.append(jnp.concatenate(parts, axis=0))
    return result


def position_of():
    return block_of(lax.axis_index("coil"), lax.axis_index("sect"))


def write_edges(rows_ref, inner_ref, outer_ref):
    odd = position_of() % 2 == 1
    low, high = rows_ref[:16], rows_ref[48:64]
    inner_ref[...] = jnp.where(odd, low, high).astype(BF16)
    outer_ref[...] = jnp.where(odd, high, low).astype(BF16)


def keep_close(*arrays):
    return [pltpu.with_memory_space_constraint(x, pltpu.VMEM) for x in arrays]


def second_kernel(
    near_ref, project_ref, rows_ref, inner_ref, outer_ref, start_ref,
    flip_ref, left_ref, spun_ref, *, breadth,
):
    coils, groups, _, wide = near_ref.shape
    start = []
    for t in range(groups):
        def add(i, total, t=t):
            return total + near_ref[i, t, 32:48, :].astype(F32)

        start.append(lax.fori_loop(0, coils, add, jnp.zeros((16, wide), F32), unroll=4))
        start_ref[t] = start[t]
    damped = apply_data_term(near_ref, project_ref, start, start, left_ref, spun_ref, breadth)
    to_rows(damped, rows_ref, flip_ref, breadth)
    write_edges(rows_ref, inner_ref, outer_ref)


def convolve(values, first_ref, second_ref, bias_ref, top, bottom, shift_ref, hidden_ref, breadth):
    count = len(values)
    for h, value in enumerate(values):
        shift_ref[24 * h : 24 * h + 8] = pltpu.roll(value, 1, 1)
        shift_ref[24 * h + 8 : 24 * h + 16] = value
        shift_ref[24 * h + 16 : 24 * h + 24] = pltpu.roll(value, LANES - 1, 1)
    ones = jnp.ones((8, LANES), F32)
    for g in range(count - 2):
        columns = jnp.concatenate([shift_ref[24 * g : 24 * g + 72], ones], axis=0).astype(BF16)
        hidden = dot(first_ref[...], columns).astype(BF16)
        hidden_ref[g] = jnp.maximum(hidden, jnp.zeros_like(hidden))
    lanes = lax.broadcasted_iota(jnp.int32, (1, LANES), 1)
    taps = []
    for g in range(count - 2):
        inside = lanes < breadth
        if g == 0:
            inside = inside & top
        if g == count - 3:
            inside = inside & bottom
        taps.append(jnp.where(inside, dot(second_ref[...], hidden_ref[g]), 0.0))
    odd = lax.broadcasted_iota(jnp.int32, (8, LANES), 0) % 2 == 1
    bias = jnp.where(odd, bias_ref[1], bias_ref[0])
    updates = []
    for h in range(count - 4):
        total = taps[h][:24] + taps[h + 1][24:48] + taps[h + 2][48:]
        update = pltpu.roll(total[:8], 1, 1) + total[8:16] + pltpu.roll(total[16:], LANES - 1, 1)
        updates.append(jnp.where(lanes < breadth, update + bias, 0.0))
    return updates


def edge_rows(first, second):
    value = jnp.where(position_of() % 2 == 1, first.astype(F32), second.astype(F32))
    return [value[:8], value[8:]]


def third_kernel(
    rows_ref, inner_ref, outer_ref, first_ref, second_ref, bias_ref, near_ref, project_ref, start_ref,
    out_ref, inner_out_ref, outer_out_ref,
    shift_ref, hidden_ref, flip_ref, left_ref, spun_ref, *, breadth,
):
    groups, _, wide = start_ref.shape
    inner, outer = inner_ref[...], outer_ref[...]
    own = [rows_ref[8 * h : 8 * h + 8] for h in range(8)]
    values = edge_rows(inner, outer) + own + edge_rows(outer, inner)
    last = 2 * lax.axis_size("coil") - 1
    updates = convolve(
        values, first_ref, second_ref, bias_ref, position_of() > 0, position_of() < last,
        shift_ref, hidden_ref, breadth,
    )
    for h in range(8):
        image = own[h] + updates[h]
        for j in range(2):
            flip_ref[64 * j + 8 * h : 64 * j + 8 * h + 8] = image[:, 128 * j : 128 * j + 128]
    image = from_rows(flip_ref, groups, wide // breadth, breadth)
    start = [start_ref[t] for t in range(groups)]
    damped = apply_data_term(near_ref, project_ref, image, start, left_ref, spun_ref, breadth)
    to_rows(damped, out_ref, flip_ref, breadth)
    write_edges(out_ref, inner_out_ref, outer_out_ref)


def pack_kernel(rows_ref, outer_ref, out_ref):
    out_ref[:64] = rows_ref[...]
    out_ref[64:] = outer_ref[...].astype(F32)


def last_kernel(
    own_ref, partner_ref, first_ref, second_ref, bias_ref, out_ref, shift_ref, hidden_ref, *, breadth,
):
    odd = position_of() % 2 == 1
    coil = lax.axis_index("coil")
    pairs = [
        (own_ref[8 * h : 8 * h + 8], partner_ref[8 * h : 8 * h + 8]) for h in range(8)
    ]
    own = [jnp.where(odd, b, a) for a, b in pairs] + [jnp.where(odd, a, b) for a, b in pairs]
    outer, skip = own_ref[64:], partner_ref[64:]
    values = edge_rows(skip, outer) + own + edge_rows(outer, skip)
    updates = convolve(
        values, first_ref, second_ref, bias_ref, coil > 0, coil < lax.axis_size("coil") - 1,
        shift_ref, hidden_ref, breadth,
    )
    upper = lax.axis_index("sect") == 0
    for h in range(16):
        image = (own[h] + updates[h])[:, :breadth]
        image = jnp.where(upper, image[:4], image[4:])
        for s in range(2):
            out_ref[h, s] = image[2 * s : 2 * s + 2]


def fast_device(measured, coil_maps, sampling, conv_first, bias_first, conv_second, bias_second):
    height, coils_here, slices_here, _, breadth = coil_maps.shape
    ranks, sects = lax.axis_size("coil"), lax.axis_size("sect")
    count = ranks * sects
    slices = slices_here * sects
    wide = slices_here * breadth
    features = conv_first.shape[0]
    both = ("coil", "sect")
    f32 = lambda *dims: jax.ShapeDtypeStruct(dims, F32)
    bf16 = lambda *dims: jax.ShapeDtypeStruct(dims, BF16)

    row_cos, row_sin = dft_tables(height)
    col_cos, col_sin = dft_tables(breadth)
    row_high, row_low = bf16_pair(np.concatenate([row_cos, row_sin], axis=1) / math.sqrt(height))
    column_high, column_low = bf16_pair(np.concatenate([col_cos, col_sin], axis=0) / math.sqrt(breadth))
    row_table = jnp.asarray(np.concatenate([row_high, row_high, row_low], axis=0))
    column_table = jnp.asarray(np.concatenate([column_high, column_high, column_low], axis=1))
    by_coil = lambda x: jnp.transpose(x, (1, 2, 3, 4, 0)).reshape(coils_here, slices_here, 2 * breadth, height)
    block_rows = 16 * (coils_here + 1)
    slab = (coils_here, slices_here, 2 * breadth, height)
    far = (by_coil(measured), by_coil(coil_maps), sampling, row_table, column_table)
    send, mask = pl.pallas_call(
        first_kernel,
        compiler_params=pltpu.CompilerParams(vmem_limit_bytes=40 << 20),
        in_specs=[pl.BlockSpec(memory_space=pl.ANY)] * 5,
        out_specs=[pl.BlockSpec(memory_space=pl.ANY)] + vmem(1),
        out_shape=[bf16(count, block_rows, wide), bf16(slices_here, breadth)],
        scratch_shapes=[
            pltpu.VMEM(slab, F32), pltpu.VMEM(slab, F32), *[pltpu.VMEM(x.shape, x.dtype) for x in far[2:]],
            pltpu.VMEM((2, wide, height), F32), pltpu.VMEM((coils_here + 1, count, 16, wide), BF16),
            pltpu.SemaphoreType.DMA((2, coils_here * slices_here)), pltpu.SemaphoreType.DMA((3,)),
            pltpu.SemaphoreType.DMA((coils_here + 1,)),
        ],
    )(*[pltpu.with_memory_space_constraint(x, pltpu.HBM) for x in far])
    near = lax.all_to_all(send, both, 0, 0, tiled=True).reshape(ranks, sects, block_rows, wide)

    other = lax.ppermute(mask, "sect", [(0, 1), (1, 0)])
    blank = np.zeros((breadth, wide - breadth))
    angle = np.concatenate([col_cos, blank, col_sin, blank], axis=1).astype(np.float32)
    span = 18 * slices
    pick_first = np.zeros((slices, 54, span + 8))
    pick_second = np.zeros((slices, span, 54))
    for a, b, e, q, s in np.ndindex(3, 3, 3, 2, slices):
        tap = 2 * (9 * a + 3 * b + e) + q
        if 0 <= s + b - 1 < slices:
            pick_first[s, tap, ((a * 3 + e) * slices + s + b - 1) * 2 + q] = 1.0
            pick_second[s + b - 1, ((a * 3 + e) * slices + s) * 2 + q, tap] = 1.0
    place = np.eye(slices * features).reshape(slices, features, slices * features)
    project, matrix_first, matrix_second = pl.pallas_call(
        table_kernel,
        compiler_params=MODEST,
        in_specs=vmem(9), out_specs=vmem(3),
        out_shape=[
            pltpu.VMEM(dims, BF16)
            for dims in (
                (sects, 2 * wide, 2 * wide), (slices * features, span + 8), (span, slices * features),
            )
        ],
    )(
        mask, other, jnp.asarray(angle), conv_first.T, bias_first.reshape(1, features), conv_second,
        *[jnp.asarray(x.astype(BF16)) for x in (pick_first, pick_second, place)],
    )
    weights = (*keep_close(matrix_first, matrix_second), bias_second)
    weight_specs = vmem(2) + [pl.BlockSpec(memory_space=pltpu.SMEM)]

    owner = {block_of(i, y): 2 * i + y for i in range(ranks) for y in range(2)}
    near_pairs = []
    for block in range(1, count - 1, 2):
        near_pairs += [(owner[block], owner[block + 1]), (owner[block + 1], owner[block])]
    swap = lambda x: lax.ppermute(x, "sect", [(0, 1), (1, 0)])

    edge = 4 * slices
    work = [
        pltpu.VMEM((32 * slices, 128), F32),
        pltpu.VMEM((16 * ranks, 2 * wide), BF16), pltpu.VMEM((16 * ranks, 2 * wide), F32),
    ]

    def room(rows):
        return [
            pltpu.VMEM(((rows + 4) * 6 * slices, LANES), F32),
            pltpu.VMEM((rows + 2, slices * features, LANES), BF16),
        ]

    row_shapes = [f32(16 * slices, LANES), bf16(edge, LANES), bf16(edge, LANES)]
    rows, inner, outer, start = pl.pallas_call(
        functools.partial(second_kernel, breadth=breadth),
        compiler_params=MODEST,
        in_specs=vmem(2), out_specs=vmem(4),
        out_shape=row_shapes + [pltpu.VMEM((sects, 16, wide), F32)], scratch_shapes=work,
    )(*keep_close(near, project))
    for _ in range(ITERS - 1):
        rows, inner, outer = pl.pallas_call(
            functools.partial(third_kernel, breadth=breadth),
            compiler_params=MODEST,
            in_specs=vmem(3) + weight_specs + vmem(3), out_specs=vmem(3), out_shape=row_shapes,
            scratch_shapes=room(8) + work,
        )(*keep_close(rows, swap(inner), lax.ppermute(outer, both, near_pairs)), *weights, *keep_close(near, project, start))
    packed = pl.pallas_call(
        pack_kernel, compiler_params=MODEST, in_specs=vmem(2), out_specs=vmem(1)[0],
        out_shape=f32(16 * slices + edge, LANES),
    )(*keep_close(rows, lax.ppermute(outer, both, near_pairs)))
    return pl.pallas_call(
        functools.partial(last_kernel, breadth=breadth),
        compiler_params=MODEST,
        in_specs=vmem(2) + weight_specs, out_specs=vmem(1)[0],
        out_shape=f32(16, slices_here, 2, breadth), scratch_shapes=room(16),
    )(*keep_close(packed, swap(packed)), *weights)


def per_device_any(measured, coil_maps, *rest):
    height, coils_here, slices_here, _, breadth = coil_maps.shape
    ranks, sects = lax.axis_size("coil"), lax.axis_size("sect")
    fits = (
        sects == 2 and slices_here == 2 and coils_here == 2 and height == 8 * ranks * sects
        and 2 * breadth % 128 == 0 and 128 < breadth < LANES and breadth % 16 == 0
    )
    return (fast_device if fits else per_device)(measured, coil_maps, *rest)


def solution(mesh):
    coil_spec = P(None, "coil", "sect", None, None)
    in_specs = (coil_spec, coil_spec, P("sect", None), P(), P(), P(), P())
    return jax.shard_map(
        per_device_any,
        mesh=mesh,
        in_specs=in_specs,
        out_specs=P("coil", "sect", None, None),
        check_vma=False,
    )
```

```python
import functools
import math

import jax
import jax.numpy as jnp
import numpy as np
from jax import lax
from jax.experimental import pallas as pl
from jax.experimental.pallas import tpu as pltpu
from jax.sharding import PartitionSpec as P

ITERS = 2
STEP = 0.5
F32 = jnp.float32
BF16 = jnp.bfloat16
HIGH = lax.Precision.HIGH
LANES = 256
MODEST = pltpu.CompilerParams(vmem_limit_bytes=24 << 20)


def dft_tables(length):
    index = np.arange(length)
    angle = (index[:, None] * index[None, :] % length) * (2.0 * math.pi / length)
    return np.cos(angle), np.sin(angle)


def with_halo(x, sides, width):
    for axis, dim in sides:
        count, length = lax.axis_size(axis), x.shape[dim]
        up = [(i, i + 1) for i in range(count - 1)]
        down = [(j, i) for i, j in up]
        before = lax.ppermute(lax.slice_in_dim(x, length - width, length, axis=dim), axis, up)
        after = lax.ppermute(lax.slice_in_dim(x, 0, width, axis=dim), axis, down)
        x = jnp.concatenate([before, x, after], axis=dim)
    return x


def stack_taps(padded, rows, slices, breadth):
    return jnp.concatenate(
        [
            padded[a : a + rows, b : b + slices, :, e : e + breadth]
            for a in range(3)
            for b in range(3)
            for e in range(3)
        ],
        axis=2,
    )


def tap_sum(taps, rows, slices, breadth):
    result = jnp.zeros((rows, slices, 2, breadth), F32)
    for place in range(27):
        a, b, e = place // 9, place // 3 % 3, place % 3
        result += taps[a : a + rows, b : b + slices, 2 * place : 2 * place + 2, e : e + breadth]
    return result


def regularize(damped, height, conv_first, bias_first, conv_second, bias_second):
    rows, slices, _, breadth = damped.shape
    extended = with_halo(damped.astype(BF16), (("coil", 0), ("sect", 1)), 2)
    padded = jnp.pad(extended, ((0, 0), (0, 0), (0, 0), (1, 1)))
    columns = stack_taps(padded, rows + 2, slices + 2, breadth)
    hidden = jnp.einsum("oc,rscw->rsow", conv_first, columns, preferred_element_type=F32)
    hidden = jax.nn.relu(hidden + bias_first[None, None, :, None]).astype(BF16)
    row_index = lax.axis_index("coil") * rows - 1 + jnp.arange(rows + 2)
    slice_index = lax.axis_index("sect") * slices - 1 + jnp.arange(slices + 2)
    row_valid = (row_index >= 0) & (row_index < height)
    slice_valid = (slice_index >= 0) & (slice_index < lax.axis_size("sect") * slices)
    inside = row_valid[:, None] & slice_valid[None, :]
    hidden = jnp.where(inside[:, :, None, None], hidden, jnp.zeros_like(hidden))
    hidden = jnp.pad(hidden, ((0, 0), (0, 0), (0, 0), (1, 1)))
    taps = jnp.einsum("tc,rscw->rstw", conv_second, hidden, preferred_element_type=F32)
    return tap_sum(taps, rows, slices, breadth) + bias_second[None, None, :, None]


def per_device(measured, coil_maps, sampling, conv_first, bias_first, conv_second, bias_second):
    height, coils_here, slices_here, _, breadth = coil_maps.shape
    count = lax.axis_size("coil")
    rows = height // count
    mask = sampling.astype(F32)

    def exchange(x):
        split = x.astype(BF16).reshape((count, rows) + x.shape[1:])
        return lax.all_to_all(split, "coil", 0, 0, tiled=True)

    row_cos, row_sin = dft_tables(height)
    col_cos, col_sin = dft_tables(breadth)
    row_table = jnp.asarray(np.stack([row_cos, row_sin]) / math.sqrt(height), F32)
    col_table = jnp.asarray(
        np.block([[col_cos, col_sin], [-col_sin, col_cos]]) / math.sqrt(breadth), F32
    ).reshape(2, breadth, 2, breadth)

    spread = jnp.einsum("tkh,kcsqw->tcsqwh", row_table, measured, precision=HIGH)
    spread = jnp.stack(
        [spread[0, :, :, 0] - spread[1, :, :, 1], spread[0, :, :, 1] + spread[1, :, :, 0]], axis=2
    )
    spread = spread * mask[None, :, None, :, None]
    inverse = jnp.einsum("qwpv,csqwh->csphv", col_table, spread, precision=HIGH)
    maps = jnp.transpose(coil_maps, (1, 2, 3, 0, 4))
    part_re = jnp.sum(maps[:, :, 0] * inverse[:, :, 0] + maps[:, :, 1] * inverse[:, :, 1], axis=0)
    part_im = jnp.sum(maps[:, :, 0] * inverse[:, :, 1] - maps[:, :, 1] * inverse[:, :, 0], axis=0)
    partial = jnp.transpose(jnp.stack([part_re, part_im], axis=1), (2, 0, 1, 3))
    first = jnp.sum(exchange(partial).astype(F32), axis=0)
    near = exchange(coil_maps).astype(F32)
    near_re, near_im = near[..., 0, :], near[..., 1, :]

    angle = jnp.asarray(np.stack([col_cos, col_sin]), F32)
    both = jnp.einsum("sl,alj,blv->absjv", mask, angle, angle, precision=HIGH) / breadth
    project_re = both[0, 0] + both[1, 1]
    project_im = both[0, 1] - both[1, 0]
    project = jnp.stack(
        [jnp.stack([project_re, project_im], 2), jnp.stack([-project_im, project_re], 2)]
    )

    image = first
    for _ in range(ITERS):
        image_re, image_im = image[:, :, 0], image[:, :, 1]
        product = jnp.stack(
            [near_re * image_re[:, None] - near_im * image_im[:, None],
             near_re * image_im[:, None] + near_im * image_re[:, None]]
        )
        spun = jnp.einsum("qnrcsj,qsjpv->pnrcsv", product, project, precision=HIGH)
        normal_re = jnp.sum(near_re * spun[0] + near_im * spun[1], axis=(0, 2))
        normal_im = jnp.sum(near_re * spun[1] - near_im * spun[0], axis=(0, 2))
        normal = jnp.stack([normal_re, normal_im], axis=2)
        damped = image - STEP * (normal - first)
        image = damped + regularize(
            damped, height, conv_first, bias_first, conv_second, bias_second
        )
    return image


def bf16_pair(table):
    high = table.astype(BF16)
    return high, (table - high.astype(np.float64)).astype(BF16)


def split3(x):
    high = x.astype(BF16)
    return high, (x - high.astype(F32)).astype(BF16)


def dot(x, y):
    return jnp.dot(x, y, preferred_element_type=F32)


def dot3(x, y):
    return dot(x[0], y[0]) + dot(x[1], y[0]) + dot(x[0], y[1])


def vmem(count):
    return [pl.BlockSpec(memory_space=pltpu.VMEM)] * count


def column_of(row):
    shape = (row.shape[1], row.shape[1])
    diagonal = lax.broadcasted_iota(jnp.int32, shape, 0) == lax.broadcasted_iota(jnp.int32, shape, 1)
    return jnp.sum(jnp.where(diagonal, jnp.broadcast_to(row, shape), 0.0), axis=1, keepdims=True)


def block_of(coil, sect):
    return 2 * coil + (sect + coil) % 2


def first_kernel(
    data_ref, maps_ref, mask_far_ref, row_far_ref, column_far_ref, send_ref, mask_out_ref,
    data_copy, maps_copy, mask_ref, row_ref, column_ref, total_ref, out_copy, sems, table_sems, send_sems,
):
    coils, slices, double, height = data_ref.shape
    breadth, wide = double // 2, slices * double // 2
    chains = [(c, s) for s in range(slices) for c in range(coils)]
    tables = ((mask_far_ref, mask_ref), (row_far_ref, row_ref), (column_far_ref, column_ref))
    tables = [pltpu.make_async_copy(x, y, table_sems.at[i]) for i, (x, y) in enumerate(tables)]
    copies = [
        [
            pltpu.make_async_copy(source.at[c, s], target.at[c, s], sems.at[k, i])
            for i, (c, s) in enumerate(chains)
        ]
        for k, (source, target) in enumerate(((data_ref, data_copy), (maps_ref, maps_copy)))
    ]
    sends = []
    pair = 2
    early = tables[:2] + copies[0][:pair]
    late = copies[0][pair:] + tables[2:] + copies[1]
    for copy in early:
        copy.start()
    for copy in late:
        copy.start()
    tables[0].wait()
    mask = mask_ref[...].astype(F32)
    mask_out_ref[...] = mask.astype(BF16)
    keep = [column_of(mask[s : s + 1]) for s in range(slices)]

    def along_rows(i):
        high, low = split3(data_copy[chains[i]])
        return dot(jnp.concatenate([high, low, high], axis=1), row_ref[...])

    def combine(i, spread):
        real, imag = spread[:breadth], spread[breadth:]
        here = keep[chains[i][1]]
        pieces = [
            (real[:, :height] - imag[:, height:]) * here, (imag[:, :height] + real[:, height:]) * here,
        ]
        high, low = split3(jnp.concatenate(pieces, axis=1))
        return jnp.concatenate([high, low, high], axis=0)

    def along_columns(right):
        return dot(column_ref[...], right)

    def finish(i, mixed):
        c, s = chains[i]
        inv_re = mixed[:breadth, :height] - mixed[breadth:, height:]
        inv_im = mixed[breadth:, :height] + mixed[:breadth, height:]
        map_re, map_im = maps_copy[c, s, :breadth], maps_copy[c, s, breadth:]
        rows = slice(s * breadth, (s + 1) * breadth)
        for q, value in enumerate((map_re * inv_re + map_im * inv_im, map_re * inv_im - map_im * inv_re)):
            total_ref[q, rows] = value + total_ref[q, rows] if c else value

    def emit(slot, parts):
        turned = [x.T.reshape(height // 8, 8, wide) for x in parts]
        both = jnp.concatenate(turned, axis=1).astype(BF16)
        for p in range(height // 8):
            out_copy[slot, p] = both[block_of(p // 2, p % 2)]
        rows = send_ref.at[:, 16 * slot : 16 * slot + 16, :]
        sends.append(pltpu.make_async_copy(out_copy.at[slot], rows, send_sems.at[slot]))
        sends[-1].start()

    def emit_maps(c):
        emit(c, [
            jnp.concatenate([maps_copy[c, s, q * breadth : (q + 1) * breadth] for s in range(slices)], axis=0)
            for q in range(2)
        ])

    count = len(chains)
    spread, right, mixed = {}, {}, {}
    for step in range(0, count + 3 * pair, pair):
        for copy in early[1:] if step == 0 else late if step == pair else []:
            copy.wait()
        for i in range(step, step + pair):
            if i < count:
                spread[i] = along_rows(i)
            if 0 <= i - 2 * pair < count:
                mixed[i - 2 * pair] = along_columns(right.pop(i - 2 * pair))
        if 0 < step <= pair * coils:
            emit_maps(step // pair - 1)
        for i in range(step, step + pair):
            if 0 <= i - pair < count:
                right[i - pair] = combine(i - pair, spread.pop(i - pair))
            if 0 <= i - 3 * pair < count:
                finish(i - 3 * pair, mixed.pop(i - 3 * pair))
    emit(coils, [total_ref[q] for q in range(2)])
    for copy in sends:
        copy.wait()


def table_kernel(
    own_ref, other_ref, angle_ref, first_ref, bias_ref, second_ref, pick_first_ref, pick_second_ref, place_ref,
    project_ref, first_out_ref, second_out_ref,
):
    slices, breadth = own_ref.shape
    wide = slices * breadth
    here = lax.axis_index("sect")
    angle = angle_ref[...]
    swapped = jnp.concatenate([angle[:, wide:], -angle[:, :wide]], axis=1)
    cosine, sine = angle[:, :breadth], angle[:, wide : wide + breadth]
    angle, swapped = split3(angle), split3(swapped)
    for t in range(project_ref.shape[0]):
        mask = jnp.where(here == t, own_ref[...].astype(F32), other_ref[...].astype(F32))
        for s in range(slices):
            row = mask[s : s + 1]
            block = dot3(split3(cosine * row), angle) + dot3(split3(sine * row), swapped)
            if s:
                block = pltpu.roll(block, s * breadth, 1)
            rows = slice(s * breadth, (s + 1) * breadth)
            project_ref[t, rows] = block.astype(BF16)
            rows = slice(wide + s * breadth, wide + (s + 1) * breadth)
            project_ref[t, rows] = jnp.concatenate([-block[:, wide:], block[:, :wide]], axis=1).astype(BF16)

    groups, _, depth = pick_first_ref.shape
    features = first_ref.shape[1]
    bias = column_of(bias_ref[...])
    parts = []
    for _ in range(3):
        parts.append(bias.astype(BF16).astype(F32))
        bias = bias - parts[-1]
    lane = lax.broadcasted_iota(jnp.int32, (features, depth), 1)
    second = 0.0
    for s in range(groups):
        block = lax.dot_general(
            first_ref[...], pick_first_ref[s], (((0,), (0,)), ((), ())), preferred_element_type=F32
        )
        for i in range(3):
            block = jnp.where(lane == depth - 8 + i, parts[i], block)
        first_out_ref[s * features : (s + 1) * features] = block.astype(BF16)
        second += dot(dot(pick_second_ref[s], second_ref[...]).astype(BF16), place_ref[s])
    second_out_ref[...] = second.astype(BF16)


def apply_data_term(near_ref, project_ref, image, start, left_ref, spun_ref, breadth):
    result = []
    coils, groups = near_ref.shape[0], near_ref.shape[1]
    wide = near_ref.shape[3]
    for t in range(groups):
        image_re, image_im = image[t][:8], image[t][8:]

        def spread(i, carry, t=t, image_re=image_re, image_im=image_im):
            reals, imags = [], []
            for c in range(2):
                maps = near_ref[i, t, 16 * c : 16 * c + 16, :].astype(F32)
                map_re, map_im = maps[:8], maps[8:]
                reals.append(map_re * image_re - map_im * image_im)
                imags.append(map_re * image_im + map_im * image_re)
            rows = pl.ds(pl.multiple_of(16 * i, 16), 16)
            left_ref[rows, :wide] = jnp.concatenate(reals, axis=0).astype(BF16)
            left_ref[rows, wide:] = jnp.concatenate(imags, axis=0).astype(BF16)
            return carry

        lax.fori_loop(0, coils, spread, 0, unroll=4)
        spun_ref[...] = dot(left_ref[...], project_ref[t])

        def gather(i, carry, t=t):
            sum_re, sum_im = carry
            for c in range(2):
                maps = near_ref[i, t, 16 * c : 16 * c + 16, :].astype(F32)
                map_re, map_im = maps[:8], maps[8:]
                rows = pl.ds(pl.multiple_of(16 * i + 8 * c, 8), 8)
                spun_re, spun_im = spun_ref[rows, :wide], spun_ref[rows, wide:]
                sum_re += map_re * spun_re + map_im * spun_im
                sum_im += map_re * spun_im - map_im * spun_re
            return sum_re, sum_im

        zero = jnp.zeros((8, wide), F32)
        normal = jnp.concatenate(lax.fori_loop(0, coils, gather, (zero, zero), unroll=4), axis=0)
        result.append((normal, t))
    return [image[t] - STEP * (normal * (1.0 / breadth) - start[t]) for normal, t in result]


def to_rows(damped, out_ref, flip_ref, breadth):
    per_group = damped[0].shape[1] // breadth
    wide = damped[0].shape[1]
    lanes = lax.broadcasted_iota(jnp.int32, (16, LANES), 1)
    for t, value in enumerate(damped):
        for s in range(per_group):
            moved = value if s == 0 else pltpu.roll(value, wide - s * breadth, 1)
            moved = jnp.where(lanes < breadth, moved[:, :LANES], 0.0)
            for q in range(2):
                place = (t * per_group + s) * 2 + q
                for j in range(2):
                    part = moved[8 * q : 8 * q + 8, 128 * j : 128 * j + 128]
                    flip_ref[pl.ds(64 * j + place, 8, stride=8), :] = part
    for j in range(2):
        out_ref[:, 128 * j : 128 * j + 128] = flip_ref[64 * j : 64 * j + 64]


def from_rows(flip_ref, groups, per_group, breadth):
    wide = per_group * breadth
    result = []
    for t in range(groups):
        parts = []
        for q in range(2):
            value = jnp.zeros((8, wide), F32)
            for s in range(per_group):
                place = (t * per_group + s) * 2 + q
                halves = [flip_ref[pl.ds(64 * j + place, 8, stride=8), :] for j in range(2)]
                piece = jnp.concatenate(halves + [jnp.zeros((8, wide - LANES), F32)], axis=1)
                value += piece if s == 0 else pltpu.roll(piece, s * breadth, 1)
            parts.append(value)
        result.append(jnp.concatenate(parts, axis=0))
    return result


def position_of():
    return block_of(lax.axis_index("coil"), lax.axis_index("sect"))


def write_edges(rows_ref, inner_ref, outer_ref):
    odd = position_of() % 2 == 1
    low, high = rows_ref[:16], rows_ref[48:64]
    inner_ref[...] = jnp.where(odd, low, high).astype(BF16)
    outer_ref[...] = jnp.where(odd, high, low).astype(BF16)


def keep_close(*arrays):
    return [pltpu.with_memory_space_constraint(x, pltpu.VMEM) for x in arrays]


def second_kernel(
    near_ref, project_ref, rows_ref, inner_ref, outer_ref, start_ref,
    flip_ref, left_ref, spun_ref, *, breadth,
):
    coils, groups, _, wide = near_ref.shape
    start = []
    for t in range(groups):
        def add(i, total, t=t):
            return total + near_ref[i, t, 32:48, :].astype(F32)

        start.append(lax.fori_loop(0, coils, add, jnp.zeros((16, wide), F32), unroll=4))
        start_ref[t] = start[t]
    damped = apply_data_term(near_ref, project_ref, start, start, left_ref, spun_ref, breadth)
    to_rows(damped, rows_ref, flip_ref, breadth)
    write_edges(rows_ref, inner_ref, outer_ref)


def convolve(values, first_ref, second_ref, bias_ref, top, bottom, shift_ref, hidden_ref, breadth):
    count = len(values)
    for h, value in enumerate(values):
        shift_ref[24 * h : 24 * h + 8] = pltpu.roll(value, 1, 1)
        shift_ref[24 * h + 8 : 24 * h + 16] = value
        shift_ref[24 * h + 16 : 24 * h + 24] = pltpu.roll(value, LANES - 1, 1)
    ones = jnp.ones((8, LANES), F32)
    for g in range(count - 2):
        columns = jnp.concatenate([shift_ref[24 * g : 24 * g + 72], ones], axis=0).astype(BF16)
        hidden = dot(first_ref[...], columns).astype(BF16)
        hidden_ref[g] = jnp.maximum(hidden, jnp.zeros_like(hidden))
    lanes = lax.broadcasted_iota(jnp.int32, (1, LANES), 1)
    taps = []
    for g in range(count - 2):
        inside = lanes < breadth
        if g == 0:
            inside = inside & top
        if g == count - 3:
            inside = inside & bottom
        taps.append(jnp.where(inside, dot(second_ref[...], hidden_ref[g]), 0.0))
    odd = lax.broadcasted_iota(jnp.int32, (8, LANES), 0) % 2 == 1
    bias = jnp.where(odd, bias_ref[1], bias_ref[0])
    updates = []
    for h in range(count - 4):
        total = taps[h][:24] + taps[h + 1][24:48] + taps[h + 2][48:]
        update = pltpu.roll(total[:8], 1, 1) + total[8:16] + pltpu.roll(total[16:], LANES - 1, 1)
        updates.append(jnp.where(lanes < breadth, update + bias, 0.0))
    return updates


def edge_rows(first, second):
    value = jnp.where(position_of() % 2 == 1, first.astype(F32), second.astype(F32))
    return [value[:8], value[8:]]


def regularized(
    rows_ref, inner_ref, outer_ref, first_ref, second_ref, bias_ref, shift_ref, hidden_ref, breadth
):
    inner, outer = inner_ref[...], outer_ref[...]
    own = [rows_ref[8 * h : 8 * h + 8] for h in range(8)]
    values = edge_rows(inner, outer) + own + edge_rows(outer, inner)
    last = 2 * lax.axis_size("coil") - 1
    updates = convolve(
        values, first_ref, second_ref, bias_ref, position_of() > 0, position_of() < last,
        shift_ref, hidden_ref, breadth,
    )
    return own, updates


def third_kernel(
    rows_ref, inner_ref, outer_ref, first_ref, second_ref, bias_ref, near_ref, project_ref, start_ref,
    out_ref, inner_out_ref, outer_out_ref,
    shift_ref, hidden_ref, flip_ref, left_ref, spun_ref, *, breadth,
):
    groups, _, wide = start_ref.shape
    own, updates = regularized(
        rows_ref, inner_ref, outer_ref, first_ref, second_ref, bias_ref, shift_ref, hidden_ref, breadth
    )
    for h in range(8):
        image = own[h] + updates[h]
        for j in range(2):
            flip_ref[64 * j + 8 * h : 64 * j + 8 * h + 8] = image[:, 128 * j : 128 * j + 128]
    image = from_rows(flip_ref, groups, wide // breadth, breadth)
    start = [start_ref[t] for t in range(groups)]
    damped = apply_data_term(near_ref, project_ref, image, start, left_ref, spun_ref, breadth)
    to_rows(damped, out_ref, flip_ref, breadth)
    write_edges(out_ref, inner_out_ref, outer_out_ref)


def last_kernel(
    rows_ref, inner_ref, outer_ref, first_ref, second_ref, bias_ref, keep_ref, give_ref,
    shift_ref, hidden_ref, *, breadth,
):
    own, updates = regularized(
        rows_ref, inner_ref, outer_ref, first_ref, second_ref, bias_ref, shift_ref, hidden_ref, breadth
    )
    upper = lax.axis_index("sect") == 0
    for h in range(8):
        image = (own[h] + updates[h])[:, :breadth]
        keep, give = jnp.where(upper, image[:4], image[4:]), jnp.where(upper, image[4:], image[:4])
        for s in range(2):
            keep_ref[h, s] = keep[2 * s : 2 * s + 2]
            give_ref[h, s] = give[2 * s : 2 * s + 2]


def join_kernel(keep_ref, got_ref, out_ref):
    odd = position_of() % 2 == 1
    keep, got = keep_ref[...], got_ref[...]
    out_ref[:8] = jnp.where(odd, got, keep)
    out_ref[8:] = jnp.where(odd, keep, got)


def fast_device(measured, coil_maps, sampling, conv_first, bias_first, conv_second, bias_second):
    height, coils_here, slices_here, _, breadth = coil_maps.shape
    ranks, sects = lax.axis_size("coil"), lax.axis_size("sect")
    count = ranks * sects
    slices = slices_here * sects
    wide = slices_here * breadth
    features = conv_first.shape[0]
    both = ("coil", "sect")
    f32 = lambda *dims: jax.ShapeDtypeStruct(dims, F32)
    bf16 = lambda *dims: jax.ShapeDtypeStruct(dims, BF16)

    row_cos, row_sin = dft_tables(height)
    col_cos, col_sin = dft_tables(breadth)
    row_high, row_low = bf16_pair(np.concatenate([row_cos, row_sin], axis=1) / math.sqrt(height))
    column_high, column_low = bf16_pair(np.concatenate([col_cos, col_sin], axis=0) / math.sqrt(breadth))
    row_table = jnp.asarray(np.concatenate([row_high, row_high, row_low], axis=0))
    column_table = jnp.asarray(np.concatenate([column_high, column_high, column_low], axis=1))
    by_coil = lambda x: jnp.transpose(x, (1, 2, 3, 4, 0)).reshape(coils_here, slices_here, 2 * breadth, height)
    block_rows = 16 * (coils_here + 1)
    slab = (coils_here, slices_here, 2 * breadth, height)
    far = (by_coil(measured), by_coil(coil_maps), sampling, row_table, column_table)
    send, mask = pl.pallas_call(
        first_kernel,
        compiler_params=pltpu.CompilerParams(vmem_limit_bytes=40 << 20),
        in_specs=[pl.BlockSpec(memory_space=pl.ANY)] * 5,
        out_specs=[pl.BlockSpec(memory_space=pl.ANY)] + vmem(1),
        out_shape=[bf16(count, block_rows, wide), bf16(slices_here, breadth)],
        scratch_shapes=[
            pltpu.VMEM(slab, F32), pltpu.VMEM(slab, F32), *[pltpu.VMEM(x.shape, x.dtype) for x in far[2:]],
            pltpu.VMEM((2, wide, height), F32), pltpu.VMEM((coils_here + 1, count, 16, wide), BF16),
            pltpu.SemaphoreType.DMA((2, coils_here * slices_here)), pltpu.SemaphoreType.DMA((3,)),
            pltpu.SemaphoreType.DMA((coils_here + 1,)),
        ],
    )(*[pltpu.with_memory_space_constraint(x, pltpu.HBM) for x in far])
    near = lax.all_to_all(send, both, 0, 0, tiled=True).reshape(ranks, sects, block_rows, wide)

    other = lax.ppermute(mask, "sect", [(0, 1), (1, 0)])
    blank = np.zeros((breadth, wide - breadth))
    angle = np.concatenate([col_cos, blank, col_sin, blank], axis=1).astype(np.float32)
    span = 18 * slices
    pick_first = np.zeros((slices, 54, span + 8))
    pick_second = np.zeros((slices, span, 54))
    for a, b, e, q, s in np.ndindex(3, 3, 3, 2, slices):
        tap = 2 * (9 * a + 3 * b + e) + q
        if 0 <= s + b - 1 < slices:
            pick_first[s, tap, ((a * 3 + e) * slices + s + b - 1) * 2 + q] = 1.0
            pick_second[s + b - 1, ((a * 3 + e) * slices + s) * 2 + q, tap] = 1.0
    place = np.eye(slices * features).reshape(slices, features, slices * features)
    project, matrix_first, matrix_second = pl.pallas_call(
        table_kernel,
        compiler_params=MODEST,
        in_specs=vmem(9), out_specs=vmem(3),
        out_shape=[
            pltpu.VMEM(dims, BF16)
            for dims in (
                (sects, 2 * wide, 2 * wide), (slices * features, span + 8), (span, slices * features),
            )
        ],
    )(
        mask, other, jnp.asarray(angle), conv_first.T, bias_first.reshape(1, features), conv_second,
        *[jnp.asarray(x.astype(BF16)) for x in (pick_first, pick_second, place)],
    )
    weights = (*keep_close(matrix_first, matrix_second), bias_second)
    weight_specs = vmem(2) + [pl.BlockSpec(memory_space=pltpu.SMEM)]

    owner = {block_of(i, y): 2 * i + y for i in range(ranks) for y in range(2)}
    near_pairs = []
    for block in range(1, count - 1, 2):
        near_pairs += [(owner[block], owner[block + 1]), (owner[block + 1], owner[block])]
    swap = lambda x: lax.ppermute(x, "sect", [(0, 1), (1, 0)])

    edge = 4 * slices
    work = [
        pltpu.VMEM((32 * slices, 128), F32),
        pltpu.VMEM((16 * ranks, 2 * wide), BF16), pltpu.VMEM((16 * ranks, 2 * wide), F32),
    ]

    def room(rows):
        return [
            pltpu.VMEM(((rows + 4) * 6 * slices, LANES), F32),
            pltpu.VMEM((rows + 2, slices * features, LANES), BF16),
        ]

    row_shapes = [f32(16 * slices, LANES), bf16(edge, LANES), bf16(edge, LANES)]
    rows, inner, outer, start = pl.pallas_call(
        functools.partial(second_kernel, breadth=breadth),
        compiler_params=MODEST,
        in_specs=vmem(2), out_specs=vmem(4),
        out_shape=row_shapes + [pltpu.VMEM((sects, 16, wide), F32)], scratch_shapes=work,
    )(*keep_close(near, project))
    for _ in range(ITERS - 1):
        rows, inner, outer = pl.pallas_call(
            functools.partial(third_kernel, breadth=breadth),
            compiler_params=MODEST,
            in_specs=vmem(3) + weight_specs + vmem(3), out_specs=vmem(3), out_shape=row_shapes,
            scratch_shapes=room(8) + work,
        )(*keep_close(rows, swap(inner), lax.ppermute(outer, both, near_pairs)), *weights, *keep_close(near, project, start))
    piece = f32(8, slices_here, 2, breadth)
    keep, give = pl.pallas_call(
        functools.partial(last_kernel, breadth=breadth),
        compiler_params=MODEST,
        in_specs=vmem(3) + weight_specs, out_specs=vmem(2), out_shape=[piece, piece],
        scratch_shapes=room(8),
    )(*keep_close(rows, swap(inner), lax.ppermute(outer, both, near_pairs)), *weights)
    return pl.pallas_call(
        join_kernel, compiler_params=MODEST, in_specs=vmem(2), out_specs=vmem(1)[0],
        out_shape=f32(16, slices_here, 2, breadth),
    )(*keep_close(keep, swap(give)))


def per_device_any(measured, coil_maps, *rest):
    height, coils_here, slices_here, _, breadth = coil_maps.shape
    ranks, sects = lax.axis_size("coil"), lax.axis_size("sect")
    fits = (
        sects == 2 and slices_here == 2 and coils_here == 2 and height == 8 * ranks * sects
        and 2 * breadth % 128 == 0 and 128 < breadth < LANES and breadth % 16 == 0
    )
    return (fast_device if fits else per_device)(measured, coil_maps, *rest)


def solution(mesh):
    coil_spec = P(None, "coil", "sect", None, None)
    in_specs = (coil_spec, coil_spec, P("sect", None), P(), P(), P(), P())
    return jax.shard_map(
        per_device_any,
        mesh=mesh,
        in_specs=in_specs,
        out_specs=P("coil", "sect", None, None),
        check_vma=False,
    )
```

```python
import functools
import math

import jax
import jax.numpy as jnp
import numpy as np
from jax import lax
from jax.experimental import pallas as pl
from jax.experimental.pallas import tpu as pltpu
from jax.sharding import PartitionSpec as P

ITERS = 2
STEP = 0.5
F32 = jnp.float32
BF16 = jnp.bfloat16
HIGH = lax.Precision.HIGH
LANES = 256
MODEST = pltpu.CompilerParams(vmem_limit_bytes=24 << 20)


def dft_tables(length):
    index = np.arange(length)
    angle = (index[:, None] * index[None, :] % length) * (2.0 * math.pi / length)
    return np.cos(angle), np.sin(angle)


def with_halo(x, sides, width):
    for axis, dim in sides:
        count, length = lax.axis_size(axis), x.shape[dim]
        up = [(i, i + 1) for i in range(count - 1)]
        down = [(j, i) for i, j in up]
        before = lax.ppermute(lax.slice_in_dim(x, length - width, length, axis=dim), axis, up)
        after = lax.ppermute(lax.slice_in_dim(x, 0, width, axis=dim), axis, down)
        x = jnp.concatenate([before, x, after], axis=dim)
    return x


def stack_taps(padded, rows, slices, breadth):
    return jnp.concatenate(
        [
            padded[a : a + rows, b : b + slices, :, e : e + breadth]
            for a in range(3)
            for b in range(3)
            for e in range(3)
        ],
        axis=2,
    )


def tap_sum(taps, rows, slices, breadth):
    result = jnp.zeros((rows, slices, 2, breadth), F32)
    for place in range(27):
        a, b, e = place // 9, place // 3 % 3, place % 3
        result += taps[a : a + rows, b : b + slices, 2 * place : 2 * place + 2, e : e + breadth]
    return result


def regularize(damped, height, conv_first, bias_first, conv_second, bias_second):
    rows, slices, _, breadth = damped.shape
    extended = with_halo(damped.astype(BF16), (("coil", 0), ("sect", 1)), 2)
    padded = jnp.pad(extended, ((0, 0), (0, 0), (0, 0), (1, 1)))
    columns = stack_taps(padded, rows + 2, slices + 2, breadth)
    hidden = jnp.einsum("oc,rscw->rsow", conv_first, columns, preferred_element_type=F32)
    hidden = jax.nn.relu(hidden + bias_first[None, None, :, None]).astype(BF16)
    row_index = lax.axis_index("coil") * rows - 1 + jnp.arange(rows + 2)
    slice_index = lax.axis_index("sect") * slices - 1 + jnp.arange(slices + 2)
    row_valid = (row_index >= 0) & (row_index < height)
    slice_valid = (slice_index >= 0) & (slice_index < lax.axis_size("sect") * slices)
    inside = row_valid[:, None] & slice_valid[None, :]
    hidden = jnp.where(inside[:, :, None, None], hidden, jnp.zeros_like(hidden))
    hidden = jnp.pad(hidden, ((0, 0), (0, 0), (0, 0), (1, 1)))
    taps = jnp.einsum("tc,rscw->rstw", conv_second, hidden, preferred_element_type=F32)
    return tap_sum(taps, rows, slices, breadth) + bias_second[None, None, :, None]


def per_device(measured, coil_maps, sampling, conv_first, bias_first, conv_second, bias_second):
    height, coils_here, slices_here, _, breadth = coil_maps.shape
    count = lax.axis_size("coil")
    rows = height // count
    mask = sampling.astype(F32)

    def exchange(x):
        split = x.astype(BF16).reshape((count, rows) + x.shape[1:])
        return lax.all_to_all(split, "coil", 0, 0, tiled=True)

    row_cos, row_sin = dft_tables(height)
    col_cos, col_sin = dft_tables(breadth)
    row_table = jnp.asarray(np.stack([row_cos, row_sin]) / math.sqrt(height), F32)
    col_table = jnp.asarray(
        np.block([[col_cos, col_sin], [-col_sin, col_cos]]) / math.sqrt(breadth), F32
    ).reshape(2, breadth, 2, breadth)

    spread = jnp.einsum("tkh,kcsqw->tcsqwh", row_table, measured, precision=HIGH)
    spread = jnp.stack(
        [spread[0, :, :, 0] - spread[1, :, :, 1], spread[0, :, :, 1] + spread[1, :, :, 0]], axis=2
    )
    spread = spread * mask[None, :, None, :, None]
    inverse = jnp.einsum("qwpv,csqwh->csphv", col_table, spread, precision=HIGH)
    maps = jnp.transpose(coil_maps, (1, 2, 3, 0, 4))
    part_re = jnp.sum(maps[:, :, 0] * inverse[:, :, 0] + maps[:, :, 1] * inverse[:, :, 1], axis=0)
    part_im = jnp.sum(maps[:, :, 0] * inverse[:, :, 1] - maps[:, :, 1] * inverse[:, :, 0], axis=0)
    partial = jnp.transpose(jnp.stack([part_re, part_im], axis=1), (2, 0, 1, 3))
    first = jnp.sum(exchange(partial).astype(F32), axis=0)
    near = exchange(coil_maps).astype(F32)
    near_re, near_im = near[..., 0, :], near[..., 1, :]

    angle = jnp.asarray(np.stack([col_cos, col_sin]), F32)
    both = jnp.einsum("sl,alj,blv->absjv", mask, angle, angle, precision=HIGH) / breadth
    project_re = both[0, 0] + both[1, 1]
    project_im = both[0, 1] - both[1, 0]
    project = jnp.stack(
        [jnp.stack([project_re, project_im], 2), jnp.stack([-project_im, project_re], 2)]
    )

    image = first
    for _ in range(ITERS):
        image_re, image_im = image[:, :, 0], image[:, :, 1]
        product = jnp.stack(
            [near_re * image_re[:, None] - near_im * image_im[:, None],
             near_re * image_im[:, None] + near_im * image_re[:, None]]
        )
        spun = jnp.einsum("qnrcsj,qsjpv->pnrcsv", product, project, precision=HIGH)
        normal_re = jnp.sum(near_re * spun[0] + near_im * spun[1], axis=(0, 2))
        normal_im = jnp.sum(near_re * spun[1] - near_im * spun[0], axis=(0, 2))
        normal = jnp.stack([normal_re, normal_im], axis=2)
        damped = image - STEP * (normal - first)
        image = damped + regularize(
            damped, height, conv_first, bias_first, conv_second, bias_second
        )
    return image


def bf16_pair(table):
    high = table.astype(BF16)
    return high, (table - high.astype(np.float64)).astype(BF16)


def split3(x):
    high = x.astype(BF16)
    return high, (x - high.astype(F32)).astype(BF16)


def dot(x, y):
    return jnp.dot(x, y, preferred_element_type=F32)


def dot3(x, y):
    return dot(x[0], y[0]) + dot(x[1], y[0]) + dot(x[0], y[1])


def vmem(count):
    return [pl.BlockSpec(memory_space=pltpu.VMEM)] * count


def column_of(row):
    shape = (row.shape[1], row.shape[1])
    diagonal = lax.broadcasted_iota(jnp.int32, shape, 0) == lax.broadcasted_iota(jnp.int32, shape, 1)
    return jnp.sum(jnp.where(diagonal, jnp.broadcast_to(row, shape), 0.0), axis=1, keepdims=True)


def block_of(coil, sect):
    return 2 * coil + (sect + coil) % 2


def back_project(data, maps, keep, row_ref, column_ref, between):
    height = data[0].shape[1]
    breadth = data[0].shape[0] // 2
    spreads, rights = [], []
    for value in data:
        high, low = split3(value)
        spreads.append(dot(jnp.concatenate([high, low, high], axis=1), row_ref[...]))
    between[0]()
    for spread in spreads:
        real, imag = spread[:breadth], spread[breadth:]
        pieces = [
            (real[:, :height] - imag[:, height:]) * keep, (imag[:, :height] + real[:, height:]) * keep,
        ]
        high, low = split3(jnp.concatenate(pieces, axis=1))
        rights.append(jnp.concatenate([high, low, high], axis=0))
    mixes = [dot(column_ref[...], x) for x in rights]
    between[1]()
    total_re, total_im = 0.0, 0.0
    for mixed, read in zip(mixes, maps):
        inv_re = mixed[:breadth, :height] - mixed[breadth:, height:]
        inv_im = mixed[breadth:, :height] + mixed[:breadth, height:]
        map_re, map_im = read(0), read(1)
        total_re += map_re * inv_re + map_im * inv_im
        total_im += map_re * inv_im - map_im * inv_re
    return total_re, total_im


def own_slice():
    return lax.axis_index("coil") % 2


def kept_columns(mask_ref, here):
    mask = mask_ref[...].astype(F32)
    return column_of(jnp.where(here == 0, mask[:1], mask[1:]))


def parts_of(maps_ref, c, s):
    breadth = maps_ref.shape[2] // 2
    return lambda q: maps_ref[c, s, q * breadth : (q + 1) * breadth]


def first_kernel(
    data_far, maps_far, mask_far, row_far, column_far,
    give_ref, data_ref, maps_ref, mask_ref, row_ref, column_ref, other_ref, sems,
):
    coils = data_far.shape[0]
    here = own_slice()
    there = 1 - here
    plan = [(mask_far, mask_ref), (row_far, row_ref)]
    plan += [(data_far.at[c, there], other_ref.at[c]) for c in range(coils)]
    plan += [(column_far, column_ref)]
    plan += [(maps_far.at[c, there], maps_ref.at[c, there]) for c in range(coils)]
    plan += [(data_far.at[c, here], data_ref.at[c]) for c in range(coils)]
    plan += [(maps_far.at[c, here], maps_ref.at[c, here]) for c in range(coils)]
    copies = [pltpu.make_async_copy(x, y, sems.at[i]) for i, (x, y) in enumerate(plan)]
    for copy in copies:
        copy.start()
    copies[0].wait()
    keep = kept_columns(mask_ref, there)
    for copy in copies[1 : 2 + coils]:
        copy.wait()

    def rest():
        for copy in copies[2 + coils :]:
            copy.wait()

    totals = back_project(
        [other_ref[c] for c in range(coils)], [parts_of(maps_ref, c, there) for c in range(coils)],
        keep, row_ref, column_ref, (rest, lambda: None),
    )
    breadth = totals[0].shape[0]
    for q in range(2):
        give_ref[q * breadth : (q + 1) * breadth] = totals[q]


def own_kernel(data_ref, maps_ref, mask_ref, row_ref, column_ref, send_ref, total_ref, out_copy, sems):
    coils, slices, double, height = maps_ref.shape
    breadth, wide = double // 2, slices * double // 2
    here = own_slice()
    sends = []

    def emit(c):
        turned = [
            jnp.concatenate([parts_of(maps_ref, c, s)(q) for s in range(slices)], axis=0)
            .T.reshape(height // 8, 8, wide)
            for q in range(2)
        ]
        both = jnp.concatenate(turned, axis=1).astype(BF16)
        for p in range(height // 8):
            out_copy[c, p] = both[block_of(p // 2, p % 2)]
        rows = send_ref.at[:, 16 * c : 16 * c + 16, :]
        sends.append(pltpu.make_async_copy(out_copy.at[c], rows, sems.at[c]))
        sends[-1].start()

    totals = back_project(
        [data_ref[c] for c in range(coils)], [parts_of(maps_ref, c, here) for c in range(coils)],
        kept_columns(mask_ref, here), row_ref, column_ref, [lambda c=c: emit(c) for c in range(2)],
    )
    for q in range(2):
        total_ref[q * breadth : (q + 1) * breadth] = totals[q]
    for copy in sends:
        copy.wait()


def sum_kernel(total_ref, got_ref, mask_ref, old_ref, send_ref, mask_out_ref, out_copy, sem):
    double, height = total_ref.shape
    turned = (total_ref[...] + got_ref[...]).T.reshape(height // 8, 8, double).astype(BF16)
    for p in range(height // 8):
        out_copy[p] = turned[block_of(p // 2, p % 2)]
    first = send_ref.shape[1] - 8
    copy = pltpu.make_async_copy(out_copy, send_ref.at[:, first : first + 8, :], sem)
    copy.start()
    mask_out_ref[...] = mask_ref[...].astype(F32).astype(BF16)
    copy.wait()


def table_kernel(
    own_ref, other_ref, angle_ref, first_ref, bias_ref, second_ref, pick_first_ref, pick_second_ref, place_ref,
    project_ref, first_out_ref, second_out_ref,
):
    slices, breadth = own_ref.shape
    wide = slices * breadth
    here = lax.axis_index("sect")
    angle = angle_ref[...]
    swapped = jnp.concatenate([angle[:, wide:], -angle[:, :wide]], axis=1)
    cosine, sine = angle[:, :breadth], angle[:, wide : wide + breadth]
    angle, swapped = split3(angle), split3(swapped)
    for t in range(project_ref.shape[0]):
        mask = jnp.where(here == t, own_ref[...].astype(F32), other_ref[...].astype(F32))
        for s in range(slices):
            row = mask[s : s + 1]
            block = dot3(split3(cosine * row), angle) + dot3(split3(sine * row), swapped)
            if s:
                block = pltpu.roll(block, s * breadth, 1)
            rows = slice(s * breadth, (s + 1) * breadth)
            project_ref[t, rows] = block.astype(BF16)
            rows = slice(wide + s * breadth, wide + (s + 1) * breadth)
            project_ref[t, rows] = jnp.concatenate([-block[:, wide:], block[:, :wide]], axis=1).astype(BF16)

    groups, _, depth = pick_first_ref.shape
    features = first_ref.shape[1]
    bias = column_of(bias_ref[...])
    parts = []
    for _ in range(3):
        parts.append(bias.astype(BF16).astype(F32))
        bias = bias - parts[-1]
    lane = lax.broadcasted_iota(jnp.int32, (features, depth), 1)
    second = 0.0
    for s in range(groups):
        block = lax.dot_general(
            first_ref[...], pick_first_ref[s], (((0,), (0,)), ((), ())), preferred_element_type=F32
        )
        for i in range(3):
            block = jnp.where(lane == depth - 8 + i, parts[i], block)
        first_out_ref[s * features : (s + 1) * features] = block.astype(BF16)
        second += dot(dot(pick_second_ref[s], second_ref[...]).astype(BF16), place_ref[s])
    second_out_ref[...] = second.astype(BF16)


def apply_data_term(near_ref, project_ref, image, start, left_ref, spun_ref, breadth):
    result = []
    coils, groups = near_ref.shape[0], near_ref.shape[1]
    wide = near_ref.shape[3]
    for t in range(groups):
        image_re, image_im = image[t][:8], image[t][8:]

        def spread(i, carry, t=t, image_re=image_re, image_im=image_im):
            reals, imags = [], []
            for c in range(2):
                maps = near_ref[i, t, 16 * c : 16 * c + 16, :].astype(F32)
                map_re, map_im = maps[:8], maps[8:]
                reals.append(map_re * image_re - map_im * image_im)
                imags.append(map_re * image_im + map_im * image_re)
            rows = pl.ds(pl.multiple_of(16 * i, 16), 16)
            left_ref[rows, :wide] = jnp.concatenate(reals, axis=0).astype(BF16)
            left_ref[rows, wide:] = jnp.concatenate(imags, axis=0).astype(BF16)
            return carry

        lax.fori_loop(0, coils, spread, 0, unroll=4)
        spun_ref[...] = dot(left_ref[...], project_ref[t])

        def gather(i, carry, t=t):
            sum_re, sum_im = carry
            for c in range(2):
                maps = near_ref[i, t, 16 * c : 16 * c + 16, :].astype(F32)
                map_re, map_im = maps[:8], maps[8:]
                rows = pl.ds(pl.multiple_of(16 * i + 8 * c, 8), 8)
                spun_re, spun_im = spun_ref[rows, :wide], spun_ref[rows, wide:]
                sum_re += map_re * spun_re + map_im * spun_im
                sum_im += map_re * spun_im - map_im * spun_re
            return sum_re, sum_im

        zero = jnp.zeros((8, wide), F32)
        normal = jnp.concatenate(lax.fori_loop(0, coils, gather, (zero, zero), unroll=4), axis=0)
        result.append((normal, t))
    return [image[t] - STEP * (normal * (1.0 / breadth) - start[t]) for normal, t in result]


def to_rows(damped, out_ref, flip_ref, breadth):
    per_group = damped[0].shape[1] // breadth
    wide = damped[0].shape[1]
    lanes = lax.broadcasted_iota(jnp.int32, (16, LANES), 1)
    for t, value in enumerate(damped):
        for s in range(per_group):
            moved = value if s == 0 else pltpu.roll(value, wide - s * breadth, 1)
            moved = jnp.where(lanes < breadth, moved[:, :LANES], 0.0)
            for q in range(2):
                place = (t * per_group + s) * 2 + q
                for j in range(2):
                    part = moved[8 * q : 8 * q + 8, 128 * j : 128 * j + 128]
                    flip_ref[pl.ds(64 * j + place, 8, stride=8), :] = part
    for j in range(2):
        out_ref[:, 128 * j : 128 * j + 128] = flip_ref[64 * j : 64 * j + 64]


def from_rows(flip_ref, groups, per_group, breadth):
    wide = per_group * breadth
    result = []
    for t in range(groups):
        parts = []
        for q in range(2):
            value = jnp.zeros((8, wide), F32)
            for s in range(per_group):
                place = (t * per_group + s) * 2 + q
                halves = [flip_ref[pl.ds(64 * j + place, 8, stride=8), :] for j in range(2)]
                piece = jnp.concatenate(halves + [jnp.zeros((8, wide - LANES), F32)], axis=1)
                value += piece if s == 0 else pltpu.roll(piece, s * breadth, 1)
            parts.append(value)
        result.append(jnp.concatenate(parts, axis=0))
    return result


def position_of():
    return block_of(lax.axis_index("coil"), lax.axis_index("sect"))


def write_edges(rows_ref, inner_ref, outer_ref):
    odd = position_of() % 2 == 1
    low, high = rows_ref[:16], rows_ref[48:64]
    inner_ref[...] = jnp.where(odd, low, high).astype(BF16)
    outer_ref[...] = jnp.where(odd, high, low).astype(BF16)


def keep_close(*arrays):
    return [pltpu.with_memory_space_constraint(x, pltpu.VMEM) for x in arrays]


def second_kernel(
    near_ref, project_ref, rows_ref, inner_ref, outer_ref, start_ref,
    flip_ref, left_ref, spun_ref, *, breadth,
):
    coils, groups, _, wide = near_ref.shape
    start = []
    first = lax.broadcasted_iota(jnp.int32, (8, wide), 1) < breadth
    for t in range(groups):
        def add(i, totals, t=t):
            return tuple(x + near_ref[2 * i + s, t, 32:40, :].astype(F32) for s, x in enumerate(totals))

        zero = jnp.zeros((8, wide), F32)
        low, high = lax.fori_loop(0, coils // 2, add, (zero, zero), unroll=4)
        parts = [
            jnp.where(first, low, pltpu.roll(high, breadth, 1)),
            jnp.where(first, pltpu.roll(low, breadth, 1), high),
        ]
        start.append(jnp.concatenate(parts, axis=0))
        start_ref[t] = start[t]
    damped = apply_data_term(near_ref, project_ref, start, start, left_ref, spun_ref, breadth)
    to_rows(damped, rows_ref, flip_ref, breadth)
    write_edges(rows_ref, inner_ref, outer_ref)


def convolve(values, first_ref, second_ref, bias_ref, top, bottom, shift_ref, hidden_ref, breadth):
    count = len(values)
    for h, value in enumerate(values):
        shift_ref[24 * h : 24 * h + 8] = pltpu.roll(value, 1, 1)
        shift_ref[24 * h + 8 : 24 * h + 16] = value
        shift_ref[24 * h + 16 : 24 * h + 24] = pltpu.roll(value, LANES - 1, 1)
    ones = jnp.ones((8, LANES), F32)
    for g in range(count - 2):
        columns = jnp.concatenate([shift_ref[24 * g : 24 * g + 72], ones], axis=0).astype(BF16)
        hidden = dot(first_ref[...], columns).astype(BF16)
        hidden_ref[g] = jnp.maximum(hidden, jnp.zeros_like(hidden))
    lanes = lax.broadcasted_iota(jnp.int32, (1, LANES), 1)
    taps = []
    for g in range(count - 2):
        inside = lanes < breadth
        if g == 0:
            inside = inside & top
        if g == count - 3:
            inside = inside & bottom
        taps.append(jnp.where(inside, dot(second_ref[...], hidden_ref[g]), 0.0))
    odd = lax.broadcasted_iota(jnp.int32, (8, LANES), 0) % 2 == 1
    bias = jnp.where(odd, bias_ref[1], bias_ref[0])
    updates = []
    for h in range(count - 4):
        total = taps[h][:24] + taps[h + 1][24:48] + taps[h + 2][48:]
        update = pltpu.roll(total[:8], 1, 1) + total[8:16] + pltpu.roll(total[16:], LANES - 1, 1)
        updates.append(jnp.where(lanes < breadth, update + bias, 0.0))
    return updates


def edge_rows(first, second):
    value = jnp.where(position_of() % 2 == 1, first.astype(F32), second.astype(F32))
    return [value[:8], value[8:]]


def regularized(
    rows_ref, inner_ref, outer_ref, first_ref, second_ref, bias_ref, shift_ref, hidden_ref, breadth
):
    inner, outer = inner_ref[...], outer_ref[...]
    own = [rows_ref[8 * h : 8 * h + 8] for h in range(8)]
    values = edge_rows(inner, outer) + own + edge_rows(outer, inner)
    last = 2 * lax.axis_size("coil") - 1
    updates = convolve(
        values, first_ref, second_ref, bias_ref, position_of() > 0, position_of() < last,
        shift_ref, hidden_ref, breadth,
    )
    return own, updates


def third_kernel(
    rows_ref, inner_ref, outer_ref, first_ref, second_ref, bias_ref, near_ref, project_ref, start_ref,
    out_ref, inner_out_ref, outer_out_ref,
    shift_ref, hidden_ref, flip_ref, left_ref, spun_ref, *, breadth,
):
    groups, _, wide = start_ref.shape
    own, updates = regularized(
        rows_ref, inner_ref, outer_ref, first_ref, second_ref, bias_ref, shift_ref, hidden_ref, breadth
    )
    for h in range(8):
        image = own[h] + updates[h]
        for j in range(2):
            flip_ref[64 * j + 8 * h : 64 * j + 8 * h + 8] = image[:, 128 * j : 128 * j + 128]
    image = from_rows(flip_ref, groups, wide // breadth, breadth)
    start = [start_ref[t] for t in range(groups)]
    damped = apply_data_term(near_ref, project_ref, image, start, left_ref, spun_ref, breadth)
    to_rows(damped, out_ref, flip_ref, breadth)
    write_edges(out_ref, inner_out_ref, outer_out_ref)


def last_kernel(
    rows_ref, inner_ref, outer_ref, first_ref, second_ref, bias_ref, keep_ref, give_ref,
    shift_ref, hidden_ref, *, breadth,
):
    own, updates = regularized(
        rows_ref, inner_ref, outer_ref, first_ref, second_ref, bias_ref, shift_ref, hidden_ref, breadth
    )
    upper = lax.axis_index("sect") == 0
    for h in range(8):
        image = (own[h] + updates[h])[:, :breadth]
        keep, give = jnp.where(upper, image[:4], image[4:]), jnp.where(upper, image[4:], image[:4])
        for s in range(2):
            keep_ref[h, s] = keep[2 * s : 2 * s + 2]
            give_ref[h, s] = give[2 * s : 2 * s + 2]


def join_kernel(keep_ref, got_ref, out_ref):
    odd = position_of() % 2 == 1
    keep, got = keep_ref[...], got_ref[...]
    out_ref[:8] = jnp.where(odd, got, keep)
    out_ref[8:] = jnp.where(odd, keep, got)


def fast_device(measured, coil_maps, sampling, conv_first, bias_first, conv_second, bias_second):
    height, coils_here, slices_here, _, breadth = coil_maps.shape
    ranks, sects = lax.axis_size("coil"), lax.axis_size("sect")
    count = ranks * sects
    slices = slices_here * sects
    wide = slices_here * breadth
    features = conv_first.shape[0]
    both = ("coil", "sect")
    f32 = lambda *dims: jax.ShapeDtypeStruct(dims, F32)
    bf16 = lambda *dims: jax.ShapeDtypeStruct(dims, BF16)

    row_cos, row_sin = dft_tables(height)
    col_cos, col_sin = dft_tables(breadth)
    row_high, row_low = bf16_pair(np.concatenate([row_cos, row_sin], axis=1) / math.sqrt(height))
    column_high, column_low = bf16_pair(np.concatenate([col_cos, col_sin], axis=0) / math.sqrt(breadth))
    row_table = jnp.asarray(np.concatenate([row_high, row_high, row_low], axis=0))
    column_table = jnp.asarray(np.concatenate([column_high, column_high, column_low], axis=1))
    by_coil = lambda x: jnp.transpose(x, (1, 2, 3, 4, 0)).reshape(coils_here, slices_here, 2 * breadth, height)
    block_rows = 16 * coils_here + 8
    far = (by_coil(measured), by_coil(coil_maps), sampling, row_table, column_table)
    double = 2 * breadth
    anywhere = pl.BlockSpec(memory_space=pl.ANY)
    roomy = pltpu.CompilerParams(vmem_limit_bytes=40 << 20)
    give, *fetched = pl.pallas_call(
        first_kernel, compiler_params=roomy,
        in_specs=[anywhere] * 5, out_specs=vmem(6),
        out_shape=[
            f32(double, height), pltpu.VMEM((coils_here, double, height), F32),
            *[pltpu.VMEM(x.shape, x.dtype) for x in far[1:]],
        ],
        scratch_shapes=[
            pltpu.VMEM((coils_here, double, height), F32), pltpu.SemaphoreType.DMA((3 + 4 * coils_here,)),
        ],
    )(*[pltpu.with_memory_space_constraint(x, pltpu.HBM) for x in far])
    got = lax.ppermute(give, "coil", [(i, i ^ 1) for i in range(ranks)])
    send, total = pl.pallas_call(
        own_kernel, compiler_params=roomy,
        in_specs=vmem(5), out_specs=[anywhere] + vmem(1),
        out_shape=[bf16(count, block_rows, wide), pltpu.VMEM((double, height), F32)],
        scratch_shapes=[pltpu.VMEM((coils_here, count, 16, wide), BF16), pltpu.SemaphoreType.DMA((coils_here,))],
    )(*keep_close(*fetched))
    send, mask = pl.pallas_call(
        sum_kernel, compiler_params=MODEST,
        in_specs=vmem(3) + [anywhere], out_specs=[anywhere] + vmem(1),
        out_shape=[bf16(count, block_rows, wide), bf16(slices_here, breadth)],
        input_output_aliases={3: 0},
        scratch_shapes=[pltpu.VMEM((count, 8, wide), BF16), pltpu.SemaphoreType.DMA],
    )(*keep_close(total, got, fetched[2]), send)
    near = lax.all_to_all(send, both, 0, 0, tiled=True).reshape(ranks, sects, block_rows, wide)

    other = lax.ppermute(mask, "sect", [(0, 1), (1, 0)])
    blank = np.zeros((breadth, wide - breadth))
    angle = np.concatenate([col_cos, blank, col_sin, blank], axis=1).astype(np.float32)
    span = 18 * slices
    pick_first = np.zeros((slices, 54, span + 8))
    pick_second = np.zeros((slices, span, 54))
    for a, b, e, q, s in np.ndindex(3, 3, 3, 2, slices):
        tap = 2 * (9 * a + 3 * b + e) + q
        if 0 <= s + b - 1 < slices:
            pick_first[s, tap, ((a * 3 + e) * slices + s + b - 1) * 2 + q] = 1.0
            pick_second[s + b - 1, ((a * 3 + e) * slices + s) * 2 + q, tap] = 1.0
    place = np.eye(slices * features).reshape(slices, features, slices * features)
    project, matrix_first, matrix_second = pl.pallas_call(
        table_kernel,
        compiler_params=MODEST,
        in_specs=vmem(9), out_specs=vmem(3),
        out_shape=[
            pltpu.VMEM(dims, BF16)
            for dims in (
                (sects, 2 * wide, 2 * wide), (slices * features, span + 8), (span, slices * features),
            )
        ],
    )(
        mask, other, jnp.asarray(angle), conv_first.T, bias_first.reshape(1, features), conv_second,
        *[jnp.asarray(x.astype(BF16)) for x in (pick_first, pick_second, place)],
    )
    weights = (*keep_close(matrix_first, matrix_second), bias_second)
    weight_specs = vmem(2) + [pl.BlockSpec(memory_space=pltpu.SMEM)]

    owner = {block_of(i, y): 2 * i + y for i in range(ranks) for y in range(2)}
    near_pairs = []
    for block in range(1, count - 1, 2):
        near_pairs += [(owner[block], owner[block + 1]), (owner[block + 1], owner[block])]
    swap = lambda x: lax.ppermute(x, "sect", [(0, 1), (1, 0)])

    edge = 4 * slices
    work = [
        pltpu.VMEM((32 * slices, 128), F32),
        pltpu.VMEM((16 * ranks, 2 * wide), BF16), pltpu.VMEM((16 * ranks, 2 * wide), F32),
    ]

    def room(rows):
        return [
            pltpu.VMEM(((rows + 4) * 6 * slices, LANES), F32),
            pltpu.VMEM((rows + 2, slices * features, LANES), BF16),
        ]

    row_shapes = [f32(16 * slices, LANES), bf16(edge, LANES), bf16(edge, LANES)]
    rows, inner, outer, start = pl.pallas_call(
        functools.partial(second_kernel, breadth=breadth),
        compiler_params=MODEST,
        in_specs=vmem(2), out_specs=vmem(4),
        out_shape=row_shapes + [pltpu.VMEM((sects, 16, wide), F32)], scratch_shapes=work,
    )(*keep_close(near, project))
    for _ in range(ITERS - 1):
        rows, inner, outer = pl.pallas_call(
            functools.partial(third_kernel, breadth=breadth),
            compiler_params=MODEST,
            in_specs=vmem(3) + weight_specs + vmem(3), out_specs=vmem(3), out_shape=row_shapes,
            scratch_shapes=room(8) + work,
        )(*keep_close(rows, swap(inner), lax.ppermute(outer, both, near_pairs)), *weights, *keep_close(near, project, start))
    piece = f32(8, slices_here, 2, breadth)
    keep, give = pl.pallas_call(
        functools.partial(last_kernel, breadth=breadth),
        compiler_params=MODEST,
        in_specs=vmem(3) + weight_specs, out_specs=vmem(2), out_shape=[piece, piece],
        scratch_shapes=room(8),
    )(*keep_close(rows, swap(inner), lax.ppermute(outer, both, near_pairs)), *weights)
    return pl.pallas_call(
        join_kernel, compiler_params=MODEST, in_specs=vmem(2), out_specs=vmem(1)[0],
        out_shape=f32(16, slices_here, 2, breadth),
    )(*keep_close(keep, swap(give)))


def per_device_any(measured, coil_maps, *rest):
    height, coils_here, slices_here, _, breadth = coil_maps.shape
    ranks, sects = lax.axis_size("coil"), lax.axis_size("sect")
    fits = (
        sects == 2 and slices_here == 2 and coils_here == 2 and height == 8 * ranks * sects
        and 2 * breadth % 128 == 0 and 128 < breadth < LANES and breadth % 16 == 0
    )
    return (fast_device if fits else per_device)(measured, coil_maps, *rest)


def solution(mesh):
    coil_spec = P(None, "coil", "sect", None, None)
    in_specs = (coil_spec, coil_spec, P("sect", None), P(), P(), P(), P())
    return jax.shard_map(
        per_device_any,
        mesh=mesh,
        in_specs=in_specs,
        out_specs=P("coil", "sect", None, None),
        check_vma=False,
    )
```

```python
import functools
import math

import jax
import jax.numpy as jnp
import numpy as np
from jax import lax
from jax.experimental import pallas as pl
from jax.experimental.pallas import tpu as pltpu
from jax.sharding import PartitionSpec as P

ITERS = 2
STEP = 0.5
F32 = jnp.float32
BF16 = jnp.bfloat16
HIGH = lax.Precision.HIGH
LANES = 256
MODEST = pltpu.CompilerParams(vmem_limit_bytes=24 << 20)


def dft_tables(length):
    index = np.arange(length)
    angle = (index[:, None] * index[None, :] % length) * (2.0 * math.pi / length)
    return np.cos(angle), np.sin(angle)


def with_halo(x, sides, width):
    for axis, dim in sides:
        count, length = lax.axis_size(axis), x.shape[dim]
        up = [(i, i + 1) for i in range(count - 1)]
        down = [(j, i) for i, j in up]
        before = lax.ppermute(lax.slice_in_dim(x, length - width, length, axis=dim), axis, up)
        after = lax.ppermute(lax.slice_in_dim(x, 0, width, axis=dim), axis, down)
        x = jnp.concatenate([before, x, after], axis=dim)
    return x


def stack_taps(padded, rows, slices, breadth):
    return jnp.concatenate(
        [
            padded[a : a + rows, b : b + slices, :, e : e + breadth]
            for a in range(3)
            for b in range(3)
            for e in range(3)
        ],
        axis=2,
    )


def tap_sum(taps, rows, slices, breadth):
    result = jnp.zeros((rows, slices, 2, breadth), F32)
    for place in range(27):
        a, b, e = place // 9, place // 3 % 3, place % 3
        result += taps[a : a + rows, b : b + slices, 2 * place : 2 * place + 2, e : e + breadth]
    return result


def regularize(damped, height, conv_first, bias_first, conv_second, bias_second):
    rows, slices, _, breadth = damped.shape
    extended = with_halo(damped.astype(BF16), (("coil", 0), ("sect", 1)), 2)
    padded = jnp.pad(extended, ((0, 0), (0, 0), (0, 0), (1, 1)))
    columns = stack_taps(padded, rows + 2, slices + 2, breadth)
    hidden = jnp.einsum("oc,rscw->rsow", conv_first, columns, preferred_element_type=F32)
    hidden = jax.nn.relu(hidden + bias_first[None, None, :, None]).astype(BF16)
    row_index = lax.axis_index("coil") * rows - 1 + jnp.arange(rows + 2)
    slice_index = lax.axis_index("sect") * slices - 1 + jnp.arange(slices + 2)
    row_valid = (row_index >= 0) & (row_index < height)
    slice_valid = (slice_index >= 0) & (slice_index < lax.axis_size("sect") * slices)
    inside = row_valid[:, None] & slice_valid[None, :]
    hidden = jnp.where(inside[:, :, None, None], hidden, jnp.zeros_like(hidden))
    hidden = jnp.pad(hidden, ((0, 0), (0, 0), (0, 0), (1, 1)))
    taps = jnp.einsum("tc,rscw->rstw", conv_second, hidden, preferred_element_type=F32)
    return tap_sum(taps, rows, slices, breadth) + bias_second[None, None, :, None]


def per_device(measured, coil_maps, sampling, conv_first, bias_first, conv_second, bias_second):
    height, coils_here, slices_here, _, breadth = coil_maps.shape
    count = lax.axis_size("coil")
    rows = height // count
    mask = sampling.astype(F32)

    def exchange(x):
        split = x.astype(BF16).reshape((count, rows) + x.shape[1:])
        return lax.all_to_all(split, "coil", 0, 0, tiled=True)

    row_cos, row_sin = dft_tables(height)
    col_cos, col_sin = dft_tables(breadth)
    row_table = jnp.asarray(np.stack([row_cos, row_sin]) / math.sqrt(height), F32)
    col_table = jnp.asarray(
        np.block([[col_cos, col_sin], [-col_sin, col_cos]]) / math.sqrt(breadth), F32
    ).reshape(2, breadth, 2, breadth)

    spread = jnp.einsum("tkh,kcsqw->tcsqwh", row_table, measured, precision=HIGH)
    spread = jnp.stack(
        [spread[0, :, :, 0] - spread[1, :, :, 1], spread[0, :, :, 1] + spread[1, :, :, 0]], axis=2
    )
    spread = spread * mask[None, :, None, :, None]
    inverse = jnp.einsum("qwpv,csqwh->csphv", col_table, spread, precision=HIGH)
    maps = jnp.transpose(coil_maps, (1, 2, 3, 0, 4))
    part_re = jnp.sum(maps[:, :, 0] * inverse[:, :, 0] + maps[:, :, 1] * inverse[:, :, 1], axis=0)
    part_im = jnp.sum(maps[:, :, 0] * inverse[:, :, 1] - maps[:, :, 1] * inverse[:, :, 0], axis=0)
    partial = jnp.transpose(jnp.stack([part_re, part_im], axis=1), (2, 0, 1, 3))
    first = jnp.sum(exchange(partial).astype(F32), axis=0)
    near = exchange(coil_maps).astype(F32)
    near_re, near_im = near[..., 0, :], near[..., 1, :]

    angle = jnp.asarray(np.stack([col_cos, col_sin]), F32)
    both = jnp.einsum("sl,alj,blv->absjv", mask, angle, angle, precision=HIGH) / breadth
    project_re = both[0, 0] + both[1, 1]
    project_im = both[0, 1] - both[1, 0]
    project = jnp.stack(
        [jnp.stack([project_re, project_im], 2), jnp.stack([-project_im, project_re], 2)]
    )

    image = first
    for _ in range(ITERS):
        image_re, image_im = image[:, :, 0], image[:, :, 1]
        product = jnp.stack(
            [near_re * image_re[:, None] - near_im * image_im[:, None],
             near_re * image_im[:, None] + near_im * image_re[:, None]]
        )
        spun = jnp.einsum("qnrcsj,qsjpv->pnrcsv", product, project, precision=HIGH)
        normal_re = jnp.sum(near_re * spun[0] + near_im * spun[1], axis=(0, 2))
        normal_im = jnp.sum(near_re * spun[1] - near_im * spun[0], axis=(0, 2))
        normal = jnp.stack([normal_re, normal_im], axis=2)
        damped = image - STEP * (normal - first)
        image = damped + regularize(
            damped, height, conv_first, bias_first, conv_second, bias_second
        )
    return image


def bf16_pair(table):
    high = table.astype(BF16)
    return high, (table - high.astype(np.float64)).astype(BF16)


def split3(x):
    high = x.astype(BF16)
    return high, (x - high.astype(F32)).astype(BF16)


def dot(x, y):
    return jnp.dot(x, y, preferred_element_type=F32)


def dot3(x, y):
    return dot(x[0], y[0]) + dot(x[1], y[0]) + dot(x[0], y[1])


def vmem(count):
    return [pl.BlockSpec(memory_space=pltpu.VMEM)] * count


def column_of(row):
    shape = (row.shape[1], row.shape[1])
    diagonal = lax.broadcasted_iota(jnp.int32, shape, 0) == lax.broadcasted_iota(jnp.int32, shape, 1)
    return jnp.sum(jnp.where(diagonal, jnp.broadcast_to(row, shape), 0.0), axis=1, keepdims=True)


def block_of(coil, sect):
    return 2 * coil + (sect + coil) % 2


def back_project(data, maps, keep, row_ref, column_ref, between):
    height = data[0].shape[1]
    breadth = data[0].shape[0] // 2
    spreads, rights = [], []
    for value in data:
        high, low = split3(value)
        spreads.append(dot(jnp.concatenate([high, low, high], axis=1), row_ref[...]))
    between[0]()
    for spread in spreads:
        real, imag = spread[:breadth], spread[breadth:]
        pieces = [
            (real[:, :height] - imag[:, height:]) * keep, (imag[:, :height] + real[:, height:]) * keep,
        ]
        high, low = split3(jnp.concatenate(pieces, axis=1))
        rights.append(jnp.concatenate([high, low, high], axis=0))
    mixes = [dot(column_ref[...], x) for x in rights]
    between[1]()
    total_re, total_im = 0.0, 0.0
    for mixed, read in zip(mixes, maps):
        inv_re = mixed[:breadth, :height] - mixed[breadth:, height:]
        inv_im = mixed[breadth:, :height] + mixed[:breadth, height:]
        map_re, map_im = read(0), read(1)
        total_re += map_re * inv_re + map_im * inv_im
        total_im += map_re * inv_im - map_im * inv_re
    return total_re, total_im


def own_slice():
    return lax.axis_index("coil") % 2


def kept_columns(mask_ref, here):
    mask = mask_ref[...].astype(F32)
    return column_of(jnp.where(here == 0, mask[:1], mask[1:]))


def parts_of(maps_ref, c, s):
    breadth = maps_ref.shape[2] // 2
    return lambda q: maps_ref[c, s, q * breadth : (q + 1) * breadth]


def first_kernel(
    data_far, maps_far, mask_far, row_far, column_far,
    give_ref, data_ref, maps_ref, mask_ref, row_ref, column_ref, other_ref, sems,
):
    coils = data_far.shape[0]
    here = own_slice()
    there = 1 - here
    plan = [(mask_far, mask_ref), (row_far, row_ref)]
    plan += [(data_far.at[c, there], other_ref.at[c]) for c in range(coils)]
    plan += [(column_far, column_ref)]
    plan += [(maps_far.at[c, there], maps_ref.at[c, there]) for c in range(coils)]
    plan += [(data_far.at[c, here], data_ref.at[c]) for c in range(coils)]
    plan += [(maps_far.at[c, here], maps_ref.at[c, here]) for c in range(coils)]
    copies = [pltpu.make_async_copy(x, y, sems.at[i]) for i, (x, y) in enumerate(plan)]
    for copy in copies:
        copy.start()
    copies[0].wait()
    keep = kept_columns(mask_ref, there)
    for copy in copies[1 : 2 + coils]:
        copy.wait()

    def rest():
        for copy in copies[2 + coils :]:
            copy.wait()

    totals = back_project(
        [other_ref[c] for c in range(coils)], [parts_of(maps_ref, c, there) for c in range(coils)],
        keep, row_ref, column_ref, (rest, lambda: None),
    )
    breadth = totals[0].shape[0]
    for q in range(2):
        give_ref[q * breadth : (q + 1) * breadth] = totals[q]


def own_kernel(data_ref, maps_ref, mask_ref, row_ref, column_ref, send_ref, total_ref, out_copy, sems):
    coils, slices, double, height = maps_ref.shape
    breadth, wide = double // 2, slices * double // 2
    here = own_slice()
    sends = []

    def emit(c):
        turned = [
            jnp.concatenate([parts_of(maps_ref, c, s)(q) for s in range(slices)], axis=0)
            .T.reshape(height // 8, 8, wide)
            for q in range(2)
        ]
        both = jnp.concatenate(turned, axis=1).astype(BF16)
        for p in range(height // 8):
            out_copy[c, p] = both[block_of(p // 2, p % 2)]
        rows = send_ref.at[:, 16 * c : 16 * c + 16, :]
        sends.append(pltpu.make_async_copy(out_copy.at[c], rows, sems.at[c]))
        sends[-1].start()

    totals = back_project(
        [data_ref[c] for c in range(coils)], [parts_of(maps_ref, c, here) for c in range(coils)],
        kept_columns(mask_ref, here), row_ref, column_ref, [lambda c=c: emit(c) for c in range(2)],
    )
    for q in range(2):
        total_ref[q * breadth : (q + 1) * breadth] = totals[q]
    for copy in sends:
        copy.wait()


def sum_kernel(total_ref, got_ref, mask_ref, old_ref, send_ref, mask_out_ref, out_copy, sem):
    double, height = total_ref.shape
    turned = (total_ref[...] + got_ref[...]).T.reshape(height // 8, 8, double).astype(BF16)
    for p in range(height // 8):
        out_copy[p] = turned[block_of(p // 2, p % 2)]
    first = send_ref.shape[1] - 8
    copy = pltpu.make_async_copy(out_copy, send_ref.at[:, first : first + 8, :], sem)
    copy.start()
    mask_out_ref[...] = mask_ref[...].astype(F32).astype(BF16)
    copy.wait()


def table_kernel(
    own_ref, other_ref, angle_ref, first_ref, bias_ref, second_ref, pick_first_ref, pick_second_ref, place_ref,
    project_ref, first_out_ref, second_out_ref,
):
    slices, breadth = own_ref.shape
    wide = slices * breadth
    here = lax.axis_index("sect")
    angle = angle_ref[...]
    swapped = jnp.concatenate([angle[:, wide:], -angle[:, :wide]], axis=1)
    cosine, sine = angle[:, :breadth], angle[:, wide : wide + breadth]
    angle, swapped = split3(angle), split3(swapped)
    for t in range(project_ref.shape[0]):
        mask = jnp.where(here == t, own_ref[...].astype(F32), other_ref[...].astype(F32))
        for s in range(slices):
            row = mask[s : s + 1]
            block = dot3(split3(cosine * row), angle) + dot3(split3(sine * row), swapped)
            if s:
                block = pltpu.roll(block, s * breadth, 1)
            rows = slice(s * breadth, (s + 1) * breadth)
            project_ref[t, rows] = block.astype(BF16)
            rows = slice(wide + s * breadth, wide + (s + 1) * breadth)
            project_ref[t, rows] = jnp.concatenate([-block[:, wide:], block[:, :wide]], axis=1).astype(BF16)

    groups, _, depth = pick_first_ref.shape
    features = first_ref.shape[1]
    bias = column_of(bias_ref[...])
    parts = []
    for _ in range(3):
        parts.append(bias.astype(BF16).astype(F32))
        bias = bias - parts[-1]
    lane = lax.broadcasted_iota(jnp.int32, (features, depth), 1)
    second = 0.0
    for s in range(groups):
        block = lax.dot_general(
            first_ref[...], pick_first_ref[s], (((0,), (0,)), ((), ())), preferred_element_type=F32
        )
        for i in range(3):
            block = jnp.where(lane == depth - 8 + i, parts[i], block)
        first_out_ref[s * features : (s + 1) * features] = block.astype(BF16)
        second += dot(dot(pick_second_ref[s], second_ref[...]).astype(BF16), place_ref[s])
    second_out_ref[...] = second.astype(BF16)


def apply_data_term(near_ref, project_ref, image, start, left_ref, spun_ref, breadth):
    coils, groups = near_ref.shape[0], near_ref.shape[1]
    wide = near_ref.shape[3]

    def maps_of(i, t, c):
        maps = near_ref[i, t, 16 * c : 16 * c + 16, :].astype(F32)
        return maps[:8], maps[8:]

    for t in range(groups):
        image_re, image_im = image[t][:8], image[t][8:]
        for i in range(coils):
            reals, imags = [], []
            for c in range(2):
                map_re, map_im = maps_of(i, t, c)
                reals.append(map_re * image_re - map_im * image_im)
                imags.append(map_re * image_im + map_im * image_re)
            left_ref[t, 16 * i : 16 * i + 16, :wide] = jnp.concatenate(reals, axis=0).astype(BF16)
            left_ref[t, 16 * i : 16 * i + 16, wide:] = jnp.concatenate(imags, axis=0).astype(BF16)
        spun_ref[t] = dot(left_ref[t], project_ref[t])
    result = []
    for t in range(groups):
        sum_re, sum_im = 0.0, 0.0
        for i in range(coils):
            for c in range(2):
                map_re, map_im = maps_of(i, t, c)
                rows = slice(16 * i + 8 * c, 16 * i + 8 * c + 8)
                spun_re, spun_im = spun_ref[t, rows, :wide], spun_ref[t, rows, wide:]
                sum_re += map_re * spun_re + map_im * spun_im
                sum_im += map_re * spun_im - map_im * spun_re
        normal = jnp.concatenate([sum_re, sum_im], axis=0)
        result.append(image[t] - STEP * (normal * (1.0 / breadth) - start[t]))
    return result


def to_rows(damped, out_ref, flip_ref, breadth):
    per_group = damped[0].shape[1] // breadth
    wide = damped[0].shape[1]
    lanes = lax.broadcasted_iota(jnp.int32, (16, LANES), 1)
    for t, value in enumerate(damped):
        for s in range(per_group):
            moved = value if s == 0 else pltpu.roll(value, wide - s * breadth, 1)
            moved = jnp.where(lanes < breadth, moved[:, :LANES], 0.0)
            for q in range(2):
                place = (t * per_group + s) * 2 + q
                for j in range(2):
                    part = moved[8 * q : 8 * q + 8, 128 * j : 128 * j + 128]
                    flip_ref[pl.ds(64 * j + place, 8, stride=8), :] = part
    for j in range(2):
        out_ref[:, 128 * j : 128 * j + 128] = flip_ref[64 * j : 64 * j + 64]


def from_rows(flip_ref, groups, per_group, breadth):
    wide = per_group * breadth
    result = []
    for t in range(groups):
        parts = []
        for q in range(2):
            value = jnp.zeros((8, wide), F32)
            for s in range(per_group):
                place = (t * per_group + s) * 2 + q
                halves = [flip_ref[pl.ds(64 * j + place, 8, stride=8), :] for j in range(2)]
                piece = jnp.concatenate(halves + [jnp.zeros((8, wide - LANES), F32)], axis=1)
                value += piece if s == 0 else pltpu.roll(piece, s * breadth, 1)
            parts.append(value)
        result.append(jnp.concatenate(parts, axis=0))
    return result


def position_of():
    return block_of(lax.axis_index("coil"), lax.axis_index("sect"))


def write_edges(rows_ref, inner_ref, outer_ref):
    odd = position_of() % 2 == 1
    low, high = rows_ref[:16], rows_ref[48:64]
    inner_ref[...] = jnp.where(odd, low, high).astype(BF16)
    outer_ref[...] = jnp.where(odd, high, low).astype(BF16)


def keep_close(*arrays):
    return [pltpu.with_memory_space_constraint(x, pltpu.VMEM) for x in arrays]


def second_kernel(
    near_ref, project_ref, rows_ref, inner_ref, outer_ref, start_ref,
    flip_ref, left_ref, spun_ref, *, breadth,
):
    coils, groups, _, wide = near_ref.shape
    start = []
    first = lax.broadcasted_iota(jnp.int32, (8, wide), 1) < breadth
    for t in range(groups):
        def add(i, totals, t=t):
            return tuple(x + near_ref[2 * i + s, t, 32:40, :].astype(F32) for s, x in enumerate(totals))

        zero = jnp.zeros((8, wide), F32)
        low, high = lax.fori_loop(0, coils // 2, add, (zero, zero), unroll=4)
        parts = [
            jnp.where(first, low, pltpu.roll(high, breadth, 1)),
            jnp.where(first, pltpu.roll(low, breadth, 1), high),
        ]
        start.append(jnp.concatenate(parts, axis=0))
        start_ref[t] = start[t]
    damped = apply_data_term(near_ref, project_ref, start, start, left_ref, spun_ref, breadth)
    to_rows(damped, rows_ref, flip_ref, breadth)
    write_edges(rows_ref, inner_ref, outer_ref)


def tap_blocks(values, places, first_ref, second_ref, shift_ref, breadth):
    for h, value in values.items():
        shift_ref[24 * h : 24 * h + 8] = pltpu.roll(value, 1, 1)
        shift_ref[24 * h + 8 : 24 * h + 16] = value
        shift_ref[24 * h + 16 : 24 * h + 24] = pltpu.roll(value, LANES - 1, 1)
    ones = jnp.ones((8, LANES), F32)
    hidden = {}
    for g in places:
        columns = jnp.concatenate([shift_ref[24 * g : 24 * g + 72], ones], axis=0).astype(BF16)
        block = dot(first_ref[...], columns).astype(BF16)
        hidden[g] = jnp.maximum(block, jnp.zeros_like(block))
    inside = lax.broadcasted_iota(jnp.int32, (1, LANES), 1) < breadth
    return {g: jnp.where(inside, dot(second_ref[...], hidden[g]), 0.0) for g in places}


def inner_kernel(rows_ref, first_ref, second_ref, taps_ref, shift_ref, *, breadth):
    values = {h: rows_ref[8 * h : 8 * h + 8] for h in range(8)}
    for g, tap in tap_blocks(values, range(6), first_ref, second_ref, shift_ref, breadth).items():
        taps_ref[g] = tap


def edge_rows(first, second):
    value = jnp.where(position_of() % 2 == 1, first.astype(F32), second.astype(F32))
    return [value[:8], value[8:]]


def regularized(
    rows_ref, taps_ref, inner_ref, outer_ref, first_ref, second_ref, bias_ref, shift_ref, breadth
):
    inner, outer = inner_ref[...], outer_ref[...]
    own = [rows_ref[8 * h : 8 * h + 8] for h in range(8)]
    values = edge_rows(inner, outer) + own + edge_rows(outer, inner)
    taps = tap_blocks(
        {h: values[h] for h in (0, 1, 2, 3, 8, 9, 10, 11)}, (0, 1, 8, 9), first_ref, second_ref, shift_ref, breadth
    )
    taps.update({g + 2: taps_ref[g] for g in range(6)})
    last = 2 * lax.axis_size("coil") - 1
    taps[0] = jnp.where(position_of() > 0, taps[0], 0.0)
    taps[9] = jnp.where(position_of() < last, taps[9], 0.0)
    lanes = lax.broadcasted_iota(jnp.int32, (1, LANES), 1)
    odd = lax.broadcasted_iota(jnp.int32, (8, LANES), 0) % 2 == 1
    bias = jnp.where(odd, bias_ref[1], bias_ref[0])
    updates = []
    for h in range(8):
        total = taps[h][:24] + taps[h + 1][24:48] + taps[h + 2][48:]
        update = pltpu.roll(total[:8], 1, 1) + total[8:16] + pltpu.roll(total[16:], LANES - 1, 1)
        updates.append(jnp.where(lanes < breadth, update + bias, 0.0))
    return own, updates


def third_kernel(
    rows_ref, taps_ref, inner_ref, outer_ref, first_ref, second_ref, bias_ref, near_ref, project_ref, start_ref,
    out_ref, inner_out_ref, outer_out_ref,
    shift_ref, flip_ref, left_ref, spun_ref, *, breadth,
):
    groups, _, wide = start_ref.shape
    own, updates = regularized(
        rows_ref, taps_ref, inner_ref, outer_ref, first_ref, second_ref, bias_ref, shift_ref, breadth
    )
    for h in range(8):
        image = own[h] + updates[h]
        for j in range(2):
            flip_ref[64 * j + 8 * h : 64 * j + 8 * h + 8] = image[:, 128 * j : 128 * j + 128]
    image = from_rows(flip_ref, groups, wide // breadth, breadth)
    start = [start_ref[t] for t in range(groups)]
    damped = apply_data_term(near_ref, project_ref, image, start, left_ref, spun_ref, breadth)
    to_rows(damped, out_ref, flip_ref, breadth)
    write_edges(out_ref, inner_out_ref, outer_out_ref)


def last_kernel(
    rows_ref, taps_ref, inner_ref, outer_ref, first_ref, second_ref, bias_ref, keep_ref, give_ref,
    shift_ref, *, breadth,
):
    own, updates = regularized(
        rows_ref, taps_ref, inner_ref, outer_ref, first_ref, second_ref, bias_ref, shift_ref, breadth
    )
    upper = lax.axis_index("sect") == 0
    for h in range(8):
        image = (own[h] + updates[h])[:, :breadth]
        keep, give = jnp.where(upper, image[:4], image[4:]), jnp.where(upper, image[4:], image[:4])
        for s in range(2):
            keep_ref[h, s] = keep[2 * s : 2 * s + 2]
            give_ref[h, s] = give[2 * s : 2 * s + 2]


def join_kernel(keep_ref, got_ref, out_ref):
    odd = position_of() % 2 == 1
    keep, got = keep_ref[...], got_ref[...]
    out_ref[:8] = jnp.where(odd, got, keep)
    out_ref[8:] = jnp.where(odd, keep, got)


def fast_device(measured, coil_maps, sampling, conv_first, bias_first, conv_second, bias_second):
    height, coils_here, slices_here, _, breadth = coil_maps.shape
    ranks, sects = lax.axis_size("coil"), lax.axis_size("sect")
    count = ranks * sects
    slices = slices_here * sects
    wide = slices_here * breadth
    features = conv_first.shape[0]
    both = ("coil", "sect")
    f32 = lambda *dims: jax.ShapeDtypeStruct(dims, F32)
    bf16 = lambda *dims: jax.ShapeDtypeStruct(dims, BF16)

    row_cos, row_sin = dft_tables(height)
    col_cos, col_sin = dft_tables(breadth)
    row_high, row_low = bf16_pair(np.concatenate([row_cos, row_sin], axis=1) / math.sqrt(height))
    column_high, column_low = bf16_pair(np.concatenate([col_cos, col_sin], axis=0) / math.sqrt(breadth))
    row_table = jnp.asarray(np.concatenate([row_high, row_high, row_low], axis=0))
    column_table = jnp.asarray(np.concatenate([column_high, column_high, column_low], axis=1))
    by_coil = lambda x: jnp.transpose(x, (1, 2, 3, 4, 0)).reshape(coils_here, slices_here, 2 * breadth, height)
    block_rows = 16 * coils_here + 8
    far = (by_coil(measured), by_coil(coil_maps), sampling, row_table, column_table)
    double = 2 * breadth
    anywhere = pl.BlockSpec(memory_space=pl.ANY)
    roomy = pltpu.CompilerParams(vmem_limit_bytes=40 << 20)
    give, *fetched = pl.pallas_call(
        first_kernel, compiler_params=roomy,
        in_specs=[anywhere] * 5, out_specs=vmem(6),
        out_shape=[
            f32(double, height), pltpu.VMEM((coils_here, double, height), F32),
            *[pltpu.VMEM(x.shape, x.dtype) for x in far[1:]],
        ],
        scratch_shapes=[
            pltpu.VMEM((coils_here, double, height), F32), pltpu.SemaphoreType.DMA((3 + 4 * coils_here,)),
        ],
    )(*[pltpu.with_memory_space_constraint(x, pltpu.HBM) for x in far])
    got = lax.ppermute(give, "coil", [(i, i ^ 1) for i in range(ranks)])
    send, total = pl.pallas_call(
        own_kernel, compiler_params=roomy,
        in_specs=vmem(5), out_specs=[anywhere] + vmem(1),
        out_shape=[bf16(count, block_rows, wide), pltpu.VMEM((double, height), F32)],
        scratch_shapes=[pltpu.VMEM((coils_here, count, 16, wide), BF16), pltpu.SemaphoreType.DMA((coils_here,))],
    )(*keep_close(*fetched))
    send, mask = pl.pallas_call(
        sum_kernel, compiler_params=MODEST,
        in_specs=vmem(3) + [anywhere], out_specs=[anywhere] + vmem(1),
        out_shape=[bf16(count, block_rows, wide), bf16(slices_here, breadth)],
        input_output_aliases={3: 0},
        scratch_shapes=[pltpu.VMEM((count, 8, wide), BF16), pltpu.SemaphoreType.DMA],
    )(*keep_close(total, got, fetched[2]), send)
    near = lax.all_to_all(send, both, 0, 0, tiled=True).reshape(ranks, sects, block_rows, wide)

    other = lax.ppermute(mask, "sect", [(0, 1), (1, 0)])
    blank = np.zeros((breadth, wide - breadth))
    angle = np.concatenate([col_cos, blank, col_sin, blank], axis=1).astype(np.float32)
    span = 18 * slices
    pick_first = np.zeros((slices, 54, span + 8))
    pick_second = np.zeros((slices, span, 54))
    for a, b, e, q, s in np.ndindex(3, 3, 3, 2, slices):
        tap = 2 * (9 * a + 3 * b + e) + q
        if 0 <= s + b - 1 < slices:
            pick_first[s, tap, ((a * 3 + e) * slices + s + b - 1) * 2 + q] = 1.0
            pick_second[s + b - 1, ((a * 3 + e) * slices + s) * 2 + q, tap] = 1.0
    place = np.eye(slices * features).reshape(slices, features, slices * features)
    project, matrix_first, matrix_second = pl.pallas_call(
        table_kernel,
        compiler_params=MODEST,
        in_specs=vmem(9), out_specs=vmem(3),
        out_shape=[
            pltpu.VMEM(dims, BF16)
            for dims in (
                (sects, 2 * wide, 2 * wide), (slices * features, span + 8), (span, slices * features),
            )
        ],
    )(
        mask, other, jnp.asarray(angle), conv_first.T, bias_first.reshape(1, features), conv_second,
        *[jnp.asarray(x.astype(BF16)) for x in (pick_first, pick_second, place)],
    )
    weights = (*keep_close(matrix_first, matrix_second), bias_second)
    weight_specs = vmem(2) + [pl.BlockSpec(memory_space=pltpu.SMEM)]

    owner = {block_of(i, y): 2 * i + y for i in range(ranks) for y in range(2)}
    near_pairs = []
    for block in range(1, count - 1, 2):
        near_pairs += [(owner[block], owner[block + 1]), (owner[block + 1], owner[block])]
    swap = lambda x: lax.ppermute(x, "sect", [(0, 1), (1, 0)])

    edge = 4 * slices
    work = [
        pltpu.VMEM((32 * slices, 128), F32),
        pltpu.VMEM((sects, 16 * ranks, 2 * wide), BF16), pltpu.VMEM((sects, 16 * ranks, 2 * wide), F32),
    ]

    shift = [pltpu.VMEM((12 * 6 * slices, LANES), F32)]

    def around(rows, inner, outer):
        taps = pl.pallas_call(
            functools.partial(inner_kernel, breadth=breadth),
            compiler_params=MODEST, in_specs=vmem(3), out_specs=vmem(1)[0],
            out_shape=pltpu.VMEM((6, 18 * slices, LANES), F32), scratch_shapes=shift,
        )(*keep_close(rows), *weights[:2])
        return keep_close(rows, taps, swap(inner), lax.ppermute(outer, both, near_pairs))

    row_shapes = [f32(16 * slices, LANES), bf16(edge, LANES), bf16(edge, LANES)]
    rows, inner, outer, start = pl.pallas_call(
        functools.partial(second_kernel, breadth=breadth),
        compiler_params=MODEST,
        in_specs=vmem(2), out_specs=vmem(4),
        out_shape=row_shapes + [pltpu.VMEM((sects, 16, wide), F32)], scratch_shapes=work,
    )(*keep_close(near, project))
    for _ in range(ITERS - 1):
        rows, inner, outer = pl.pallas_call(
            functools.partial(third_kernel, breadth=breadth),
            compiler_params=MODEST,
            in_specs=vmem(4) + weight_specs + vmem(3), out_specs=vmem(3), out_shape=row_shapes,
            scratch_shapes=shift + work,
        )(*around(rows, inner, outer), *weights, *keep_close(near, project, start))
    piece = f32(8, slices_here, 2, breadth)
    keep, give = pl.pallas_call(
        functools.partial(last_kernel, breadth=breadth),
        compiler_params=MODEST,
        in_specs=vmem(4) + weight_specs, out_specs=vmem(2), out_shape=[piece, piece],
        scratch_shapes=shift,
    )(*around(rows, inner, outer), *weights)
    return pl.pallas_call(
        join_kernel, compiler_params=MODEST, in_specs=vmem(2), out_specs=vmem(1)[0],
        out_shape=f32(16, slices_here, 2, breadth),
    )(*keep_close(keep, swap(give)))


def per_device_any(measured, coil_maps, *rest):
    height, coils_here, slices_here, _, breadth = coil_maps.shape
    ranks, sects = lax.axis_size("coil"), lax.axis_size("sect")
    fits = (
        sects == 2 and slices_here == 2 and coils_here == 2 and height == 8 * ranks * sects
        and 2 * breadth % 128 == 0 and 128 < breadth < LANES and breadth % 16 == 0
    )
    return (fast_device if fits else per_device)(measured, coil_maps, *rest)


def solution(mesh):
    coil_spec = P(None, "coil", "sect", None, None)
    in_specs = (coil_spec, coil_spec, P("sect", None), P(), P(), P(), P())
    return jax.shard_map(
        per_device_any,
        mesh=mesh,
        in_specs=in_specs,
        out_specs=P("coil", "sect", None, None),
        check_vma=False,
    )
```

```python
import functools
import math

import jax
import jax.numpy as jnp
import numpy as np
from jax import lax
from jax.experimental import pallas as pl
from jax.experimental.pallas import tpu as pltpu
from jax.sharding import PartitionSpec as P

ITERS = 2
STEP = 0.5
F32 = jnp.float32
BF16 = jnp.bfloat16
HIGH = lax.Precision.HIGH
LANES = 256
MODEST = pltpu.CompilerParams(vmem_limit_bytes=24 << 20)


def dft_tables(length):
    index = np.arange(length)
    angle = (index[:, None] * index[None, :] % length) * (2.0 * math.pi / length)
    return np.cos(angle), np.sin(angle)


def with_halo(x, sides, width):
    for axis, dim in sides:
        count, length = lax.axis_size(axis), x.shape[dim]
        up = [(i, i + 1) for i in range(count - 1)]
        down = [(j, i) for i, j in up]
        before = lax.ppermute(lax.slice_in_dim(x, length - width, length, axis=dim), axis, up)
        after = lax.ppermute(lax.slice_in_dim(x, 0, width, axis=dim), axis, down)
        x = jnp.concatenate([before, x, after], axis=dim)
    return x


def stack_taps(padded, rows, slices, breadth):
    return jnp.concatenate(
        [
            padded[a : a + rows, b : b + slices, :, e : e + breadth]
            for a in range(3)
            for b in range(3)
            for e in range(3)
        ],
        axis=2,
    )


def tap_sum(taps, rows, slices, breadth):
    result = jnp.zeros((rows, slices, 2, breadth), F32)
    for place in range(27):
        a, b, e = place // 9, place // 3 % 3, place % 3
        result += taps[a : a + rows, b : b + slices, 2 * place : 2 * place + 2, e : e + breadth]
    return result


def regularize(damped, height, conv_first, bias_first, conv_second, bias_second):
    rows, slices, _, breadth = damped.shape
    extended = with_halo(damped.astype(BF16), (("coil", 0), ("sect", 1)), 2)
    padded = jnp.pad(extended, ((0, 0), (0, 0), (0, 0), (1, 1)))
    columns = stack_taps(padded, rows + 2, slices + 2, breadth)
    hidden = jnp.einsum("oc,rscw->rsow", conv_first, columns, preferred_element_type=F32)
    hidden = jax.nn.relu(hidden + bias_first[None, None, :, None]).astype(BF16)
    row_index = lax.axis_index("coil") * rows - 1 + jnp.arange(rows + 2)
    slice_index = lax.axis_index("sect") * slices - 1 + jnp.arange(slices + 2)
    row_valid = (row_index >= 0) & (row_index < height)
    slice_valid = (slice_index >= 0) & (slice_index < lax.axis_size("sect") * slices)
    inside = row_valid[:, None] & slice_valid[None, :]
    hidden = jnp.where(inside[:, :, None, None], hidden, jnp.zeros_like(hidden))
    hidden = jnp.pad(hidden, ((0, 0), (0, 0), (0, 0), (1, 1)))
    taps = jnp.einsum("tc,rscw->rstw", conv_second, hidden, preferred_element_type=F32)
    return tap_sum(taps, rows, slices, breadth) + bias_second[None, None, :, None]


def per_device(measured, coil_maps, sampling, conv_first, bias_first, conv_second, bias_second):
    height, coils_here, slices_here, _, breadth = coil_maps.shape
    count = lax.axis_size("coil")
    rows = height // count
    mask = sampling.astype(F32)

    def exchange(x):
        split = x.astype(BF16).reshape((count, rows) + x.shape[1:])
        return lax.all_to_all(split, "coil", 0, 0, tiled=True)

    row_cos, row_sin = dft_tables(height)
    col_cos, col_sin = dft_tables(breadth)
    row_table = jnp.asarray(np.stack([row_cos, row_sin]) / math.sqrt(height), F32)
    col_table = jnp.asarray(
        np.block([[col_cos, col_sin], [-col_sin, col_cos]]) / math.sqrt(breadth), F32
    ).reshape(2, breadth, 2, breadth)

    spread = jnp.einsum("tkh,kcsqw->tcsqwh", row_table, measured, precision=HIGH)
    spread = jnp.stack(
        [spread[0, :, :, 0] - spread[1, :, :, 1], spread[0, :, :, 1] + spread[1, :, :, 0]], axis=2
    )
    spread = spread * mask[None, :, None, :, None]
    inverse = jnp.einsum("qwpv,csqwh->csphv", col_table, spread, precision=HIGH)
    maps = jnp.transpose(coil_maps, (1, 2, 3, 0, 4))
    part_re = jnp.sum(maps[:, :, 0] * inverse[:, :, 0] + maps[:, :, 1] * inverse[:, :, 1], axis=0)
    part_im = jnp.sum(maps[:, :, 0] * inverse[:, :, 1] - maps[:, :, 1] * inverse[:, :, 0], axis=0)
    partial = jnp.transpose(jnp.stack([part_re, part_im], axis=1), (2, 0, 1, 3))
    first = jnp.sum(exchange(partial).astype(F32), axis=0)
    near = exchange(coil_maps).astype(F32)
    near_re, near_im = near[..., 0, :], near[..., 1, :]

    angle = jnp.asarray(np.stack([col_cos, col_sin]), F32)
    both = jnp.einsum("sl,alj,blv->absjv", mask, angle, angle, precision=HIGH) / breadth
    project_re = both[0, 0] + both[1, 1]
    project_im = both[0, 1] - both[1, 0]
    project = jnp.stack(
        [jnp.stack([project_re, project_im], 2), jnp.stack([-project_im, project_re], 2)]
    )

    image = first
    for _ in range(ITERS):
        image_re, image_im = image[:, :, 0], image[:, :, 1]
        product = jnp.stack(
            [near_re * image_re[:, None] - near_im * image_im[:, None],
             near_re * image_im[:, None] + near_im * image_re[:, None]]
        )
        spun = jnp.einsum("qnrcsj,qsjpv->pnrcsv", product, project, precision=HIGH)
        normal_re = jnp.sum(near_re * spun[0] + near_im * spun[1], axis=(0, 2))
        normal_im = jnp.sum(near_re * spun[1] - near_im * spun[0], axis=(0, 2))
        normal = jnp.stack([normal_re, normal_im], axis=2)
        damped = image - STEP * (normal - first)
        image = damped + regularize(
            damped, height, conv_first, bias_first, conv_second, bias_second
        )
    return image


def bf16_pair(table):
    high = table.astype(BF16)
    return high, (table - high.astype(np.float64)).astype(BF16)


def split3(x):
    high = x.astype(BF16)
    return high, (x - high.astype(F32)).astype(BF16)


def dot(x, y):
    return jnp.dot(x, y, preferred_element_type=F32)


def dot3(x, y):
    return dot(x[0], y[0]) + dot(x[1], y[0]) + dot(x[0], y[1])


def vmem(count):
    return [pl.BlockSpec(memory_space=pltpu.VMEM)] * count


def column_of(row):
    shape = (row.shape[1], row.shape[1])
    diagonal = lax.broadcasted_iota(jnp.int32, shape, 0) == lax.broadcasted_iota(jnp.int32, shape, 1)
    return jnp.sum(jnp.where(diagonal, jnp.broadcast_to(row, shape), 0.0), axis=1, keepdims=True)


def block_of(coil, sect):
    return 2 * coil + (sect + coil) % 2


def back_project(data, maps, keep, row_ref, column_ref, between):
    height = data[0].shape[1]
    breadth = data[0].shape[0] // 2
    spreads, rights = [], []
    for value in data:
        high, low = split3(value)
        spreads.append(dot(jnp.concatenate([high, low, high], axis=1), row_ref[...]))
    between[0]()
    for spread in spreads:
        real, imag = spread[:breadth], spread[breadth:]
        pieces = [
            (real[:, :height] - imag[:, height:]) * keep, (imag[:, :height] + real[:, height:]) * keep,
        ]
        high, low = split3(jnp.concatenate(pieces, axis=1))
        rights.append(jnp.concatenate([high, low, high], axis=0))
    mixes = [dot(column_ref[...], x) for x in rights]
    between[1]()
    total_re, total_im = 0.0, 0.0
    for mixed, read in zip(mixes, maps):
        inv_re = mixed[:breadth, :height] - mixed[breadth:, height:]
        inv_im = mixed[breadth:, :height] + mixed[:breadth, height:]
        map_re, map_im = read(0), read(1)
        total_re += map_re * inv_re + map_im * inv_im
        total_im += map_re * inv_im - map_im * inv_re
    return total_re, total_im


def own_slice():
    return lax.axis_index("coil") % 2


def kept_columns(mask_ref, here):
    mask = mask_ref[...].astype(F32)
    return column_of(jnp.where(here == 0, mask[:1], mask[1:]))


def parts_of(maps_ref, c, s):
    breadth = maps_ref.shape[2] // 2
    return lambda q: maps_ref[c, s, q * breadth : (q + 1) * breadth]


def first_kernel(
    data_far, maps_far, mask_far, row_far, column_far,
    give_ref, data_ref, maps_ref, mask_ref, row_ref, column_ref, other_ref, sems,
):
    coils = data_far.shape[0]
    here = own_slice()
    there = 1 - here
    depth = row_far.shape[0] // 3
    plan = [(mask_far, mask_ref)]
    plan += [(row_far.at[i * depth : (i + 1) * depth], row_ref.at[i * depth : (i + 1) * depth]) for i in range(3)]
    plan += [(data_far.at[c, there], other_ref.at[c]) for c in range(coils)]
    plan += [(column_far, column_ref)]
    plan += [(maps_far.at[c, there], maps_ref.at[c, there]) for c in range(coils)]
    plan += [(data_far.at[c, here], data_ref.at[c]) for c in range(coils)]
    plan += [(maps_far.at[c, here], maps_ref.at[c, here]) for c in range(coils)]
    copies = [pltpu.make_async_copy(x, y, sems.at[i]) for i, (x, y) in enumerate(plan)]
    for copy in copies:
        copy.start()
    copies[0].wait()
    keep = kept_columns(mask_ref, there)
    for copy in copies[1 : 4 + coils]:
        copy.wait()

    def rest():
        for copy in copies[4 + coils :]:
            copy.wait()

    totals = back_project(
        [other_ref[c] for c in range(coils)], [parts_of(maps_ref, c, there) for c in range(coils)],
        keep, row_ref, column_ref, (rest, lambda: None),
    )
    breadth = totals[0].shape[0]
    for q in range(2):
        give_ref[q * breadth : (q + 1) * breadth] = totals[q]


def own_kernel(data_ref, maps_ref, mask_ref, row_ref, column_ref, send_ref, total_ref, out_copy, sems):
    coils, slices, double, height = maps_ref.shape
    breadth, wide = double // 2, slices * double // 2
    here = own_slice()
    sends = []

    def emit(c):
        turned = [
            jnp.concatenate([parts_of(maps_ref, c, s)(q) for s in range(slices)], axis=0)
            .T.reshape(height // 8, 8, wide)
            for q in range(2)
        ]
        both = jnp.concatenate(turned, axis=1).astype(BF16)
        for p in range(height // 8):
            out_copy[c, p] = both[block_of(p // 2, p % 2)]
        rows = send_ref.at[:, 16 * c : 16 * c + 16, :]
        sends.append(pltpu.make_async_copy(out_copy.at[c], rows, sems.at[c]))
        sends[-1].start()

    totals = back_project(
        [data_ref[c] for c in range(coils)], [parts_of(maps_ref, c, here) for c in range(coils)],
        kept_columns(mask_ref, here), row_ref, column_ref, [lambda c=c: emit(c) for c in range(2)],
    )
    for q in range(2):
        total_ref[q * breadth : (q + 1) * breadth] = totals[q]
    for copy in sends:
        copy.wait()


def sum_kernel(total_ref, got_ref, mask_ref, old_ref, send_ref, mask_out_ref, out_copy, sem):
    double, height = total_ref.shape
    turned = (total_ref[...] + got_ref[...]).T.reshape(height // 8, 8, double).astype(BF16)
    for p in range(height // 8):
        out_copy[p] = turned[block_of(p // 2, p % 2)]
    first = send_ref.shape[1] - 8
    copy = pltpu.make_async_copy(out_copy, send_ref.at[:, first : first + 8, :], sem)
    copy.start()
    mask_out_ref[...] = mask_ref[...].astype(F32).astype(BF16)
    copy.wait()


def table_kernel(
    own_ref, other_ref, angle_ref, first_ref, bias_ref, second_ref, pick_first_ref, pick_second_ref, place_ref,
    out_bias_ref, project_ref, first_out_ref, second_out_ref, bias_out_ref,
):
    slices, breadth = own_ref.shape
    wide = slices * breadth
    here = lax.axis_index("sect")
    angle = angle_ref[...]
    swapped = jnp.concatenate([angle[:, wide:], -angle[:, :wide]], axis=1)
    cosine, sine = angle[:, :breadth], angle[:, wide : wide + breadth]
    angle, swapped = split3(angle), split3(swapped)
    for t in range(project_ref.shape[0]):
        mask = jnp.where(here == t, own_ref[...].astype(F32), other_ref[...].astype(F32))
        for s in range(slices):
            row = mask[s : s + 1]
            block = dot3(split3(cosine * row), angle) + dot3(split3(sine * row), swapped)
            if s:
                block = pltpu.roll(block, s * breadth, 1)
            rows = slice(s * breadth, (s + 1) * breadth)
            project_ref[t, rows] = block.astype(BF16)
            rows = slice(wide + s * breadth, wide + (s + 1) * breadth)
            project_ref[t, rows] = jnp.concatenate([-block[:, wide:], block[:, :wide]], axis=1).astype(BF16)

    odd = lax.broadcasted_iota(jnp.int32, bias_out_ref.shape, 0) % 2 == 1
    inside = lax.broadcasted_iota(jnp.int32, bias_out_ref.shape, 1) < breadth
    bias_out_ref[...] = jnp.where(inside, jnp.where(odd, out_bias_ref[1], out_bias_ref[0]), 0.0)

    groups, _, depth = pick_first_ref.shape
    features = first_ref.shape[1]
    bias = column_of(bias_ref[...])
    parts = []
    for _ in range(3):
        parts.append(bias.astype(BF16).astype(F32))
        bias = bias - parts[-1]
    lane = lax.broadcasted_iota(jnp.int32, (features, depth), 1)
    second = 0.0
    for s in range(groups):
        block = lax.dot_general(
            first_ref[...], pick_first_ref[s], (((0,), (0,)), ((), ())), preferred_element_type=F32
        )
        for i in range(3):
            block = jnp.where(lane == depth - 8 + i, parts[i], block)
        first_out_ref[s * features : (s + 1) * features] = block.astype(BF16)
        second += dot(dot(pick_second_ref[s], second_ref[...]).astype(BF16), place_ref[s])
    second_out_ref[...] = second.astype(BF16)


def apply_data_term(near_ref, project_ref, image, start, left_ref, spun_ref, breadth):
    coils, groups = near_ref.shape[0], near_ref.shape[1]
    wide = near_ref.shape[3]

    def maps_of(i, t, c):
        maps = near_ref[i, t, 16 * c : 16 * c + 16, :].astype(F32)
        return maps[:8], maps[8:]

    for t in range(groups):
        image_re, image_im = image[t][:8], image[t][8:]
        for i in range(coils):
            reals, imags = [], []
            for c in range(2):
                map_re, map_im = maps_of(i, t, c)
                reals.append(map_re * image_re - map_im * image_im)
                imags.append(map_re * image_im + map_im * image_re)
            left_ref[t, 16 * i : 16 * i + 16, :wide] = jnp.concatenate(reals, axis=0).astype(BF16)
            left_ref[t, 16 * i : 16 * i + 16, wide:] = jnp.concatenate(imags, axis=0).astype(BF16)
        spun_ref[t] = dot(left_ref[t], project_ref[t])
    result = []
    for t in range(groups):
        sum_re, sum_im = 0.0, 0.0
        for i in range(coils):
            for c in range(2):
                map_re, map_im = maps_of(i, t, c)
                rows = slice(16 * i + 8 * c, 16 * i + 8 * c + 8)
                spun_re, spun_im = spun_ref[t, rows, :wide], spun_ref[t, rows, wide:]
                sum_re += map_re * spun_re + map_im * spun_im
                sum_im += map_re * spun_im - map_im * spun_re
        normal = jnp.concatenate([sum_re, sum_im], axis=0)
        result.append(image[t] - STEP * (normal * (1.0 / breadth) - start[t]))
    return result


def to_rows(damped, out_ref, flip_ref, breadth):
    per_group = damped[0].shape[1] // breadth
    wide = damped[0].shape[1]
    lanes = lax.broadcasted_iota(jnp.int32, (16, LANES), 1)
    for t, value in enumerate(damped):
        for s in range(per_group):
            moved = value if s == 0 else pltpu.roll(value, wide - s * breadth, 1)
            moved = jnp.where(lanes < breadth, moved[:, :LANES], 0.0)
            for q in range(2):
                place = (t * per_group + s) * 2 + q
                for j in range(2):
                    part = moved[8 * q : 8 * q + 8, 128 * j : 128 * j + 128]
                    flip_ref[pl.ds(64 * j + place, 8, stride=8), :] = part
    for j in range(2):
        out_ref[:, 128 * j : 128 * j + 128] = flip_ref[64 * j : 64 * j + 64]


def from_rows(flip_ref, groups, per_group, breadth):
    wide = per_group * breadth
    result = []
    for t in range(groups):
        parts = []
        for q in range(2):
            value = jnp.zeros((8, wide), F32)
            for s in range(per_group):
                place = (t * per_group + s) * 2 + q
                halves = [flip_ref[pl.ds(64 * j + place, 8, stride=8), :] for j in range(2)]
                piece = jnp.concatenate(halves + [jnp.zeros((8, wide - LANES), F32)], axis=1)
                value += piece if s == 0 else pltpu.roll(piece, s * breadth, 1)
            parts.append(value)
        result.append(jnp.concatenate(parts, axis=0))
    return result


def position_of():
    return block_of(lax.axis_index("coil"), lax.axis_index("sect"))


def write_edges(rows_ref, inner_ref, outer_ref):
    odd = position_of() % 2 == 1
    low, high = rows_ref[:16], rows_ref[48:64]
    inner_ref[...] = jnp.where(odd, low, high).astype(BF16)
    outer_ref[...] = jnp.where(odd, high, low).astype(BF16)


def keep_close(*arrays):
    return [pltpu.with_memory_space_constraint(x, pltpu.VMEM) for x in arrays]


def second_kernel(
    near_ref, project_ref, rows_ref, inner_ref, outer_ref, start_ref,
    flip_ref, left_ref, spun_ref, *, breadth,
):
    coils, groups, _, wide = near_ref.shape
    start = []
    first = lax.broadcasted_iota(jnp.int32, (8, wide), 1) < breadth
    for t in range(groups):
        def add(i, totals, t=t):
            return tuple(x + near_ref[2 * i + s, t, 32:40, :].astype(F32) for s, x in enumerate(totals))

        zero = jnp.zeros((8, wide), F32)
        low, high = lax.fori_loop(0, coils // 2, add, (zero, zero), unroll=4)
        parts = [
            jnp.where(first, low, pltpu.roll(high, breadth, 1)),
            jnp.where(first, pltpu.roll(low, breadth, 1), high),
        ]
        start.append(jnp.concatenate(parts, axis=0))
        start_ref[t] = start[t]
    damped = apply_data_term(near_ref, project_ref, start, start, left_ref, spun_ref, breadth)
    to_rows(damped, rows_ref, flip_ref, breadth)
    write_edges(rows_ref, inner_ref, outer_ref)


def tap_blocks(values, places, first_ref, second_ref, shift_ref, breadth):
    for h, value in values.items():
        shift_ref[24 * h : 24 * h + 8] = pltpu.roll(value, 1, 1)
        shift_ref[24 * h + 8 : 24 * h + 16] = value
        shift_ref[24 * h + 16 : 24 * h + 24] = pltpu.roll(value, LANES - 1, 1)
    ones = jnp.ones((8, LANES), F32)
    hidden = {}
    for g in places:
        columns = jnp.concatenate([shift_ref[24 * g : 24 * g + 72], ones], axis=0).astype(BF16)
        block = dot(first_ref[...], columns).astype(BF16)
        hidden[g] = jnp.maximum(block, jnp.zeros_like(block))
    inside = lax.broadcasted_iota(jnp.int32, (1, LANES), 1) < breadth
    return {g: jnp.where(inside, dot(second_ref[...], hidden[g]), 0.0) for g in places}


def inner_kernel(rows_ref, first_ref, second_ref, taps_ref, shift_ref, *, breadth):
    values = {h: rows_ref[8 * h : 8 * h + 8] for h in range(8)}
    for g, tap in tap_blocks(values, range(6), first_ref, second_ref, shift_ref, breadth).items():
        taps_ref[g] = tap


def edge_rows(first, second):
    value = jnp.where(position_of() % 2 == 1, first.astype(F32), second.astype(F32))
    return [value[:8], value[8:]]


def regularized(
    rows_ref, taps_ref, inner_ref, outer_ref, first_ref, second_ref, bias_ref, shift_ref, breadth
):
    inner, outer = inner_ref[...], outer_ref[...]
    own = [rows_ref[8 * h : 8 * h + 8] for h in range(8)]
    values = edge_rows(inner, outer) + own + edge_rows(outer, inner)
    taps = tap_blocks(
        {h: values[h] for h in (0, 1, 2, 3, 8, 9, 10, 11)}, (0, 1, 8, 9), first_ref, second_ref, shift_ref, breadth
    )
    taps.update({g + 2: taps_ref[g] for g in range(6)})
    last = 2 * lax.axis_size("coil") - 1
    taps[0] = jnp.where(position_of() > 0, taps[0], 0.0)
    taps[9] = jnp.where(position_of() < last, taps[9], 0.0)
    lanes = lax.broadcasted_iota(jnp.int32, (1, LANES), 1)
    bias = bias_ref[...]
    updates = []
    for h in range(8):
        total = taps[h][:24] + taps[h + 1][24:48] + taps[h + 2][48:]
        update = pltpu.roll(total[:8], 1, 1) + total[8:16] + pltpu.roll(total[16:], LANES - 1, 1)
        updates.append(jnp.where(lanes < breadth, update, 0.0) + bias)
    return own, updates


def third_kernel(
    rows_ref, taps_ref, inner_ref, outer_ref, first_ref, second_ref, bias_ref, near_ref, project_ref, start_ref,
    out_ref, inner_out_ref, outer_out_ref,
    shift_ref, flip_ref, left_ref, spun_ref, *, breadth,
):
    groups, _, wide = start_ref.shape
    own, updates = regularized(
        rows_ref, taps_ref, inner_ref, outer_ref, first_ref, second_ref, bias_ref, shift_ref, breadth
    )
    for h in range(8):
        image = own[h] + updates[h]
        for j in range(2):
            flip_ref[64 * j + 8 * h : 64 * j + 8 * h + 8] = image[:, 128 * j : 128 * j + 128]
    image = from_rows(flip_ref, groups, wide // breadth, breadth)
    start = [start_ref[t] for t in range(groups)]
    damped = apply_data_term(near_ref, project_ref, image, start, left_ref, spun_ref, breadth)
    to_rows(damped, out_ref, flip_ref, breadth)
    write_edges(out_ref, inner_out_ref, outer_out_ref)


def last_kernel(
    rows_ref, taps_ref, inner_ref, outer_ref, first_ref, second_ref, bias_ref, keep_ref, give_ref,
    shift_ref, *, breadth,
):
    own, updates = regularized(
        rows_ref, taps_ref, inner_ref, outer_ref, first_ref, second_ref, bias_ref, shift_ref, breadth
    )
    upper = lax.axis_index("sect") == 0
    for h in range(8):
        image = (own[h] + updates[h])[:, :breadth]
        keep, give = jnp.where(upper, image[:4], image[4:]), jnp.where(upper, image[4:], image[:4])
        for s in range(2):
            keep_ref[h, s] = keep[2 * s : 2 * s + 2]
            give_ref[h, s] = give[2 * s : 2 * s + 2]


def join_kernel(keep_ref, got_ref, out_ref):
    odd = position_of() % 2 == 1
    keep, got = keep_ref[...], got_ref[...]
    out_ref[:8] = jnp.where(odd, got, keep)
    out_ref[8:] = jnp.where(odd, keep, got)


def fast_device(measured, coil_maps, sampling, conv_first, bias_first, conv_second, bias_second):
    height, coils_here, slices_here, _, breadth = coil_maps.shape
    ranks, sects = lax.axis_size("coil"), lax.axis_size("sect")
    count = ranks * sects
    slices = slices_here * sects
    wide = slices_here * breadth
    features = conv_first.shape[0]
    both = ("coil", "sect")
    f32 = lambda *dims: jax.ShapeDtypeStruct(dims, F32)
    bf16 = lambda *dims: jax.ShapeDtypeStruct(dims, BF16)

    row_cos, row_sin = dft_tables(height)
    col_cos, col_sin = dft_tables(breadth)
    row_high, row_low = bf16_pair(np.concatenate([row_cos, row_sin], axis=1) / math.sqrt(height))
    column_high, column_low = bf16_pair(np.concatenate([col_cos, col_sin], axis=0) / math.sqrt(breadth))
    row_table = jnp.asarray(np.concatenate([row_high, row_high, row_low], axis=0))
    column_table = jnp.asarray(np.concatenate([column_high, column_high, column_low], axis=1))
    by_coil = lambda x: jnp.transpose(x, (1, 2, 3, 4, 0)).reshape(coils_here, slices_here, 2 * breadth, height)
    block_rows = 16 * coils_here + 8
    far = (by_coil(measured), by_coil(coil_maps), sampling, row_table, column_table)
    double = 2 * breadth
    anywhere = pl.BlockSpec(memory_space=pl.ANY)
    roomy = pltpu.CompilerParams(vmem_limit_bytes=40 << 20)
    give, *fetched = pl.pallas_call(
        first_kernel, compiler_params=roomy,
        in_specs=[anywhere] * 5, out_specs=vmem(6),
        out_shape=[
            f32(double, height), pltpu.VMEM((coils_here, double, height), F32),
            *[pltpu.VMEM(x.shape, x.dtype) for x in far[1:]],
        ],
        scratch_shapes=[
            pltpu.VMEM((coils_here, double, height), F32), pltpu.SemaphoreType.DMA((5 + 4 * coils_here,)),
        ],
    )(*[pltpu.with_memory_space_constraint(x, pltpu.HBM) for x in far])
    got = lax.ppermute(give, "coil", [(i, i ^ 1) for i in range(ranks)])
    send, total = pl.pallas_call(
        own_kernel, compiler_params=roomy,
        in_specs=vmem(5), out_specs=[anywhere] + vmem(1),
        out_shape=[bf16(count, block_rows, wide), pltpu.VMEM((double, height), F32)],
        scratch_shapes=[pltpu.VMEM((coils_here, count, 16, wide), BF16), pltpu.SemaphoreType.DMA((coils_here,))],
    )(*keep_close(*fetched))
    send, mask = pl.pallas_call(
        sum_kernel, compiler_params=MODEST,
        in_specs=vmem(3) + [anywhere], out_specs=[anywhere] + vmem(1),
        out_shape=[bf16(count, block_rows, wide), bf16(slices_here, breadth)],
        input_output_aliases={3: 0},
        scratch_shapes=[pltpu.VMEM((count, 8, wide), BF16), pltpu.SemaphoreType.DMA],
    )(*keep_close(total, got, fetched[2]), send)
    near = lax.all_to_all(send, both, 0, 0, tiled=True).reshape(ranks, sects, block_rows, wide)

    other = lax.ppermute(mask, "sect", [(0, 1), (1, 0)])
    blank = np.zeros((breadth, wide - breadth))
    angle = np.concatenate([col_cos, blank, col_sin, blank], axis=1).astype(np.float32)
    span = 18 * slices
    pick_first = np.zeros((slices, 54, span + 8))
    pick_second = np.zeros((slices, span, 54))
    for a, b, e, q, s in np.ndindex(3, 3, 3, 2, slices):
        tap = 2 * (9 * a + 3 * b + e) + q
        if 0 <= s + b - 1 < slices:
            pick_first[s, tap, ((a * 3 + e) * slices + s + b - 1) * 2 + q] = 1.0
            pick_second[s + b - 1, ((a * 3 + e) * slices + s) * 2 + q, tap] = 1.0
    place = np.eye(slices * features).reshape(slices, features, slices * features)
    project, matrix_first, matrix_second, bias = pl.pallas_call(
        table_kernel,
        compiler_params=MODEST,
        in_specs=vmem(9) + [pl.BlockSpec(memory_space=pltpu.SMEM)], out_specs=vmem(4),
        out_shape=[
            pltpu.VMEM(dims, BF16)
            for dims in (
                (sects, 2 * wide, 2 * wide), (slices * features, span + 8), (span, slices * features),
            )
        ] + [pltpu.VMEM((2 * slices, LANES), F32)],
    )(
        mask, other, jnp.asarray(angle), conv_first.T, bias_first.reshape(1, features), conv_second,
        *[jnp.asarray(x.astype(BF16)) for x in (pick_first, pick_second, place)], bias_second,
    )
    weights = keep_close(matrix_first, matrix_second, bias)
    weight_specs = vmem(3)

    owner = {block_of(i, y): 2 * i + y for i in range(ranks) for y in range(2)}
    near_pairs = []
    for block in range(1, count - 1, 2):
        near_pairs += [(owner[block], owner[block + 1]), (owner[block + 1], owner[block])]
    swap = lambda x: lax.ppermute(x, "sect", [(0, 1), (1, 0)])

    edge = 4 * slices
    work = [
        pltpu.VMEM((32 * slices, 128), F32),
        pltpu.VMEM((sects, 16 * ranks, 2 * wide), BF16), pltpu.VMEM((sects, 16 * ranks, 2 * wide), F32),
    ]

    shift = [pltpu.VMEM((12 * 6 * slices, LANES), F32)]

    def around(rows, inner, outer):
        taps = pl.pallas_call(
            functools.partial(inner_kernel, breadth=breadth),
            compiler_params=MODEST, in_specs=vmem(3), out_specs=vmem(1)[0],
            out_shape=pltpu.VMEM((6, 18 * slices, LANES), F32), scratch_shapes=shift,
        )(*keep_close(rows), *weights[:2])
        return keep_close(rows, taps, swap(inner), lax.ppermute(outer, both, near_pairs))

    row_shapes = [f32(16 * slices, LANES), bf16(edge, LANES), bf16(edge, LANES)]
    rows, inner, outer, start = pl.pallas_call(
        functools.partial(second_kernel, breadth=breadth),
        compiler_params=MODEST,
        in_specs=vmem(2), out_specs=vmem(4),
        out_shape=row_shapes + [pltpu.VMEM((sects, 16, wide), F32)], scratch_shapes=work,
    )(*keep_close(near, project))
    for _ in range(ITERS - 1):
        rows, inner, outer = pl.pallas_call(
            functools.partial(third_kernel, breadth=breadth),
            compiler_params=MODEST,
            in_specs=vmem(4) + weight_specs + vmem(3), out_specs=vmem(3), out_shape=row_shapes,
            scratch_shapes=shift + work,
        )(*around(rows, inner, outer), *weights, *keep_close(near, project, start))
    piece = f32(8, slices_here, 2, breadth)
    keep, give = pl.pallas_call(
        functools.partial(last_kernel, breadth=breadth),
        compiler_params=MODEST,
        in_specs=vmem(4) + weight_specs, out_specs=vmem(2), out_shape=[piece, piece],
        scratch_shapes=shift,
    )(*around(rows, inner, outer), *weights)
    return pl.pallas_call(
        join_kernel, compiler_params=MODEST, in_specs=vmem(2), out_specs=vmem(1)[0],
        out_shape=f32(16, slices_here, 2, breadth),
    )(*keep_close(keep, swap(give)))


def per_device_any(measured, coil_maps, *rest):
    height, coils_here, slices_here, _, breadth = coil_maps.shape
    ranks, sects = lax.axis_size("coil"), lax.axis_size("sect")
    fits = (
        sects == 2 and slices_here == 2 and coils_here == 2 and height == 8 * ranks * sects
        and 2 * breadth % 128 == 0 and 128 < breadth < LANES and breadth % 16 == 0
    )
    return (fast_device if fits else per_device)(measured, coil_maps, *rest)


def solution(mesh):
    coil_spec = P(None, "coil", "sect", None, None)
    in_specs = (coil_spec, coil_spec, P("sect", None), P(), P(), P(), P())
    return jax.shard_map(
        per_device_any,
        mesh=mesh,
        in_specs=in_specs,
        out_specs=P("coil", "sect", None, None),
        check_vma=False,
    )
```

```python
import functools
import math

import jax
import jax.numpy as jnp
import numpy as np
from jax import lax
from jax.experimental import pallas as pl
from jax.experimental.pallas import tpu as pltpu
from jax.sharding import PartitionSpec as P

ITERS = 2
STEP = 0.5
F32 = jnp.float32
BF16 = jnp.bfloat16
HIGH = lax.Precision.HIGH
LANES = 256
MODEST = pltpu.CompilerParams(vmem_limit_bytes=24 << 20)


def dft_tables(length):
    index = np.arange(length)
    angle = (index[:, None] * index[None, :] % length) * (2.0 * math.pi / length)
    return np.cos(angle), np.sin(angle)


def with_halo(x, sides, width):
    for axis, dim in sides:
        count, length = lax.axis_size(axis), x.shape[dim]
        up = [(i, i + 1) for i in range(count - 1)]
        down = [(j, i) for i, j in up]
        before = lax.ppermute(lax.slice_in_dim(x, length - width, length, axis=dim), axis, up)
        after = lax.ppermute(lax.slice_in_dim(x, 0, width, axis=dim), axis, down)
        x = jnp.concatenate([before, x, after], axis=dim)
    return x


def stack_taps(padded, rows, slices, breadth):
    return jnp.concatenate(
        [
            padded[a : a + rows, b : b + slices, :, e : e + breadth]
            for a in range(3)
            for b in range(3)
            for e in range(3)
        ],
        axis=2,
    )


def tap_sum(taps, rows, slices, breadth):
    result = jnp.zeros((rows, slices, 2, breadth), F32)
    for place in range(27):
        a, b, e = place // 9, place // 3 % 3, place % 3
        result += taps[a : a + rows, b : b + slices, 2 * place : 2 * place + 2, e : e + breadth]
    return result


def regularize(damped, height, conv_first, bias_first, conv_second, bias_second):
    rows, slices, _, breadth = damped.shape
    extended = with_halo(damped.astype(BF16), (("coil", 0), ("sect", 1)), 2)
    padded = jnp.pad(extended, ((0, 0), (0, 0), (0, 0), (1, 1)))
    columns = stack_taps(padded, rows + 2, slices + 2, breadth)
    hidden = jnp.einsum("oc,rscw->rsow", conv_first, columns, preferred_element_type=F32)
    hidden = jax.nn.relu(hidden + bias_first[None, None, :, None]).astype(BF16)
    row_index = lax.axis_index("coil") * rows - 1 + jnp.arange(rows + 2)
    slice_index = lax.axis_index("sect") * slices - 1 + jnp.arange(slices + 2)
    row_valid = (row_index >= 0) & (row_index < height)
    slice_valid = (slice_index >= 0) & (slice_index < lax.axis_size("sect") * slices)
    inside = row_valid[:, None] & slice_valid[None, :]
    hidden = jnp.where(inside[:, :, None, None], hidden, jnp.zeros_like(hidden))
    hidden = jnp.pad(hidden, ((0, 0), (0, 0), (0, 0), (1, 1)))
    taps = jnp.einsum("tc,rscw->rstw", conv_second, hidden, preferred_element_type=F32)
    return tap_sum(taps, rows, slices, breadth) + bias_second[None, None, :, None]


def per_device(measured, coil_maps, sampling, conv_first, bias_first, conv_second, bias_second):
    height, coils_here, slices_here, _, breadth = coil_maps.shape
    count = lax.axis_size("coil")
    rows = height // count
    mask = sampling.astype(F32)

    def exchange(x):
        split = x.astype(BF16).reshape((count, rows) + x.shape[1:])
        return lax.all_to_all(split, "coil", 0, 0, tiled=True)

    row_cos, row_sin = dft_tables(height)
    col_cos, col_sin = dft_tables(breadth)
    row_table = jnp.asarray(np.stack([row_cos, row_sin]) / math.sqrt(height), F32)
    col_table = jnp.asarray(
        np.block([[col_cos, col_sin], [-col_sin, col_cos]]) / math.sqrt(breadth), F32
    ).reshape(2, breadth, 2, breadth)

    spread = jnp.einsum("tkh,kcsqw->tcsqwh", row_table, measured, precision=HIGH)
    spread = jnp.stack(
        [spread[0, :, :, 0] - spread[1, :, :, 1], spread[0, :, :, 1] + spread[1, :, :, 0]], axis=2
    )
    spread = spread * mask[None, :, None, :, None]
    inverse = jnp.einsum("qwpv,csqwh->csphv", col_table, spread, precision=HIGH)
    maps = jnp.transpose(coil_maps, (1, 2, 3, 0, 4))
    part_re = jnp.sum(maps[:, :, 0] * inverse[:, :, 0] + maps[:, :, 1] * inverse[:, :, 1], axis=0)
    part_im = jnp.sum(maps[:, :, 0] * inverse[:, :, 1] - maps[:, :, 1] * inverse[:, :, 0], axis=0)
    partial = jnp.transpose(jnp.stack([part_re, part_im], axis=1), (2, 0, 1, 3))
    first = jnp.sum(exchange(partial).astype(F32), axis=0)
    near = exchange(coil_maps).astype(F32)
    near_re, near_im = near[..., 0, :], near[..., 1, :]

    angle = jnp.asarray(np.stack([col_cos, col_sin]), F32)
    both = jnp.einsum("sl,alj,blv->absjv", mask, angle, angle, precision=HIGH) / breadth
    project_re = both[0, 0] + both[1, 1]
    project_im = both[0, 1] - both[1, 0]
    project = jnp.stack(
        [jnp.stack([project_re, project_im], 2), jnp.stack([-project_im, project_re], 2)]
    )

    image = first
    for _ in range(ITERS):
        image_re, image_im = image[:, :, 0], image[:, :, 1]
        product = jnp.stack(
            [near_re * image_re[:, None] - near_im * image_im[:, None],
             near_re * image_im[:, None] + near_im * image_re[:, None]]
        )
        spun = jnp.einsum("qnrcsj,qsjpv->pnrcsv", product, project, precision=HIGH)
        normal_re = jnp.sum(near_re * spun[0] + near_im * spun[1], axis=(0, 2))
        normal_im = jnp.sum(near_re * spun[1] - near_im * spun[0], axis=(0, 2))
        normal = jnp.stack([normal_re, normal_im], axis=2)
        damped = image - STEP * (normal - first)
        image = damped + regularize(
            damped, height, conv_first, bias_first, conv_second, bias_second
        )
    return image


def bf16_pair(table):
    high = table.astype(BF16)
    return high, (table - high.astype(np.float64)).astype(BF16)


def split3(x):
    high = x.astype(BF16)
    return high, (x - high.astype(F32)).astype(BF16)


def dot(x, y):
    return jnp.dot(x, y, preferred_element_type=F32)


def dot3(x, y):
    return dot(x[0], y[0]) + dot(x[1], y[0]) + dot(x[0], y[1])


def vmem(count):
    return [pl.BlockSpec(memory_space=pltpu.VMEM)] * count


def column_of(row):
    shape = (row.shape[1], row.shape[1])
    diagonal = lax.broadcasted_iota(jnp.int32, shape, 0) == lax.broadcasted_iota(jnp.int32, shape, 1)
    return jnp.sum(jnp.where(diagonal, jnp.broadcast_to(row, shape), 0.0), axis=1, keepdims=True)


def block_of(coil, sect):
    return 2 * coil + (sect + coil) % 2


def back_project(data, maps, keep, row_ref, column_ref, between):
    height = data[0].shape[1]
    breadth = data[0].shape[0] // 2
    spreads, rights = [], []
    table = jnp.concatenate([row_ref[:height], row_ref[:height], row_ref[height:]], axis=0)
    for value in data:
        high, low = split3(value)
        spreads.append(dot(jnp.concatenate([high, low, high], axis=1), table))
    between[0]()
    for spread in spreads:
        real, imag = spread[:breadth], spread[breadth:]
        pieces = [
            (real[:, :height] - imag[:, height:]) * keep, (imag[:, :height] + real[:, height:]) * keep,
        ]
        high, low = split3(jnp.concatenate(pieces, axis=1))
        rights.append(jnp.concatenate([high, low, high], axis=0))
    mixes = [dot(column_ref[...], x) for x in rights]
    between[1]()
    total_re, total_im = 0.0, 0.0
    for mixed, read in zip(mixes, maps):
        inv_re = mixed[:breadth, :height] - mixed[breadth:, height:]
        inv_im = mixed[breadth:, :height] + mixed[:breadth, height:]
        map_re, map_im = read(0), read(1)
        total_re += map_re * inv_re + map_im * inv_im
        total_im += map_re * inv_im - map_im * inv_re
    return total_re, total_im


def own_slice():
    return lax.axis_index("coil") % 2


def kept_columns(mask_ref, here):
    mask = mask_ref[...].astype(F32)
    return column_of(jnp.where(here == 0, mask[:1], mask[1:]))


def parts_of(maps_ref, c, s):
    breadth = maps_ref.shape[2] // 2
    return lambda q: maps_ref[c, s, q * breadth : (q + 1) * breadth]


def first_kernel(
    data_far, maps_far, mask_far, row_far, column_far,
    give_ref, data_ref, maps_ref, mask_ref, row_ref, column_ref, other_ref, sems,
):
    coils = data_far.shape[0]
    here = own_slice()
    there = 1 - here
    plan = [(mask_far, mask_ref), (row_far, row_ref)]
    plan += [(data_far.at[c, there], other_ref.at[c]) for c in range(coils)]
    plan += [(column_far, column_ref)]
    plan += [(maps_far.at[c, there], maps_ref.at[c, there]) for c in range(coils)]
    plan += [(data_far.at[c, here], data_ref.at[c]) for c in range(coils)]
    plan += [(maps_far.at[c, here], maps_ref.at[c, here]) for c in range(coils)]
    copies = [pltpu.make_async_copy(x, y, sems.at[i]) for i, (x, y) in enumerate(plan)]
    for copy in copies:
        copy.start()
    copies[0].wait()
    keep = kept_columns(mask_ref, there)
    for copy in copies[1 : 2 + coils]:
        copy.wait()

    def rest():
        for copy in copies[2 + coils :]:
            copy.wait()

    totals = back_project(
        [other_ref[c] for c in range(coils)], [parts_of(maps_ref, c, there) for c in range(coils)],
        keep, row_ref, column_ref, (rest, lambda: None),
    )
    breadth = totals[0].shape[0]
    for q in range(2):
        give_ref[q * breadth : (q + 1) * breadth] = totals[q]


def own_kernel(data_ref, maps_ref, mask_ref, row_ref, column_ref, send_ref, total_ref, out_copy, sems):
    coils, slices, double, height = maps_ref.shape
    breadth, wide = double // 2, slices * double // 2
    here = own_slice()
    sends = []

    def emit(c):
        turned = [
            jnp.concatenate([parts_of(maps_ref, c, s)(q) for s in range(slices)], axis=0)
            .T.reshape(height // 8, 8, wide)
            for q in range(2)
        ]
        both = jnp.concatenate(turned, axis=1).astype(BF16)
        for p in range(height // 8):
            out_copy[c, p] = both[block_of(p // 2, p % 2)]
        rows = send_ref.at[:, 16 * c : 16 * c + 16, :]
        sends.append(pltpu.make_async_copy(out_copy.at[c], rows, sems.at[c]))
        sends[-1].start()

    totals = back_project(
        [data_ref[c] for c in range(coils)], [parts_of(maps_ref, c, here) for c in range(coils)],
        kept_columns(mask_ref, here), row_ref, column_ref, (lambda: [emit(c) for c in range(coils)], lambda: None),
    )
    for q in range(2):
        total_ref[q * breadth : (q + 1) * breadth] = totals[q]
    for copy in sends:
        copy.wait()


def sum_kernel(total_ref, got_ref, mask_ref, old_ref, send_ref, mask_out_ref, out_copy, sem):
    double, height = total_ref.shape
    total = total_ref[...] + got_ref[...]
    turned = (total * jnp.abs(total)).T.reshape(height // 8, 8, double).astype(BF16)
    for p in range(height // 8):
        out_copy[p] = turned[block_of(p // 2, p % 2)]
    first = send_ref.shape[1] - 8
    copy = pltpu.make_async_copy(out_copy, send_ref.at[:, first : first + 8, :], sem)
    copy.start()
    mask_out_ref[...] = mask_ref[...].astype(F32).astype(BF16)
    copy.wait()


def table_kernel(
    own_ref, other_ref, angle_ref, first_ref, bias_ref, second_ref, pick_first_ref, pick_second_ref, place_ref,
    out_bias_ref, project_ref, first_out_ref, second_out_ref, bias_out_ref,
):
    slices, breadth = own_ref.shape
    wide = slices * breadth
    here = lax.axis_index("sect")
    angle = angle_ref[...]
    swapped = jnp.concatenate([angle[:, wide:], -angle[:, :wide]], axis=1)
    cosine, sine = angle[:, :breadth], angle[:, wide : wide + breadth]
    angle, swapped = split3(angle), split3(swapped)
    for t in range(project_ref.shape[0]):
        mask = jnp.where(here == t, own_ref[...].astype(F32), other_ref[...].astype(F32))
        for s in range(slices):
            row = mask[s : s + 1]
            block = dot3(split3(cosine * row), angle) + dot3(split3(sine * row), swapped)
            if s:
                block = pltpu.roll(block, s * breadth, 1)
            rows = slice(s * breadth, (s + 1) * breadth)
            project_ref[t, rows] = block.astype(BF16)
            rows = slice(wide + s * breadth, wide + (s + 1) * breadth)
            project_ref[t, rows] = jnp.concatenate([-block[:, wide:], block[:, :wide]], axis=1).astype(BF16)

    odd = lax.broadcasted_iota(jnp.int32, bias_out_ref.shape, 0) % 2 == 1
    inside = lax.broadcasted_iota(jnp.int32, bias_out_ref.shape, 1) < breadth
    bias_out_ref[...] = jnp.where(inside, jnp.where(odd, out_bias_ref[1], out_bias_ref[0]), 0.0)

    groups, _, depth = pick_first_ref.shape
    features = first_ref.shape[1]
    bias = column_of(bias_ref[...])
    parts = []
    for _ in range(3):
        parts.append(bias.astype(BF16).astype(F32))
        bias = bias - parts[-1]
    lane = lax.broadcasted_iota(jnp.int32, (features, depth), 1)
    second = 0.0
    for s in range(groups):
        block = lax.dot_general(
            first_ref[...], pick_first_ref[s], (((0,), (0,)), ((), ())), preferred_element_type=F32
        )
        for i in range(3):
            block = jnp.where(lane == depth - 8 + i, parts[i], block)
        first_out_ref[s * features : (s + 1) * features] = block.astype(BF16)
        second += dot(dot(pick_second_ref[s], second_ref[...]).astype(BF16), place_ref[s])
    second_out_ref[...] = second.astype(BF16)


def apply_data_term(near_ref, project_ref, image, start, left_ref, spun_ref, breadth):
    coils, groups = near_ref.shape[0], near_ref.shape[1]
    wide = near_ref.shape[3]

    def maps_of(i, t, c):
        maps = near_ref[i, t, 16 * c : 16 * c + 16, :].astype(F32)
        return maps[:8], maps[8:]

    for t in range(groups):
        image_re, image_im = image[t][:8], image[t][8:]
        for i in range(coils):
            reals, imags = [], []
            for c in range(2):
                map_re, map_im = maps_of(i, t, c)
                reals.append(map_re * image_re - map_im * image_im)
                imags.append(map_re * image_im + map_im * image_re)
            left_ref[t, 16 * i : 16 * i + 16, :wide] = jnp.concatenate(reals, axis=0).astype(BF16)
            left_ref[t, 16 * i : 16 * i + 16, wide:] = jnp.concatenate(imags, axis=0).astype(BF16)
        spun_ref[t] = dot(left_ref[t], project_ref[t])
    result = []
    for t in range(groups):
        sum_re, sum_im = 0.0, 0.0
        for i in range(coils):
            for c in range(2):
                map_re, map_im = maps_of(i, t, c)
                rows = slice(16 * i + 8 * c, 16 * i + 8 * c + 8)
                spun_re, spun_im = spun_ref[t, rows, :wide], spun_ref[t, rows, wide:]
                sum_re += map_re * spun_re + map_im * spun_im
                sum_im += map_re * spun_im - map_im * spun_re
        normal = jnp.concatenate([sum_re, sum_im], axis=0)
        result.append(image[t] - STEP * (normal * (1.0 / breadth) - start[t]))
    return result


def to_rows(damped, out_ref, flip_ref, breadth):
    per_group = damped[0].shape[1] // breadth
    wide = damped[0].shape[1]
    lanes = lax.broadcasted_iota(jnp.int32, (16, LANES), 1)
    for t, value in enumerate(damped):
        for s in range(per_group):
            moved = value if s == 0 else pltpu.roll(value, wide - s * breadth, 1)
            moved = jnp.where(lanes < breadth, moved[:, :LANES], 0.0)
            for q in range(2):
                place = (t * per_group + s) * 2 + q
                for j in range(2):
                    part = moved[8 * q : 8 * q + 8, 128 * j : 128 * j + 128]
                    flip_ref[pl.ds(64 * j + place, 8, stride=8), :] = part
    for j in range(2):
        out_ref[:, 128 * j : 128 * j + 128] = flip_ref[64 * j : 64 * j + 64]


def from_rows(flip_ref, groups, per_group, breadth):
    wide = per_group * breadth
    result = []
    for t in range(groups):
        parts = []
        for q in range(2):
            value = jnp.zeros((8, wide), F32)
            for s in range(per_group):
                place = (t * per_group + s) * 2 + q
                halves = [flip_ref[pl.ds(64 * j + place, 8, stride=8), :] for j in range(2)]
                piece = jnp.concatenate(halves + [jnp.zeros((8, wide - LANES), F32)], axis=1)
                value += piece if s == 0 else pltpu.roll(piece, s * breadth, 1)
            parts.append(value)
        result.append(jnp.concatenate(parts, axis=0))
    return result


def position_of():
    return block_of(lax.axis_index("coil"), lax.axis_index("sect"))


def write_edges(rows_ref, inner_ref, outer_ref):
    odd = position_of() % 2 == 1
    low, high = rows_ref[:16], rows_ref[48:64]
    inner_ref[...] = jnp.where(odd, low, high).astype(BF16)
    outer_ref[...] = jnp.where(odd, high, low).astype(BF16)


def keep_close(*arrays):
    return [pltpu.with_memory_space_constraint(x, pltpu.VMEM) for x in arrays]


def signed_root(value):
    root = jnp.sqrt(jnp.abs(value))
    return jnp.where(value < 0.0, -root, root)


def second_kernel(
    near_ref, project_ref, rows_ref, inner_ref, outer_ref, start_ref,
    flip_ref, left_ref, spun_ref, *, breadth,
):
    coils, groups, _, wide = near_ref.shape
    start = []
    first = lax.broadcasted_iota(jnp.int32, (8, wide), 1) < breadth
    for t in range(groups):
        def add(i, totals, t=t):
            return tuple(x + signed_root(near_ref[2 * i + s, t, 32:40, :].astype(F32)) for s, x in enumerate(totals))

        zero = jnp.zeros((8, wide), F32)
        low, high = lax.fori_loop(0, coils // 2, add, (zero, zero), unroll=4)
        parts = [
            jnp.where(first, low, pltpu.roll(high, breadth, 1)),
            jnp.where(first, pltpu.roll(low, breadth, 1), high),
        ]
        start.append(jnp.concatenate(parts, axis=0))
        start_ref[t] = start[t]
    damped = apply_data_term(near_ref, project_ref, start, start, left_ref, spun_ref, breadth)
    to_rows(damped, rows_ref, flip_ref, breadth)
    write_edges(rows_ref, inner_ref, outer_ref)


def tap_blocks(values, places, first_ref, second_ref, shift_ref, breadth):
    for h, value in values.items():
        shift_ref[24 * h : 24 * h + 8] = pltpu.roll(value, 1, 1)
        shift_ref[24 * h + 8 : 24 * h + 16] = value
        shift_ref[24 * h + 16 : 24 * h + 24] = pltpu.roll(value, LANES - 1, 1)
    ones = jnp.ones((8, LANES), F32)
    hidden = {}
    for g in places:
        columns = jnp.concatenate([shift_ref[24 * g : 24 * g + 72], ones], axis=0).astype(BF16)
        block = dot(first_ref[...], columns).astype(BF16)
        hidden[g] = jnp.maximum(block, jnp.zeros_like(block))
    inside = lax.broadcasted_iota(jnp.int32, (1, LANES), 1) < breadth
    return {g: jnp.where(inside, dot(second_ref[...], hidden[g]), 0.0) for g in places}


def inner_kernel(rows_ref, first_ref, second_ref, taps_ref, shift_ref, *, breadth):
    values = {h: rows_ref[8 * h : 8 * h + 8] for h in range(8)}
    for g, tap in tap_blocks(values, range(6), first_ref, second_ref, shift_ref, breadth).items():
        taps_ref[g] = tap


def edge_rows(first, second):
    value = jnp.where(position_of() % 2 == 1, first.astype(F32), second.astype(F32))
    return [value[:8], value[8:]]


def regularized(
    rows_ref, taps_ref, inner_ref, outer_ref, first_ref, second_ref, bias_ref, shift_ref, breadth
):
    inner, outer = inner_ref[...], outer_ref[...]
    own = [rows_ref[8 * h : 8 * h + 8] for h in range(8)]
    values = edge_rows(inner, outer) + own + edge_rows(outer, inner)
    taps = tap_blocks(
        {h: values[h] for h in (0, 1, 2, 3, 8, 9, 10, 11)}, (0, 1, 8, 9), first_ref, second_ref, shift_ref, breadth
    )
    taps.update({g + 2: taps_ref[g] for g in range(6)})
    last = 2 * lax.axis_size("coil") - 1
    taps[0] = jnp.where(position_of() > 0, taps[0], 0.0)
    taps[9] = jnp.where(position_of() < last, taps[9], 0.0)
    lanes = lax.broadcasted_iota(jnp.int32, (1, LANES), 1)
    bias = bias_ref[...]
    updates = []
    for h in range(8):
        total = taps[h][:24] + taps[h + 1][24:48] + taps[h + 2][48:]
        update = pltpu.roll(total[:8], 1, 1) + total[8:16] + pltpu.roll(total[16:], LANES - 1, 1)
        updates.append(jnp.where(lanes < breadth, update, 0.0) + bias)
    return own, updates


def third_kernel(
    rows_ref, taps_ref, inner_ref, outer_ref, first_ref, second_ref, bias_ref, near_ref, project_ref, start_ref,
    out_ref, inner_out_ref, outer_out_ref,
    shift_ref, flip_ref, left_ref, spun_ref, *, breadth,
):
    groups, _, wide = start_ref.shape
    own, updates = regularized(
        rows_ref, taps_ref, inner_ref, outer_ref, first_ref, second_ref, bias_ref, shift_ref, breadth
    )
    for h in range(8):
        image = own[h] + updates[h]
        for j in range(2):
            flip_ref[64 * j + 8 * h : 64 * j + 8 * h + 8] = image[:, 128 * j : 128 * j + 128]
    image = from_rows(flip_ref, groups, wide // breadth, breadth)
    start = [start_ref[t] for t in range(groups)]
    damped = apply_data_term(near_ref, project_ref, image, start, left_ref, spun_ref, breadth)
    to_rows(damped, out_ref, flip_ref, breadth)
    write_edges(out_ref, inner_out_ref, outer_out_ref)


def last_kernel(
    rows_ref, taps_ref, inner_ref, outer_ref, first_ref, second_ref, bias_ref, keep_ref, give_ref,
    shift_ref, *, breadth,
):
    own, updates = regularized(
        rows_ref, taps_ref, inner_ref, outer_ref, first_ref, second_ref, bias_ref, shift_ref, breadth
    )
    upper = lax.axis_index("sect") == 0
    for h in range(8):
        image = (own[h] + updates[h])[:, :breadth]
        keep, give = jnp.where(upper, image[:4], image[4:]), jnp.where(upper, image[4:], image[:4])
        for s in range(2):
            keep_ref[h, s] = keep[2 * s : 2 * s + 2]
            give_ref[h, s] = give[2 * s : 2 * s + 2]


def join_kernel(keep_ref, got_ref, out_ref, sems):
    place = position_of() % 2
    copies = [
        pltpu.make_async_copy(x, out_ref.at[pl.ds(8 * y, 8)], sems.at[i])
        for i, (x, y) in enumerate(((keep_ref, place), (got_ref, 1 - place)))
    ]
    for copy in copies:
        copy.start()
    for copy in copies:
        copy.wait()


def fast_device(measured, coil_maps, sampling, conv_first, bias_first, conv_second, bias_second):
    height, coils_here, slices_here, _, breadth = coil_maps.shape
    ranks, sects = lax.axis_size("coil"), lax.axis_size("sect")
    count = ranks * sects
    slices = slices_here * sects
    wide = slices_here * breadth
    features = conv_first.shape[0]
    both = ("coil", "sect")
    f32 = lambda *dims: jax.ShapeDtypeStruct(dims, F32)
    bf16 = lambda *dims: jax.ShapeDtypeStruct(dims, BF16)

    row_cos, row_sin = dft_tables(height)
    col_cos, col_sin = dft_tables(breadth)
    row_high, row_low = bf16_pair(np.concatenate([row_cos, row_sin], axis=1) / math.sqrt(height))
    column_high, column_low = bf16_pair(np.concatenate([col_cos, col_sin], axis=0) / math.sqrt(breadth))
    row_table = jnp.asarray(np.concatenate([row_high, row_low], axis=0))
    column_table = jnp.asarray(np.concatenate([column_high, column_high, column_low], axis=1))
    by_coil = lambda x: jnp.transpose(x, (1, 2, 3, 4, 0)).reshape(coils_here, slices_here, 2 * breadth, height)
    block_rows = 16 * coils_here + 8
    far = (by_coil(measured), by_coil(coil_maps), sampling, row_table, column_table)
    double = 2 * breadth
    anywhere = pl.BlockSpec(memory_space=pl.ANY)
    roomy = pltpu.CompilerParams(vmem_limit_bytes=40 << 20)
    give, *fetched = pl.pallas_call(
        first_kernel, compiler_params=roomy,
        in_specs=[anywhere] * 5, out_specs=vmem(6),
        out_shape=[
            f32(double, height), pltpu.VMEM((coils_here, double, height), F32),
            *[pltpu.VMEM(x.shape, x.dtype) for x in far[1:]],
        ],
        scratch_shapes=[
            pltpu.VMEM((coils_here, double, height), F32), pltpu.SemaphoreType.DMA((3 + 4 * coils_here,)),
        ],
    )(*[pltpu.with_memory_space_constraint(x, pltpu.HBM) for x in far])
    got = lax.ppermute(give, "coil", [(i, i ^ 1) for i in range(ranks)])
    send, total = pl.pallas_call(
        own_kernel, compiler_params=roomy,
        in_specs=vmem(5), out_specs=[anywhere] + vmem(1),
        out_shape=[bf16(count, block_rows, wide), pltpu.VMEM((double, height), F32)],
        scratch_shapes=[pltpu.VMEM((coils_here, count, 16, wide), BF16), pltpu.SemaphoreType.DMA((coils_here,))],
    )(*keep_close(*fetched))
    send, mask = pl.pallas_call(
        sum_kernel, compiler_params=MODEST,
        in_specs=vmem(3) + [anywhere], out_specs=[anywhere] + vmem(1),
        out_shape=[bf16(count, block_rows, wide), bf16(slices_here, breadth)],
        input_output_aliases={3: 0},
        scratch_shapes=[pltpu.VMEM((count, 8, wide), BF16), pltpu.SemaphoreType.DMA],
    )(*keep_close(total, got, fetched[2]), send)
    near = lax.all_to_all(send, both, 0, 0, tiled=True).reshape(ranks, sects, block_rows, wide)

    other = lax.ppermute(mask, "sect", [(0, 1), (1, 0)])
    blank = np.zeros((breadth, wide - breadth))
    angle = np.concatenate([col_cos, blank, col_sin, blank], axis=1).astype(np.float32)
    span = 18 * slices
    pick_first = np.zeros((slices, 54, span + 8))
    pick_second = np.zeros((slices, span, 54))
    for a, b, e, q, s in np.ndindex(3, 3, 3, 2, slices):
        tap = 2 * (9 * a + 3 * b + e) + q
        if 0 <= s + b - 1 < slices:
            pick_first[s, tap, ((a * 3 + e) * slices + s + b - 1) * 2 + q] = 1.0
            pick_second[s + b - 1, ((a * 3 + e) * slices + s) * 2 + q, tap] = 1.0
    place = np.eye(slices * features).reshape(slices, features, slices * features)
    project, matrix_first, matrix_second, bias = pl.pallas_call(
        table_kernel,
        compiler_params=MODEST,
        in_specs=vmem(9) + [pl.BlockSpec(memory_space=pltpu.SMEM)], out_specs=vmem(4),
        out_shape=[
            pltpu.VMEM(dims, BF16)
            for dims in (
                (sects, 2 * wide, 2 * wide), (slices * features, span + 8), (span, slices * features),
            )
        ] + [pltpu.VMEM((2 * slices, LANES), F32)],
    )(
        mask, other, jnp.asarray(angle), conv_first.T, bias_first.reshape(1, features), conv_second,
        *[jnp.asarray(x.astype(BF16)) for x in (pick_first, pick_second, place)], bias_second,
    )
    weights = keep_close(matrix_first, matrix_second, bias)
    weight_specs = vmem(3)

    owner = {block_of(i, y): 2 * i + y for i in range(ranks) for y in range(2)}
    near_pairs = []
    for block in range(1, count - 1, 2):
        near_pairs += [(owner[block], owner[block + 1]), (owner[block + 1], owner[block])]
    swap = lambda x: lax.ppermute(x, "sect", [(0, 1), (1, 0)])

    edge = 4 * slices
    work = [
        pltpu.VMEM((32 * slices, 128), F32),
        pltpu.VMEM((sects, 16 * ranks, 2 * wide), BF16), pltpu.VMEM((sects, 16 * ranks, 2 * wide), F32),
    ]

    shift = [pltpu.VMEM((12 * 6 * slices, LANES), F32)]

    def around(rows, inner, outer):
        taps = pl.pallas_call(
            functools.partial(inner_kernel, breadth=breadth),
            compiler_params=MODEST, in_specs=vmem(3), out_specs=vmem(1)[0],
            out_shape=pltpu.VMEM((6, 18 * slices, LANES), F32), scratch_shapes=shift,
        )(*keep_close(rows), *weights[:2])
        return keep_close(rows, taps, swap(inner), lax.ppermute(outer, both, near_pairs))

    row_shapes = [f32(16 * slices, LANES), bf16(edge, LANES), bf16(edge, LANES)]
    rows, inner, outer, start = pl.pallas_call(
        functools.partial(second_kernel, breadth=breadth),
        compiler_params=MODEST,
        in_specs=vmem(2), out_specs=vmem(4),
        out_shape=row_shapes + [pltpu.VMEM((sects, 16, wide), F32)], scratch_shapes=work,
    )(*keep_close(near, project))
    for _ in range(ITERS - 1):
        rows, inner, outer = pl.pallas_call(
            functools.partial(third_kernel, breadth=breadth),
            compiler_params=MODEST,
            in_specs=vmem(4) + weight_specs + vmem(3), out_specs=vmem(3), out_shape=row_shapes,
            scratch_shapes=shift + work,
        )(*around(rows, inner, outer), *weights, *keep_close(near, project, start))
    piece = f32(8, slices_here, 2, breadth)
    keep, give = pl.pallas_call(
        functools.partial(last_kernel, breadth=breadth),
        compiler_params=MODEST,
        in_specs=vmem(4) + weight_specs, out_specs=vmem(2), out_shape=[piece, piece],
        scratch_shapes=shift,
    )(*around(rows, inner, outer), *weights)
    return pl.pallas_call(
        join_kernel, compiler_params=MODEST, in_specs=vmem(2), out_specs=anywhere,
        out_shape=f32(16, slices_here, 2, breadth), scratch_shapes=[pltpu.SemaphoreType.DMA((2,))],
    )(*keep_close(keep, swap(give)))


def per_device_any(measured, coil_maps, *rest):
    height, coils_here, slices_here, _, breadth = coil_maps.shape
    ranks, sects = lax.axis_size("coil"), lax.axis_size("sect")
    fits = (
        sects == 2 and slices_here == 2 and coils_here == 2 and height == 8 * ranks * sects
        and 2 * breadth % 128 == 0 and 128 < breadth < LANES and breadth % 16 == 0
    )
    return (fast_device if fits else per_device)(measured, coil_maps, *rest)


def solution(mesh):
    coil_spec = P(None, "coil", "sect", None, None)
    in_specs = (coil_spec, coil_spec, P("sect", None), P(), P(), P(), P())
    return jax.shard_map(
        per_device_any,
        mesh=mesh,
        in_specs=in_specs,
        out_specs=P("coil", "sect", None, None),
        check_vma=False,
    )
```

```python
import functools
import math

import jax
import jax.numpy as jnp
import numpy as np
from jax import lax
from jax.experimental import pallas as pl
from jax.experimental.pallas import tpu as pltpu
from jax.sharding import PartitionSpec as P

ITERS = 2
STEP = 0.5
F32 = jnp.float32
BF16 = jnp.bfloat16
HIGH = lax.Precision.HIGH
LANES = 256
MODEST = pltpu.CompilerParams(vmem_limit_bytes=24 << 20)


def dft_tables(length):
    index = np.arange(length)
    angle = (index[:, None] * index[None, :] % length) * (2.0 * math.pi / length)
    return np.cos(angle), np.sin(angle)


def with_halo(x, sides, width):
    for axis, dim in sides:
        count, length = lax.axis_size(axis), x.shape[dim]
        up = [(i, i + 1) for i in range(count - 1)]
        down = [(j, i) for i, j in up]
        before = lax.ppermute(lax.slice_in_dim(x, length - width, length, axis=dim), axis, up)
        after = lax.ppermute(lax.slice_in_dim(x, 0, width, axis=dim), axis, down)
        x = jnp.concatenate([before, x, after], axis=dim)
    return x


def stack_taps(padded, rows, slices, breadth):
    return jnp.concatenate(
        [
            padded[a : a + rows, b : b + slices, :, e : e + breadth]
            for a in range(3)
            for b in range(3)
            for e in range(3)
        ],
        axis=2,
    )


def tap_sum(taps, rows, slices, breadth):
    result = jnp.zeros((rows, slices, 2, breadth), F32)
    for place in range(27):
        a, b, e = place // 9, place // 3 % 3, place % 3
        result += taps[a : a + rows, b : b + slices, 2 * place : 2 * place + 2, e : e + breadth]
    return result


def regularize(damped, height, conv_first, bias_first, conv_second, bias_second):
    rows, slices, _, breadth = damped.shape
    extended = with_halo(damped.astype(BF16), (("coil", 0), ("sect", 1)), 2)
    padded = jnp.pad(extended, ((0, 0), (0, 0), (0, 0), (1, 1)))
    columns = stack_taps(padded, rows + 2, slices + 2, breadth)
    hidden = jnp.einsum("oc,rscw->rsow", conv_first, columns, preferred_element_type=F32)
    hidden = jax.nn.relu(hidden + bias_first[None, None, :, None]).astype(BF16)
    row_index = lax.axis_index("coil") * rows - 1 + jnp.arange(rows + 2)
    slice_index = lax.axis_index("sect") * slices - 1 + jnp.arange(slices + 2)
    row_valid = (row_index >= 0) & (row_index < height)
    slice_valid = (slice_index >= 0) & (slice_index < lax.axis_size("sect") * slices)
    inside = row_valid[:, None] & slice_valid[None, :]
    hidden = jnp.where(inside[:, :, None, None], hidden, jnp.zeros_like(hidden))
    hidden = jnp.pad(hidden, ((0, 0), (0, 0), (0, 0), (1, 1)))
    taps = jnp.einsum("tc,rscw->rstw", conv_second, hidden, preferred_element_type=F32)
    return tap_sum(taps, rows, slices, breadth) + bias_second[None, None, :, None]


def per_device(measured, coil_maps, sampling, conv_first, bias_first, conv_second, bias_second):
    height, coils_here, slices_here, _, breadth = coil_maps.shape
    count = lax.axis_size("coil")
    rows = height // count
    mask = sampling.astype(F32)

    def exchange(x):
        split = x.astype(BF16).reshape((count, rows) + x.shape[1:])
        return lax.all_to_all(split, "coil", 0, 0, tiled=True)

    row_cos, row_sin = dft_tables(height)
    col_cos, col_sin = dft_tables(breadth)
    row_table = jnp.asarray(np.stack([row_cos, row_sin]) / math.sqrt(height), F32)
    col_table = jnp.asarray(
        np.block([[col_cos, col_sin], [-col_sin, col_cos]]) / math.sqrt(breadth), F32
    ).reshape(2, breadth, 2, breadth)

    spread = jnp.einsum("tkh,kcsqw->tcsqwh", row_table, measured, precision=HIGH)
    spread = jnp.stack(
        [spread[0, :, :, 0] - spread[1, :, :, 1], spread[0, :, :, 1] + spread[1, :, :, 0]], axis=2
    )
    spread = spread * mask[None, :, None, :, None]
    inverse = jnp.einsum("qwpv,csqwh->csphv", col_table, spread, precision=HIGH)
    maps = jnp.transpose(coil_maps, (1, 2, 3, 0, 4))
    part_re = jnp.sum(maps[:, :, 0] * inverse[:, :, 0] + maps[:, :, 1] * inverse[:, :, 1], axis=0)
    part_im = jnp.sum(maps[:, :, 0] * inverse[:, :, 1] - maps[:, :, 1] * inverse[:, :, 0], axis=0)
    partial = jnp.transpose(jnp.stack([part_re, part_im], axis=1), (2, 0, 1, 3))
    first = jnp.sum(exchange(partial).astype(F32), axis=0)
    near = exchange(coil_maps).astype(F32)
    near_re, near_im = near[..., 0, :], near[..., 1, :]

    angle = jnp.asarray(np.stack([col_cos, col_sin]), F32)
    both = jnp.einsum("sl,alj,blv->absjv", mask, angle, angle, precision=HIGH) / breadth
    project_re = both[0, 0] + both[1, 1]
    project_im = both[0, 1] - both[1, 0]
    project = jnp.stack(
        [jnp.stack([project_re, project_im], 2), jnp.stack([-project_im, project_re], 2)]
    )

    image = first
    for _ in range(ITERS):
        image_re, image_im = image[:, :, 0], image[:, :, 1]
        product = jnp.stack(
            [near_re * image_re[:, None] - near_im * image_im[:, None],
             near_re * image_im[:, None] + near_im * image_re[:, None]]
        )
        spun = jnp.einsum("qnrcsj,qsjpv->pnrcsv", product, project, precision=HIGH)
        normal_re = jnp.sum(near_re * spun[0] + near_im * spun[1], axis=(0, 2))
        normal_im = jnp.sum(near_re * spun[1] - near_im * spun[0], axis=(0, 2))
        normal = jnp.stack([normal_re, normal_im], axis=2)
        damped = image - STEP * (normal - first)
        image = damped + regularize(
            damped, height, conv_first, bias_first, conv_second, bias_second
        )
    return image


def bf16_pair(table):
    high = table.astype(BF16)
    return high, (table - high.astype(np.float64)).astype(BF16)


def split3(x):
    high = x.astype(BF16)
    return high, (x - high.astype(F32)).astype(BF16)


def dot(x, y):
    return jnp.dot(x, y, preferred_element_type=F32)


def dot3(x, y):
    return dot(x[0], y[0]) + dot(x[1], y[0]) + dot(x[0], y[1])


def vmem(count):
    return [pl.BlockSpec(memory_space=pltpu.VMEM)] * count


def column_of(row):
    shape = (row.shape[1], row.shape[1])
    diagonal = lax.broadcasted_iota(jnp.int32, shape, 0) == lax.broadcasted_iota(jnp.int32, shape, 1)
    return jnp.sum(jnp.where(diagonal, jnp.broadcast_to(row, shape), 0.0), axis=1, keepdims=True)


def block_of(coil, sect):
    return 2 * coil + (sect + coil) % 2


def back_project(data, maps, keep, row_ref, column_ref, between):
    height = data[0].shape[1]
    breadth = data[0].shape[0] // 2
    spreads, rights = [], []
    table = jnp.concatenate([row_ref[:height], row_ref[:height], row_ref[height:]], axis=0)
    for value in data:
        high, low = split3(value)
        spreads.append(dot(jnp.concatenate([high, low, high], axis=1), table))
    between[0]()
    for spread in spreads:
        real, imag = spread[:breadth], spread[breadth:]
        pieces = [
            (real[:, :height] - imag[:, height:]) * keep, (imag[:, :height] + real[:, height:]) * keep,
        ]
        high, low = split3(jnp.concatenate(pieces, axis=1))
        rights.append(jnp.concatenate([high, low, high], axis=0))
    mixes = [dot(column_ref[...], x) for x in rights]
    between[1]()
    total_re, total_im = 0.0, 0.0
    for mixed, read in zip(mixes, maps):
        inv_re = mixed[:breadth, :height] - mixed[breadth:, height:]
        inv_im = mixed[breadth:, :height] + mixed[:breadth, height:]
        map_re, map_im = read(0), read(1)
        total_re += map_re * inv_re + map_im * inv_im
        total_im += map_re * inv_im - map_im * inv_re
    return total_re, total_im


def own_slice():
    return lax.axis_index("coil") % 2


def kept_columns(mask_ref, here):
    mask = mask_ref[...].astype(F32)
    return column_of(jnp.where(here == 0, mask[:1], mask[1:]))


def parts_of(maps_ref, c, s):
    breadth = maps_ref.shape[2] // 2
    return lambda q: maps_ref[c, s, q * breadth : (q + 1) * breadth]


def first_kernel(
    data_far, maps_far, mask_far, row_far, column_far,
    give_ref, data_ref, maps_ref, mask_ref, row_ref, column_ref, other_ref, sems,
):
    coils = data_far.shape[0]
    here = own_slice()
    there = 1 - here
    plan = [(mask_far, mask_ref), (row_far, row_ref)]
    plan += [(data_far.at[c, there], other_ref.at[c]) for c in range(coils)]
    plan += [(column_far, column_ref)]
    plan += [(maps_far.at[c, there], maps_ref.at[c, there]) for c in range(coils)]
    plan += [(data_far.at[c, here], data_ref.at[c]) for c in range(coils)]
    plan += [(maps_far.at[c, here], maps_ref.at[c, here]) for c in range(coils)]
    copies = [pltpu.make_async_copy(x, y, sems.at[i]) for i, (x, y) in enumerate(plan)]
    for copy in copies:
        copy.start()
    copies[0].wait()
    keep = kept_columns(mask_ref, there)
    for copy in copies[1 : 2 + coils]:
        copy.wait()

    def rest():
        for copy in copies[2 + coils :]:
            copy.wait()

    totals = back_project(
        [other_ref[c] for c in range(coils)], [parts_of(maps_ref, c, there) for c in range(coils)],
        keep, row_ref, column_ref, (rest, lambda: None),
    )
    breadth = totals[0].shape[0]
    for q in range(2):
        give_ref[q * breadth : (q + 1) * breadth] = totals[q]


def own_kernel(data_ref, maps_ref, mask_ref, row_ref, column_ref, send_ref, total_ref, out_copy, sems):
    coils, slices, double, height = maps_ref.shape
    breadth, wide = double // 2, slices * double // 2
    here = own_slice()
    sends = []

    def emit(c):
        turned = [
            jnp.concatenate([parts_of(maps_ref, c, s)(q) for s in range(slices)], axis=0)
            .T.reshape(height // 8, 8, wide)
            for q in range(2)
        ]
        both = jnp.concatenate(turned, axis=1).astype(BF16)
        for p in range(height // 8):
            out_copy[c, p] = both[block_of(p // 2, p % 2)]
        rows = send_ref.at[:, 16 * c : 16 * c + 16, :]
        sends.append(pltpu.make_async_copy(out_copy.at[c], rows, sems.at[c]))
        sends[-1].start()

    totals = back_project(
        [data_ref[c] for c in range(coils)], [parts_of(maps_ref, c, here) for c in range(coils)],
        kept_columns(mask_ref, here), row_ref, column_ref, (lambda: [emit(c) for c in range(coils)], lambda: None),
    )
    for q in range(2):
        total_ref[q * breadth : (q + 1) * breadth] = totals[q]
    for copy in sends:
        copy.wait()


def sum_kernel(total_ref, got_ref, mask_ref, old_ref, send_ref, mask_out_ref, out_copy, sem):
    double, height = total_ref.shape
    total = total_ref[...] + got_ref[...]
    turned = (total * jnp.abs(total)).T.reshape(height // 8, 8, double).astype(BF16)
    for p in range(height // 8):
        out_copy[p] = turned[block_of(p // 2, p % 2)]
    first = send_ref.shape[1] - 8
    copy = pltpu.make_async_copy(out_copy, send_ref.at[:, first : first + 8, :], sem)
    copy.start()
    mask_out_ref[...] = mask_ref[...].astype(F32).astype(BF16)
    copy.wait()


def table_kernel(
    own_ref, other_ref, angle_ref, first_ref, bias_ref, second_ref, pick_first_ref, pick_second_ref, place_ref,
    out_bias_ref, project_ref, first_out_ref, second_out_ref, bias_out_ref,
):
    slices, breadth = own_ref.shape
    wide = slices * breadth
    here = lax.axis_index("sect")
    angle = angle_ref[...]
    swapped = jnp.concatenate([angle[:, wide:], -angle[:, :wide]], axis=1)
    cosine, sine = angle[:, :breadth], angle[:, wide : wide + breadth]
    angle, swapped = split3(angle), split3(swapped)
    for t in range(project_ref.shape[0]):
        mask = jnp.where(here == t, own_ref[...].astype(F32), other_ref[...].astype(F32))
        for s in range(slices):
            row = mask[s : s + 1]
            block = dot3(split3(cosine * row), angle) + dot3(split3(sine * row), swapped)
            if s:
                block = pltpu.roll(block, s * breadth, 1)
            rows = slice(s * breadth, (s + 1) * breadth)
            project_ref[t, rows] = block.astype(BF16)
            rows = slice(wide + s * breadth, wide + (s + 1) * breadth)
            project_ref[t, rows] = jnp.concatenate([-block[:, wide:], block[:, :wide]], axis=1).astype(BF16)

    odd = lax.broadcasted_iota(jnp.int32, bias_out_ref.shape, 0) % 2 == 1
    inside = lax.broadcasted_iota(jnp.int32, bias_out_ref.shape, 1) < breadth
    bias_out_ref[...] = jnp.where(inside, jnp.where(odd, out_bias_ref[1], out_bias_ref[0]), 0.0)

    groups, _, depth = pick_first_ref.shape
    features = first_ref.shape[1]
    bias = column_of(bias_ref[...])
    parts = []
    for _ in range(3):
        parts.append(bias.astype(BF16).astype(F32))
        bias = bias - parts[-1]
    lane = lax.broadcasted_iota(jnp.int32, (features, depth), 1)
    second = 0.0
    for s in range(groups):
        block = lax.dot_general(
            first_ref[...], pick_first_ref[s], (((0,), (0,)), ((), ())), preferred_element_type=F32
        )
        for i in range(3):
            block = jnp.where(lane == depth - 8 + i, parts[i], block)
        first_out_ref[s * features : (s + 1) * features] = block.astype(BF16)
        second += dot(dot(pick_second_ref[s], second_ref[...]).astype(BF16), place_ref[s])
    second_out_ref[...] = second.astype(BF16)


def apply_data_term(near_ref, project_ref, image, start, left_ref, spun_ref, breadth):
    coils, groups = near_ref.shape[0], near_ref.shape[1]
    wide = near_ref.shape[3]

    def maps_of(i, t, c):
        maps = near_ref[i, t, 16 * c : 16 * c + 16, :].astype(F32)
        return maps[:8], maps[8:]

    for t in range(groups):
        image_re, image_im = image[t][:8], image[t][8:]
        for i in range(coils):
            reals, imags = [], []
            for c in range(2):
                map_re, map_im = maps_of(i, t, c)
                reals.append(map_re * image_re - map_im * image_im)
                imags.append(map_re * image_im + map_im * image_re)
            left_ref[t, 16 * i : 16 * i + 16, :wide] = jnp.concatenate(reals, axis=0).astype(BF16)
            left_ref[t, 16 * i : 16 * i + 16, wide:] = jnp.concatenate(imags, axis=0).astype(BF16)
        spun_ref[t] = dot(left_ref[t], project_ref[t])
    result = []
    for t in range(groups):
        sum_re, sum_im = 0.0, 0.0
        for i in range(coils):
            for c in range(2):
                map_re, map_im = maps_of(i, t, c)
                rows = slice(16 * i + 8 * c, 16 * i + 8 * c + 8)
                spun_re, spun_im = spun_ref[t, rows, :wide], spun_ref[t, rows, wide:]
                sum_re += map_re * spun_re + map_im * spun_im
                sum_im += map_re * spun_im - map_im * spun_re
        normal = jnp.concatenate([sum_re, sum_im], axis=0)
        result.append(image[t] - STEP * (normal * (1.0 / breadth) - start[t]))
    return result


def to_rows(damped, out_ref, flip_ref, breadth):
    per_group = damped[0].shape[1] // breadth
    wide = damped[0].shape[1]
    lanes = lax.broadcasted_iota(jnp.int32, (16, LANES), 1)
    for t, value in enumerate(damped):
        for s in range(per_group):
            moved = value if s == 0 else pltpu.roll(value, wide - s * breadth, 1)
            moved = jnp.where(lanes < breadth, moved[:, :LANES], 0.0)
            for q in range(2):
                place = (t * per_group + s) * 2 + q
                for j in range(2):
                    part = moved[8 * q : 8 * q + 8, 128 * j : 128 * j + 128]
                    flip_ref[pl.ds(64 * j + place, 8, stride=8), :] = part
    for j in range(2):
        out_ref[:, 128 * j : 128 * j + 128] = flip_ref[64 * j : 64 * j + 64]


def from_rows(flip_ref, groups, per_group, breadth):
    wide = per_group * breadth
    result = []
    for t in range(groups):
        parts = []
        for q in range(2):
            value = jnp.zeros((8, wide), F32)
            for s in range(per_group):
                place = (t * per_group + s) * 2 + q
                halves = [flip_ref[pl.ds(64 * j + place, 8, stride=8), :] for j in range(2)]
                piece = jnp.concatenate(halves + [jnp.zeros((8, wide - LANES), F32)], axis=1)
                value += piece if s == 0 else pltpu.roll(piece, s * breadth, 1)
            parts.append(value)
        result.append(jnp.concatenate(parts, axis=0))
    return result


def position_of():
    return block_of(lax.axis_index("coil"), lax.axis_index("sect"))


def write_edges(rows_ref, inner_ref, outer_ref):
    odd = position_of() % 2 == 1
    low, high = rows_ref[:16], rows_ref[48:64]
    inner_ref[...] = jnp.where(odd, low, high).astype(BF16)
    outer_ref[...] = jnp.where(odd, high, low).astype(BF16)


def keep_close(*arrays):
    return [pltpu.with_memory_space_constraint(x, pltpu.VMEM) for x in arrays]


def signed_root(value):
    root = jnp.sqrt(jnp.abs(value))
    return jnp.where(value < 0.0, -root, root)


def second_kernel(
    near_ref, project_ref, rows_ref, inner_ref, outer_ref, start_ref,
    flip_ref, left_ref, spun_ref, *, breadth,
):
    coils, groups, _, wide = near_ref.shape
    start = []
    first = lax.broadcasted_iota(jnp.int32, (8, wide), 1) < breadth
    for t in range(groups):
        low, high = [
            sum(signed_root(near_ref[i, t, 32:40, :].astype(F32)) for i in range(s, coils, 2)) for s in range(2)
        ]
        parts = [
            jnp.where(first, low, pltpu.roll(high, breadth, 1)),
            jnp.where(first, pltpu.roll(low, breadth, 1), high),
        ]
        start.append(jnp.concatenate(parts, axis=0))
        start_ref[t] = start[t]
    damped = apply_data_term(near_ref, project_ref, start, start, left_ref, spun_ref, breadth)
    to_rows(damped, rows_ref, flip_ref, breadth)
    write_edges(rows_ref, inner_ref, outer_ref)


def tap_blocks(values, places, first_ref, second_ref, shift_ref, breadth):
    for h, value in values.items():
        shift_ref[24 * h : 24 * h + 8] = pltpu.roll(value, 1, 1)
        shift_ref[24 * h + 8 : 24 * h + 16] = value
        shift_ref[24 * h + 16 : 24 * h + 24] = pltpu.roll(value, LANES - 1, 1)
    ones = jnp.ones((8, LANES), F32)
    hidden = {}
    for g in places:
        columns = jnp.concatenate([shift_ref[24 * g : 24 * g + 72], ones], axis=0).astype(BF16)
        block = dot(first_ref[...], columns).astype(BF16)
        hidden[g] = jnp.maximum(block, jnp.zeros_like(block))
    inside = lax.broadcasted_iota(jnp.int32, (1, LANES), 1) < breadth
    return {g: jnp.where(inside, dot(second_ref[...], hidden[g]), 0.0) for g in places}


def inner_kernel(rows_ref, first_ref, second_ref, taps_ref, shift_ref, *, breadth):
    values = {h: rows_ref[8 * h : 8 * h + 8] for h in range(8)}
    for g, tap in tap_blocks(values, range(6), first_ref, second_ref, shift_ref, breadth).items():
        taps_ref[g] = tap


def edge_rows(first, second):
    value = jnp.where(position_of() % 2 == 1, first.astype(F32), second.astype(F32))
    return [value[:8], value[8:]]


def regularized(
    rows_ref, taps_ref, inner_ref, outer_ref, first_ref, second_ref, bias_ref, shift_ref, breadth
):
    inner, outer = inner_ref[...], outer_ref[...]
    own = [rows_ref[8 * h : 8 * h + 8] for h in range(8)]
    values = edge_rows(inner, outer) + own + edge_rows(outer, inner)
    taps = tap_blocks(
        {h: values[h] for h in (0, 1, 2, 3, 8, 9, 10, 11)}, (0, 1, 8, 9), first_ref, second_ref, shift_ref, breadth
    )
    taps.update({g + 2: taps_ref[g] for g in range(6)})
    last = 2 * lax.axis_size("coil") - 1
    taps[0] = jnp.where(position_of() > 0, taps[0], 0.0)
    taps[9] = jnp.where(position_of() < last, taps[9], 0.0)
    lanes = lax.broadcasted_iota(jnp.int32, (1, LANES), 1)
    bias = bias_ref[...]
    updates = []
    for h in range(8):
        total = taps[h][:24] + taps[h + 1][24:48] + taps[h + 2][48:]
        update = pltpu.roll(total[:8], 1, 1) + total[8:16] + pltpu.roll(total[16:], LANES - 1, 1)
        updates.append(jnp.where(lanes < breadth, update, 0.0) + bias)
    return own, updates


def third_kernel(
    rows_ref, taps_ref, inner_ref, outer_ref, first_ref, second_ref, bias_ref, near_ref, project_ref, start_ref,
    out_ref, inner_out_ref, outer_out_ref,
    shift_ref, flip_ref, left_ref, spun_ref, *, breadth,
):
    groups, _, wide = start_ref.shape
    own, updates = regularized(
        rows_ref, taps_ref, inner_ref, outer_ref, first_ref, second_ref, bias_ref, shift_ref, breadth
    )
    for h in range(8):
        image = own[h] + updates[h]
        for j in range(2):
            flip_ref[64 * j + 8 * h : 64 * j + 8 * h + 8] = image[:, 128 * j : 128 * j + 128]
    image = from_rows(flip_ref, groups, wide // breadth, breadth)
    start = [start_ref[t] for t in range(groups)]
    damped = apply_data_term(near_ref, project_ref, image, start, left_ref, spun_ref, breadth)
    to_rows(damped, out_ref, flip_ref, breadth)
    write_edges(out_ref, inner_out_ref, outer_out_ref)


def last_kernel(
    rows_ref, taps_ref, inner_ref, outer_ref, first_ref, second_ref, bias_ref, keep_ref, give_ref,
    shift_ref, *, breadth,
):
    own, updates = regularized(
        rows_ref, taps_ref, inner_ref, outer_ref, first_ref, second_ref, bias_ref, shift_ref, breadth
    )
    upper = lax.axis_index("sect") == 0
    for h in range(8):
        image = (own[h] + updates[h])[:, :breadth]
        keep, give = jnp.where(upper, image[:4], image[4:]), jnp.where(upper, image[4:], image[:4])
        for s in range(2):
            keep_ref[h, s] = keep[2 * s : 2 * s + 2]
            give_ref[h, s] = give[2 * s : 2 * s + 2]


def join_kernel(keep_ref, got_ref, out_ref, sems):
    place = position_of() % 2
    copies = [
        pltpu.make_async_copy(x, out_ref.at[pl.ds(8 * y, 8)], sems.at[i])
        for i, (x, y) in enumerate(((keep_ref, place), (got_ref, 1 - place)))
    ]
    for copy in copies:
        copy.start()
    for copy in copies:
        copy.wait()


def fast_device(measured, coil_maps, sampling, conv_first, bias_first, conv_second, bias_second):
    height, coils_here, slices_here, _, breadth = coil_maps.shape
    ranks, sects = lax.axis_size("coil"), lax.axis_size("sect")
    count = ranks * sects
    slices = slices_here * sects
    wide = slices_here * breadth
    features = conv_first.shape[0]
    both = ("coil", "sect")
    f32 = lambda *dims: jax.ShapeDtypeStruct(dims, F32)
    bf16 = lambda *dims: jax.ShapeDtypeStruct(dims, BF16)

    row_cos, row_sin = dft_tables(height)
    col_cos, col_sin = dft_tables(breadth)
    row_high, row_low = bf16_pair(np.concatenate([row_cos, row_sin], axis=1) / math.sqrt(height))
    column_high, column_low = bf16_pair(np.concatenate([col_cos, col_sin], axis=0) / math.sqrt(breadth))
    row_table = jnp.asarray(np.concatenate([row_high, row_low], axis=0))
    column_table = jnp.asarray(np.concatenate([column_high, column_high, column_low], axis=1))
    by_coil = lambda x: jnp.transpose(x, (1, 2, 3, 4, 0)).reshape(coils_here, slices_here, 2 * breadth, height)
    block_rows = 16 * coils_here + 8
    far = (by_coil(measured), by_coil(coil_maps), sampling, row_table, column_table)
    double = 2 * breadth
    anywhere = pl.BlockSpec(memory_space=pl.ANY)
    roomy = pltpu.CompilerParams(vmem_limit_bytes=40 << 20)
    give, *fetched = pl.pallas_call(
        first_kernel, compiler_params=roomy,
        in_specs=[anywhere] * 5, out_specs=vmem(6),
        out_shape=[
            f32(double, height), pltpu.VMEM((coils_here, double, height), F32),
            *[pltpu.VMEM(x.shape, x.dtype) for x in far[1:]],
        ],
        scratch_shapes=[
            pltpu.VMEM((coils_here, double, height), F32), pltpu.SemaphoreType.DMA((3 + 4 * coils_here,)),
        ],
    )(*[pltpu.with_memory_space_constraint(x, pltpu.HBM) for x in far])
    got = lax.ppermute(give, "coil", [(i, i ^ 1) for i in range(ranks)])
    send, total = pl.pallas_call(
        own_kernel, compiler_params=roomy,
        in_specs=vmem(5), out_specs=[anywhere] + vmem(1),
        out_shape=[bf16(count, block_rows, wide), pltpu.VMEM((double, height), F32)],
        scratch_shapes=[pltpu.VMEM((coils_here, count, 16, wide), BF16), pltpu.SemaphoreType.DMA((coils_here,))],
    )(*keep_close(*fetched))
    send, mask = pl.pallas_call(
        sum_kernel, compiler_params=MODEST,
        in_specs=vmem(3) + [anywhere], out_specs=[anywhere] + vmem(1),
        out_shape=[bf16(count, block_rows, wide), bf16(slices_here, breadth)],
        input_output_aliases={3: 0},
        scratch_shapes=[pltpu.VMEM((count, 8, wide), BF16), pltpu.SemaphoreType.DMA],
    )(*keep_close(total, got, fetched[2]), send)
    near = lax.all_to_all(send, both, 0, 0, tiled=True).reshape(ranks, sects, block_rows, wide)

    other = lax.ppermute(mask, "sect", [(0, 1), (1, 0)])
    blank = np.zeros((breadth, wide - breadth))
    angle = np.concatenate([col_cos, blank, col_sin, blank], axis=1).astype(np.float32)
    span = 18 * slices
    pick_first = np.zeros((slices, 54, span + 8))
    pick_second = np.zeros((slices, span, 54))
    for a, b, e, q, s in np.ndindex(3, 3, 3, 2, slices):
        tap = 2 * (9 * a + 3 * b + e) + q
        if 0 <= s + b - 1 < slices:
            pick_first[s, tap, ((a * 3 + e) * slices + s + b - 1) * 2 + q] = 1.0
            pick_second[s + b - 1, ((a * 3 + e) * slices + s) * 2 + q, tap] = 1.0
    place = np.eye(slices * features).reshape(slices, features, slices * features)
    project, matrix_first, matrix_second, bias = pl.pallas_call(
        table_kernel,
        compiler_params=MODEST,
        in_specs=vmem(9) + [pl.BlockSpec(memory_space=pltpu.SMEM)], out_specs=vmem(4),
        out_shape=[
            pltpu.VMEM(dims, BF16)
            for dims in (
                (sects, 2 * wide, 2 * wide), (slices * features, span + 8), (span, slices * features),
            )
        ] + [pltpu.VMEM((2 * slices, LANES), F32)],
    )(
        mask, other, jnp.asarray(angle), conv_first.T, bias_first.reshape(1, features), conv_second,
        *[jnp.asarray(x.astype(BF16)) for x in (pick_first, pick_second, place)], bias_second,
    )
    weights = keep_close(matrix_first, matrix_second, bias)
    weight_specs = vmem(3)

    owner = {block_of(i, y): 2 * i + y for i in range(ranks) for y in range(2)}
    near_pairs = []
    for block in range(1, count - 1, 2):
        near_pairs += [(owner[block], owner[block + 1]), (owner[block + 1], owner[block])]
    swap = lambda x: lax.ppermute(x, "sect", [(0, 1), (1, 0)])

    edge = 4 * slices
    work = [
        pltpu.VMEM((32 * slices, 128), F32),
        pltpu.VMEM((sects, 16 * ranks, 2 * wide), BF16), pltpu.VMEM((sects, 16 * ranks, 2 * wide), F32),
    ]

    shift = [pltpu.VMEM((12 * 6 * slices, LANES), F32)]

    def around(rows, inner, outer):
        taps = pl.pallas_call(
            functools.partial(inner_kernel, breadth=breadth),
            compiler_params=MODEST, in_specs=vmem(3), out_specs=vmem(1)[0],
            out_shape=pltpu.VMEM((6, 18 * slices, LANES), F32), scratch_shapes=shift,
        )(*keep_close(rows), *weights[:2])
        return keep_close(rows, taps, swap(inner), lax.ppermute(outer, both, near_pairs))

    row_shapes = [f32(16 * slices, LANES), bf16(edge, LANES), bf16(edge, LANES)]
    rows, inner, outer, start = pl.pallas_call(
        functools.partial(second_kernel, breadth=breadth),
        compiler_params=MODEST,
        in_specs=vmem(2), out_specs=vmem(4),
        out_shape=row_shapes + [pltpu.VMEM((sects, 16, wide), F32)], scratch_shapes=work,
    )(*keep_close(near, project))
    for _ in range(ITERS - 1):
        rows, inner, outer = pl.pallas_call(
            functools.partial(third_kernel, breadth=breadth),
            compiler_params=MODEST,
            in_specs=vmem(4) + weight_specs + vmem(3), out_specs=vmem(3), out_shape=row_shapes,
            scratch_shapes=shift + work,
        )(*around(rows, inner, outer), *weights, *keep_close(near, project, start))
    piece = f32(8, slices_here, 2, breadth)
    keep, give = pl.pallas_call(
        functools.partial(last_kernel, breadth=breadth),
        compiler_params=MODEST,
        in_specs=vmem(4) + weight_specs, out_specs=vmem(2), out_shape=[piece, piece],
        scratch_shapes=shift,
    )(*around(rows, inner, outer), *weights)
    return pl.pallas_call(
        join_kernel, compiler_params=MODEST, in_specs=vmem(2), out_specs=anywhere,
        out_shape=f32(16, slices_here, 2, breadth), scratch_shapes=[pltpu.SemaphoreType.DMA((2,))],
    )(*keep_close(keep, swap(give)))


def per_device_any(measured, coil_maps, *rest):
    height, coils_here, slices_here, _, breadth = coil_maps.shape
    ranks, sects = lax.axis_size("coil"), lax.axis_size("sect")
    fits = (
        sects == 2 and slices_here == 2 and coils_here == 2 and height == 8 * ranks * sects
        and 2 * breadth % 128 == 0 and 128 < breadth < LANES and breadth % 16 == 0
    )
    return (fast_device if fits else per_device)(measured, coil_maps, *rest)


def solution(mesh):
    coil_spec = P(None, "coil", "sect", None, None)
    in_specs = (coil_spec, coil_spec, P("sect", None), P(), P(), P(), P())
    return jax.shard_map(
        per_device_any,
        mesh=mesh,
        in_specs=in_specs,
        out_specs=P("coil", "sect", None, None),
        check_vma=False,
    )
```
